256 devices in a mesh: role: 2 (over core), slot: 32 (over z, x), tp: 4 (over y).
Axes of the slice: x: 4, y: 4, z: 8, core: 2. Of those that a mesh axis runs over, the one named last changes fastest.
Arguments:
- queries: bfloat16 [2, 8192, 8192], P('role', 'slot', 'tp'), may hold values from -16 to 16
- cache_keys: bfloat16 [2, 256, 8, 256, 128], P('role', 'slot', 'tp'), may hold values from -16 to 16
- cache_values: bfloat16 [2, 256, 8, 256, 128], P('role', 'slot', 'tp'), may hold values from -6 to 6
- new_keys: bfloat16 [2, 8192, 1024], P('role', 'slot', 'tp'), may hold values from -16 to 16
- new_values: bfloat16 [2, 8192, 1024], P('role', 'slot', 'tp'), may hold values from -6 to 6
- out_weight: bfloat16 [2, 8192, 8192], P('role', 'tp'), may hold values from -0.0625 to 0.0625
- fork_src: int32 [256], P(('role', 'slot')), may hold values from 0 to 255, as said below
- cache_blocks: int32 [256], P('slot'), may hold values from 1 to 2, 320 in all
Outputs:
- layer_out: bfloat16 [2, 8192, 8192], P('role', ('slot', 'tp'))
The draws below stay inside these ranges and needn't reach their ends.
Inputs may be any that keep to these rules, and one draw needn't show every extreme that they name: For every index a < 32, exactly 2 of the slots j with j // 8 = a have fork_src[j] = j (survivors); every other entry names a survivor. For all a and b, at most 1 slots j with j // 8 = a and fork_src[j] != j have fork_src[j] // 8 = b, and for every a some b has exactly 1.
All inputs are finite; a program needn't handle non-finite values. No bound on the sum of `cache_blocks` on one device may be relied on, other than what follows from the above.
Results may differ from the reference program's by a relative error of at most 0.0095.
Values may be sent and summed in bfloat16 or wider, within the bound.
No kernel may reach another device: no remote copies, remote signals or barrier semaphores. Data moves between devices by JAX's collectives and lax.ppermute only.
A program may use at most 128 MiB of HBM per device.

```python
import math
import jax
import jax.numpy as jnp
import numpy as np
from jax import lax

D = 8192
QH = 64
KVH = 8
HD = 128
NODE_DEV = 8
MAXBLK = 2
BLK = 128
STEP = 32
NODES = 256
ROWS = 8192
MAXTOK = 256
HEAD_GROUPS = 4


def base_sample(key, salt, full_shape):
    return jnp.clip(jax.random.normal(jax.random.fold_in(key, salt), full_shape, jnp.float32), -6.0, 6.0)


def draw_queries(key, part):
    sample = base_sample(key, 11, (2, ROWS, QH, HD))
    return sample.reshape(2, ROWS, QH * HD).astype(jnp.bfloat16)


def draw_cache_keys(key, part):
    full_shape = (2, NODES, KVH, MAXTOK, HD)
    sample = base_sample(key, 13, full_shape)
    return sample.astype(jnp.bfloat16)


def draw_new_keys(key, part):
    full_shape = (2, ROWS, KVH, HD)
    sample = base_sample(key, 15, full_shape)
    return sample.reshape(2, ROWS, KVH * HD).astype(jnp.bfloat16)


def draw_fork_src(key, part):
    devices = NODES // NODE_DEV
    keep_count = NODE_DEV // 4
    order_keys = jax.random.split(jax.random.fold_in(key, 21), devices)
    orders = jax.vmap(lambda one_key: jax.random.permutation(one_key, NODE_DEV))(order_keys)
    slot_rank = jnp.argsort(orders, axis=1, stable=True)
    shifts = jax.random.randint(jax.random.fold_in(key, 22), (devices,), 0, devices)
    pick_index = jax.random.randint(jax.random.fold_in(key, 23), (devices, NODE_DEV), 0, keep_count)
    device_ids = jnp.arange(devices)[:, None]
    free_rank = slot_rank - keep_count
    source_dev = (device_ids + shifts[:, None] + free_rank) % devices
    source_slot = orders[source_dev, pick_index]
    forked = source_dev * NODE_DEV + source_slot
    own_ids = device_ids * NODE_DEV + jnp.arange(NODE_DEV)[None, :]
    return jnp.where(slot_rank < keep_count, own_ids, forked).reshape(NODES).astype(jnp.int32)


def level_of(key, dims, pieces, least, top_value):
    loudness = 1.0
    for dim, blocks in pieces:
        steps = jax.random.uniform(jax.random.fold_in(jax.random.fold_in(key, 6), dim), (blocks,), jnp.float32, least / len(pieces), top_value / len(pieces))
        loudness = loudness * jnp.repeat(jnp.exp(steps), dims[dim] // blocks).reshape((-1,) + (1,) * (len(dims) - 1 - dim))
    return loudness


def split_up(number_of, total, bound, slope):
    portions = [(1 << 20) // math.isqrt(standing ** slope) + 1 for standing in range(2, number_of + 1)]
    surplus, given = total - bound - (number_of - 1), [1] * (number_of - 1)
    while surplus > 0:
        candidates = [i for i in range(number_of - 1) if given[i] < bound]
        mass, budget = sum([portions[i] for i in candidates]), surplus
        for i in candidates:
            more = min(bound - given[i], max(1, budget * portions[i] // mass), surplus)
            given[i] = given[i] + more
            surplus = surplus - more
    return np.array([bound] + given)


def ragged_sizes(stream_key, amount, total, bound, skew):
    if amount == 2:
        one = jax.random.randint(stream_key, (), max(1, total - bound), min(bound, total - 1) + 1)
        return jnp.stack([one, total - one])
    tallies = jnp.asarray(split_up(amount, total, bound, skew), jnp.int32)
    pairs = (amount - 1) // 2
    source_of, receiver = tallies[1:1 + 2 * pairs:2], tallies[2:2 + 2 * pairs:2]
    slack = jnp.minimum(source_of - 1, bound - receiver)
    passed = jax.random.randint(jax.random.fold_in(stream_key, 1), (pairs,), 0, 1 << 20) % (slack + 1)
    tallies = tallies.at[1:1 + 2 * pairs:2].set(source_of - passed).at[2:2 + 2 * pairs:2].set(receiver + passed)
    return tallies[jax.random.permutation(jax.random.fold_in(stream_key, 2), amount)]


def gaussian(stream_key, shape, spread, most, cuts=(), kind=jnp.bfloat16):
    array = jax.random.normal(stream_key, shape, jnp.float32) * spread
    if len(cuts) > 0:
        array = level_of(stream_key, shape, cuts, -0.22, 0.18) * array
    return jnp.clip(array, min=-most, max=most).astype(kind)


def setup_inputs(seed: int = 0) -> dict:
    arg_keys = jax.random.split(jax.random.key(seed), 9)
    queries = draw_queries(jax.random.fold_in(arg_keys[8], 71), 0)
    cache_keys = draw_cache_keys(jax.random.fold_in(arg_keys[8], 71), 0)
    cache_values = gaussian(arg_keys[2], (2, NODES, KVH, MAXTOK, HD), 1.0, 6.0, ((0, 2), (1, 32), (2, 4)))
    new_keys = draw_new_keys(jax.random.fold_in(arg_keys[8], 71), 0)
    new_values = gaussian(arg_keys[4], (2, ROWS, KVH * HD), 1.0, 6.0, ((0, 2), (1, 32), (2, 4)))
    out_weight = gaussian(arg_keys[5], (2, QH * HD, D), (QH * HD) ** -0.5, 0.0625, ((0, 2), (1, 4)))
    fork_src = draw_fork_src(jax.random.fold_in(arg_keys[8], 71), 0)
    cache_blocks = ragged_sizes(arg_keys[7], NODES, NODES * MAXBLK // 2 + NODES // 4, MAXBLK, 2).astype(jnp.int32)
    return dict(queries=queries, cache_keys=cache_keys, cache_values=cache_values, new_keys=new_keys, new_values=new_values, out_weight=out_weight, fork_src=fork_src, cache_blocks=cache_blocks)


def partial_softmax(query_matrix_rows, key_matrix_rows, value_matrix_rows, allowed, logit_scale):
    attention_logits = jnp.einsum("syu,swu->syw", query_matrix_rows.astype(jnp.float32), key_matrix_rows.astype(jnp.float32)) * logit_scale
    attention_logits = jnp.where(allowed[None], attention_logits, -jnp.inf)
    part_max = jnp.max(attention_logits, axis=-1)
    softmax_weights = jnp.exp(attention_logits - part_max[..., None])
    part_sum = jnp.sum(softmax_weights, axis=-1)
    rounded_result = lax.optimization_barrier(softmax_weights.astype(jnp.bfloat16)).astype(jnp.float32)
    partial_output = jnp.einsum("fzo,fol->fzl", rounded_result, value_matrix_rows.astype(jnp.float32))
    return partial_output, part_max, part_sum


def normalise(part):
    partial_output, part_max, part_sum = part
    return (partial_output / part_sum[..., None]).astype(jnp.bfloat16), part_max, part_sum


def combine(cache_part, step_part):
    cache_att, cache_max, cache_sum = cache_part
    step_out, step_max, step_sum = step_part
    cache_float = lax.optimization_barrier(cache_att).astype(jnp.float32)
    joint_max = jnp.maximum(cache_max, step_max)
    cache_weight = jnp.exp(cache_max - joint_max) * cache_sum
    step_scale = jnp.exp(step_max - joint_max)
    numer = cache_float * cache_weight[..., None] + step_out * step_scale[..., None]
    denom = cache_weight + step_sum * step_scale
    return (numer / denom[..., None]).astype(jnp.bfloat16)


def reference(queries, cache_keys, cache_values, new_keys, new_values, out_weight, fork_src, cache_blocks):
    group_size = QH // KVH
    logit_scale = float(HD) ** -0.5
    lengths = jnp.take(cache_blocks, fork_src).astype(jnp.int32) * BLK
    row_step = jnp.arange(STEP * group_size) // group_size
    causal = jnp.arange(STEP)[None, :] <= row_step[:, None]
    block_width = QH * HD // HEAD_GROUPS
    results = []
    for model_index in range(2):
        query_nodes = queries[model_index].reshape(NODES, STEP, KVH, group_size, HD).transpose(0, 2, 1, 3, 4).reshape(NODES, KVH, STEP * group_size, HD)
        step_keys = new_keys[model_index].reshape(NODES, STEP, KVH, HD).transpose(0, 2, 1, 3)
        step_values = new_values[model_index].reshape(NODES, STEP, KVH, HD).transpose(0, 2, 1, 3)

        def one_node(node_index):
            parent = fork_src[node_index].astype(jnp.int32)
            allowed = (jnp.arange(MAXTOK) < lengths[node_index])[None, :]
            cache_part = normalise(partial_softmax(query_nodes[node_index], cache_keys[model_index, parent], cache_values[model_index, parent], allowed, logit_scale))
            step_part = partial_softmax(query_nodes[node_index], step_keys[node_index], step_values[node_index], causal, logit_scale)
            return combine(cache_part, step_part)

        attention = lax.map(one_node, jnp.arange(NODES, dtype=jnp.int32))
        attention = attention.reshape(NODES, KVH, STEP, group_size, HD).transpose(0, 2, 1, 3, 4).reshape(ROWS, QH * HD)
        summed = jnp.zeros((ROWS, D), jnp.float32)
        for part_index in range(HEAD_GROUPS):
            lower = part_index * block_width
            partial_value = jnp.dot(attention[:, lower:lower + block_width], out_weight[model_index, lower:lower + block_width], preferred_element_type=jnp.float32)
            summed = summed + lax.optimization_barrier(partial_value.astype(jnp.bfloat16)).astype(jnp.float32)
        results.append(summed.astype(jnp.bfloat16))
    return jnp.stack(results)
```

```python
import functools

import jax
import jax.numpy as jnp
from jax import lax
from jax.experimental import pallas as pl
from jax.experimental.pallas import tpu as pltpu
from jax.sharding import PartitionSpec as P

BLK = 128
NX = 4
NZ = 8
NTP = 4
NODE = 8
STEP = 32
FAST = 2
CHUNKS = 2

T_SURV = 0
T_FROM = 8
T_RANK = 16
T_LEN = 24
T_REL = 32
T_SEL = 40
T_SIZE = 64


def zperm(d):
    return [(s, (s + NX * d) % (NX * NZ)) for s in range(NX * NZ)]


def xperm(d):
    return [(s, (s // NX) * NX + (s % NX + d) % NX) for s in range(NX * NZ)]


def yperm(d):
    return [(t, (t + d) % NTP) for t in range(NTP)]


def plan_body(here_ref, parents_ref, blocks_ref, plan_ref):
    here = here_ref[0]
    row = here // NX
    col = here % NX
    for i in range(T_SIZE):
        plan_ref[i] = 0

    def surv_step(j, count):
        keep = parents_ref[here * NODE + j] == here * NODE + j

        @pl.when(keep)
        def _():
            plan_ref[T_SURV + jnp.minimum(count, 1)] = j

        return count + keep.astype(jnp.int32)

    lax.fori_loop(0, NODE, surv_step, jnp.int32(0))

    def own_step(j, counts):
        slot = here * NODE + j
        parent = parents_ref[slot]
        moving = parent != slot
        dist = (col - (parent // NODE) % NX + NX) % NX
        plan_ref[T_LEN + j] = blocks_ref[parent] * BLK
        plan_ref[T_FROM + j] = jnp.where(moving, dist, NX)
        rank = jnp.int32(0)
        out = []
        for d in range(NX):
            hit = moving & (dist == d)
            rank = jnp.where(hit, counts[d], rank)
            out.append(counts[d] + hit.astype(jnp.int32))
        plan_ref[T_RANK + j] = jnp.minimum(rank, FAST - 1)
        return tuple(out)

    lax.fori_loop(0, NODE, own_step, (jnp.int32(0),) * NX)

    for d in range(NX):
        peer = row * NX + (col + d) % NX

        def peer_step(j, count, peer=peer, d=d):
            slot = peer * NODE + j
            parent = parents_ref[slot]
            source = parent // NODE
            hit = (parent != slot) & (source % NX == col)

            @pl.when(hit & (count < FAST))
            def _():
                def below(k, seen):
                    node = source * NODE + k
                    is_below = (node < parent) & (parents_ref[node] == node)
                    return seen | is_below.astype(jnp.int32)

                order = lax.fori_loop(0, NODE, below, jnp.int32(0))
                plan_ref[T_REL + d * FAST + count] = (row - source // NX + NZ) % NZ
                plan_ref[T_SEL + d * FAST + count] = order

            return count + hit.astype(jnp.int32)

        lax.fori_loop(0, NODE, peer_step, jnp.int32(0))


def make_plan(here, parents, blocks):
    smem = pl.BlockSpec(memory_space=pltpu.SMEM)
    return pl.pallas_call(
        plan_body,
        out_shape=jax.ShapeDtypeStruct((T_SIZE,), jnp.int32),
        in_specs=[smem, smem, smem],
        out_specs=smem,
        name="plan",
    )(here, parents, blocks)


def pack_body(plan_ref, keys_ref, values_ref, first_ref, second_ref, sems):
    copies = []
    for s in range(2):
        node = plan_ref[T_SURV + s]
        for b, out in enumerate((first_ref, second_ref)):
            for kv, src in enumerate((keys_ref, values_ref)):
                copies.append(
                    pltpu.make_async_copy(
                        src.at[node, :, pl.ds(b * BLK, BLK), :],
                        out.at[kv, s],
                        sems.at[len(copies)],
                    )
                )
    for c in copies:
        c.start()
    for c in copies:
        c.wait()


def pack(plan, keys, values):
    heads, _, dim = keys.shape[1:]
    shape = jax.ShapeDtypeStruct((2, 2, heads, BLK, dim), keys.dtype)
    hbm = pl.BlockSpec(memory_space=pl.ANY)
    return pl.pallas_call(
        pack_body,
        out_shape=(shape, shape),
        in_specs=[pl.BlockSpec(memory_space=pltpu.SMEM), hbm, hbm],
        out_specs=(hbm, hbm),
        scratch_shapes=[pltpu.SemaphoreType.DMA((8,))],
        name="pack",
    )(plan, keys, values)


def ring_gather(own):
    up, down = own, own
    got = {0: (own, own)}
    for k in (1, 2, 3):
        up = lax.ppermute(up, "slot", zperm(1))
        down = lax.ppermute(down, "slot", zperm(-1))
        got[k] = (up, up)
        got[NZ - k] = (down, down)
    half_up = lax.ppermute(up[0:1], "slot", zperm(1))
    half_down = lax.ppermute(down[1:2], "slot", zperm(-1))
    got[4] = (half_up, half_down)
    return got


def select_body(plan_ref, *refs):
    srcs = refs[:9]
    outs = refs[9 : 9 + NX]
    sems = refs[9 + NX]

    def source(rel, kv):
        if rel < 4:
            return srcs[rel], kv
        if rel == 4:
            return srcs[4 + kv], 0
        return srcs[rel + 1], kv

    def issue(start):
        for d in range(NX):
            for i in range(FAST):
                rel = plan_ref[T_REL + d * FAST + i]
                order = plan_ref[T_SEL + d * FAST + i]
                for kv in range(2):
                    sem = sems.at[(d * FAST + i) * 2 + kv]
                    if start:
                        for r in range(NZ):
                            ref, lead = source(r, kv)

                            @pl.when(rel == r)
                            def _(ref=ref, lead=lead):
                                pltpu.make_async_copy(
                                    ref.at[lead, order], outs[d].at[kv, i], sem
                                ).start()
                    else:
                        pltpu.make_async_copy(srcs[0].at[kv, 0], outs[d].at[kv, i], sem).wait()

    issue(True)
    issue(False)


def select(plan, got):
    own = got[0][0]
    srcs = [got[r][0] for r in range(4)] + [got[4][0], got[4][1]] + [got[r][0] for r in (5, 6, 7)]
    shape = jax.ShapeDtypeStruct((2, FAST) + own.shape[2:], own.dtype)
    hbm = pl.BlockSpec(memory_space=pl.ANY)
    return pl.pallas_call(
        select_body,
        out_shape=(shape,) * NX,
        in_specs=[pl.BlockSpec(memory_space=pltpu.SMEM)] + [hbm] * 9,
        out_specs=(hbm,) * NX,
        scratch_shapes=[pltpu.SemaphoreType.DMA((NX * FAST * 2,))],
        name="select",
    )(plan, *srcs)


def place_body(plan_ref, *refs):
    caches = refs[0:2]
    firsts = refs[2 : 2 + NX]
    seconds = refs[2 + NX : 2 + 2 * NX]
    outs = refs[2 + 2 * NX : 4 + 2 * NX]
    sems = refs[4 + 2 * NX]

    for j in range(NODE):
        dist = plan_ref[T_FROM + j]
        rank = plan_ref[T_RANK + j]
        for kv in range(2):
            for b in range(2):
                dst = outs[kv].at[j, :, pl.ds(b * BLK, BLK), :]
                sem = sems.at[(j * 2 + kv) * 2 + b]

                @pl.when(dist == NX)
                def _(kv=kv, b=b, dst=dst, sem=sem, j=j):
                    pltpu.make_async_copy(
                        caches[kv].at[j, :, pl.ds(b * BLK, BLK), :], dst, sem
                    ).start()

                for d in range(NX):

                    @pl.when(dist == d)
                    def _(kv=kv, b=b, dst=dst, sem=sem, rank=rank, d=d):
                        src = (firsts, seconds)[b][d]
                        pltpu.make_async_copy(src.at[kv, rank], dst, sem).start()

    for j in range(NODE):
        for kv in range(2):
            for b in range(2):
                pltpu.make_async_copy(
                    caches[kv].at[j, :, pl.ds(b * BLK, BLK), :],
                    outs[kv].at[j, :, pl.ds(b * BLK, BLK), :],
                    sems.at[(j * 2 + kv) * 2 + b],
                ).wait()


def place(plan, keys, values, firsts, seconds):
    hbm = pl.BlockSpec(memory_space=pl.ANY)
    shape = jax.ShapeDtypeStruct(keys.shape, keys.dtype)
    return pl.pallas_call(
        place_body,
        out_shape=(shape, shape),
        in_specs=[pl.BlockSpec(memory_space=pltpu.SMEM)] + [hbm] * (2 + 2 * NX),
        out_specs=(hbm, hbm),
        scratch_shapes=[pltpu.SemaphoreType.DMA((NODE * 4,))],
        name="place",
    )(plan, keys, values, *firsts, *seconds)


def attend_body(heads, group, dim, scale, plan_ref, q_ref, k_ref, v_ref, nk_ref, nv_ref, out_ref):
    length = plan_ref[T_LEN + pl.program_id(0)]
    rows = STEP * group
    tokens = k_ref.shape[2]
    nt = (((1,), (1,)), ((), ()))
    nn = (((1,), (0,)), ((), ()))
    cache_ok = lax.broadcasted_iota(jnp.int32, (rows, tokens), 1) < length
    step_of = lax.broadcasted_iota(jnp.int32, (rows, STEP), 0) % STEP
    step_ok = lax.broadcasted_iota(jnp.int32, (rows, STEP), 1) <= step_of
    for h in range(heads):
        base = h * group * dim
        q = jnp.concatenate(
            [q_ref[:, base + g * dim : base + (g + 1) * dim] for g in range(group)], axis=0
        )
        nk = nk_ref[:, h * dim : (h + 1) * dim]
        nv = nv_ref[:, h * dim : (h + 1) * dim]
        sc = lax.dot_general(q, k_ref[0, h], nt, preferred_element_type=jnp.float32) * scale
        ss = lax.dot_general(q, nk, nt, preferred_element_type=jnp.float32) * scale
        sc = jnp.where(cache_ok, sc, -jnp.inf)
        ss = jnp.where(step_ok, ss, -jnp.inf)
        top = jnp.maximum(
            jnp.max(sc, axis=1, keepdims=True), jnp.max(ss, axis=1, keepdims=True)
        )
        pc = jnp.exp(sc - top)
        ps = jnp.exp(ss - top)
        total = jnp.sum(pc, axis=1, keepdims=True) + jnp.sum(ps, axis=1, keepdims=True)
        o = lax.dot_general(
            pc.astype(jnp.bfloat16), v_ref[0, h], nn, preferred_element_type=jnp.float32
        ) + lax.dot_general(ps.astype(jnp.bfloat16), nv, nn, preferred_element_type=jnp.float32)
        o = (o / total).astype(out_ref.dtype)
        for g in range(group):
            out_ref[:, base + g * dim : base + (g + 1) * dim] = o[g * STEP : (g + 1) * STEP]


def attend(plan, queries, keys, values, new_keys, new_values):
    heads, tokens, dim = keys.shape[1:]
    width = queries.shape[1]
    group = width // (heads * dim)
    kv_spec = pl.BlockSpec((1, heads, tokens, dim), lambda n, p: (n, 0, 0, 0))
    q_spec = pl.BlockSpec((STEP, width), lambda n, p: (n, 0))
    n_spec = pl.BlockSpec((STEP, heads * dim), lambda n, p: (n, 0))
    return pl.pallas_call(
        functools.partial(attend_body, heads, group, dim, float(dim) ** -0.5),
        out_shape=jax.ShapeDtypeStruct(queries.shape, queries.dtype),
        grid_spec=pltpu.PrefetchScalarGridSpec(
            num_scalar_prefetch=1,
            grid=(NODE,),
            in_specs=[q_spec, kv_spec, kv_spec, n_spec, n_spec],
            out_specs=q_spec,
        ),
        name="attend",
    )(plan, queries, keys, values, new_keys, new_values)


def project_body(tp_ref, att_ref, w_ref, r0_ref, r1_ref, r2_ref, r3_ref, rel_ref):
    part = att_ref.shape[0] // NTP

    @pl.when(pl.program_id(0) == 0)
    def _():
        for d in range(NTP):
            row = pl.multiple_of(((tp_ref[0] + d) % NTP) * part, part)
            rel_ref[d * part : (d + 1) * part, :] = att_ref[pl.ds(row, part), :]

    res = jnp.dot(rel_ref[...], w_ref[...], preferred_element_type=jnp.float32)
    for d, ref in enumerate((r0_ref, r1_ref, r2_ref, r3_ref)):
        ref[...] = res[d * part : (d + 1) * part].astype(ref.dtype)


def project(tp, att, weight, chunk, tile):
    rows, inner = att.shape
    width = weight.shape[1] // CHUNKS
    steps = width // tile
    part = rows // NTP
    out = jax.ShapeDtypeStruct((part, width), att.dtype)
    out_spec = pl.BlockSpec((part, tile), lambda n, t: (0, n))
    return pl.pallas_call(
        project_body,
        out_shape=(out,) * NTP,
        grid_spec=pltpu.PrefetchScalarGridSpec(
            num_scalar_prefetch=1,
            grid=(steps,),
            in_specs=[
                pl.BlockSpec((rows, inner), lambda n, t: (0, 0)),
                pl.BlockSpec((inner, tile), lambda n, t: (0, chunk * steps + n)),
            ],
            out_specs=(out_spec,) * NTP,
            scratch_shapes=[pltpu.VMEM((rows, inner), att.dtype)],
        ),
        name="project",
    )(tp, att, weight)


def add2(a, b):
    return (a.astype(jnp.float32) + b.astype(jnp.float32)).astype(a.dtype)


def scatter_sum(parts):
    r0, r1, r2, r3 = parts
    half = r0.shape[1] // 2
    up, down = yperm(1), yperm(-1)
    relay_a = lax.ppermute(r2[:, :half], "tp", up)
    relay_b = lax.ppermute(r2[:, half:], "tp", down)
    direct_b = lax.ppermute(r1[:, half:], "tp", up)
    direct_a = lax.ppermute(r3[:, :half], "tp", down)
    far_a = lax.ppermute(add2(r1[:, :half], relay_a), "tp", up)
    far_b = lax.ppermute(add2(r3[:, half:], relay_b), "tp", down)
    f32 = jnp.float32
    out_a = r0[:, :half].astype(f32) + far_a.astype(f32) + direct_a.astype(f32)
    out_b = r0[:, half:].astype(f32) + far_b.astype(f32) + direct_b.astype(f32)
    return [out_a.astype(r0.dtype), out_b.astype(r0.dtype)]


def general_fetch(parents, keys, values):
    slot_count = lax.axis_size("slot")
    slot_here = lax.axis_index("slot")
    moving_all = parents != jnp.arange(parents.shape[0], dtype=jnp.int32)
    from_here = (moving_all & (parents // NODE == slot_here)).reshape(slot_count, NODE)
    local = (parents % NODE).reshape(slot_count, NODE)
    send_node = jnp.sum(jnp.where(from_here, local, 0), axis=1)
    got_keys = lax.all_to_all(keys[send_node], "slot", 0, 0, tiled=True)
    got_values = lax.all_to_all(values[send_node], "slot", 0, 0, tiled=True)
    own = lax.dynamic_slice_in_dim(parents, slot_here * NODE, NODE)
    moving = (own != slot_here * NODE + jnp.arange(NODE, dtype=jnp.int32))[:, None, None, None]
    source = own // NODE
    return (
        jnp.where(moving, got_keys[source], keys),
        jnp.where(moving, got_values[source], values),
    )


def shards(
    queries, cache_keys, cache_values, new_keys, new_values, out_weight, fork_src, cache_blocks
):
    keys, values = cache_keys[0], cache_values[0]
    slot_here = lax.axis_index("slot").astype(jnp.int32)
    tp_here = lax.axis_index("tp").astype(jnp.int32).reshape(1)
    peers = lax.axis_size("role") * lax.axis_size("slot")
    meta = jnp.concatenate([fork_src, cache_blocks])
    meta = jnp.broadcast_to(meta[None], (peers, meta.shape[0]))
    meta = lax.all_to_all(meta, ("role", "slot"), 0, 0, tiled=True)
    n_src = fork_src.shape[0]
    parents = meta[:, :n_src].reshape(-1)
    blocks = meta[: peers // 2, n_src:].reshape(-1)
    plan = make_plan(slot_here.reshape(1), parents, blocks)

    slots = jnp.arange(parents.shape[0], dtype=jnp.int32)
    column = jnp.where(parents != slots, (parents // NODE) % NX, NX).reshape(-1, NODE)
    load = jnp.stack([jnp.sum((column == c).astype(jnp.int32), axis=1) for c in range(NX)])
    fits = jnp.max(load) <= FAST

    first, second = pack(plan, keys, values)
    got_first = ring_gather(first)
    got_second = ring_gather(second)

    def fast(_):
        moved = []
        for got in (got_first, got_second):
            outs = select(plan, got)
            moved.append([outs[0]] + [lax.ppermute(outs[d], "slot", xperm(d)) for d in (1, 2, 3)])
        return place(plan, keys, values, moved[0], moved[1])

    def general(_):
        return general_fetch(parents, keys, values)

    node_keys, node_values = lax.cond(fits, fast, general, 0)
    att = attend(plan, queries[0], node_keys, node_values, new_keys[0], new_values[0])
    pieces = []
    for c in range(CHUNKS):
        pieces += scatter_sum(project(tp_here, att, out_weight[0], c, 1024))
    return jnp.concatenate(pieces, axis=1)[None]


def solution(mesh):
    in_specs = (
        P("role", "slot", "tp"),
        P("role", "slot", "tp", None, None),
        P("role", "slot", "tp", None, None),
        P("role", "slot", "tp"),
        P("role", "slot", "tp"),
        P("role", "tp", None),
        P(("role", "slot")),
        P("slot"),
    )
    out_specs = P("role", ("slot", "tp"), None)
    return jax.shard_map(shards, mesh=mesh, in_specs=in_specs, out_specs=out_specs, check_vma=False)
```

```python
import functools

import jax
import jax.numpy as jnp
from jax import lax
from jax.experimental import pallas as pl
from jax.experimental.pallas import tpu as pltpu
from jax.sharding import PartitionSpec as P


BLK = 128
NX = 4
NZ = 8
NTP = 4
NODE = 8
STEP = 32
FAST = 2

T_FROM = 0
T_RANK = 8
T_LEN = 16
T_REL = 24
T_SEL = 32
T_LOAD = 40
T_SIZE = 48


def zperm(d):
    return [(s, (s + NX * d) % (NX * NZ)) for s in range(NX * NZ)]


def xperm(d):
    return [(s, (s // NX) * NX + (s % NX + d) % NX) for s in range(NX * NZ)]


def yperm(d):
    return [(t, (t + d) % NTP) for t in range(NTP)]


def halves_perm(other, n_slot):
    pairs = []
    for role in range(2):
        for k in range(n_slot // 2):
            for h in range(2):
                dest = (h ^ other) * n_slot + role * (n_slot // 2) + k
                pairs.append((role * n_slot + 2 * k + h, dest))
    return pairs


def plan_body(here_ref, parents_ref, blocks_ref, plan_ref):
    here = here_ref[0]
    row = here // NX
    col = here % NX
    zero = jnp.int32(0)
    for i in range(T_SIZE):
        plan_ref[i] = 0

    def own_step(j, counts):
        slot = here * NODE + j
        parent = parents_ref[slot]
        moving = parent != slot
        dist = (col - (parent // NODE) % NX + NX) % NX
        plan_ref[T_LEN + j] = blocks_ref[parent] * BLK
        plan_ref[T_FROM + j] = jnp.where(moving, dist, NX)
        rank = zero
        out = []
        for d in range(NX):
            hit = moving & (dist == d)
            rank = jnp.where(hit, counts[d], rank)
            out.append(counts[d] + hit.astype(jnp.int32))
        plan_ref[T_RANK + j] = jnp.minimum(rank, FAST - 1)
        return tuple(out)

    lax.fori_loop(0, NODE, own_step, (zero,) * NX)

    for d in range(NX):
        peer = row * NX + (col + d) % NX

        def peer_step(j, count, peer=peer, d=d):
            slot = peer * NODE + j
            parent = parents_ref[slot]
            source = parent // NODE
            hit = (parent != slot) & (source % NX == col)

            @pl.when(hit & (count < FAST))
            def _():
                def below(k, seen):
                    node = source * NODE + k
                    is_below = (node < parent) & (parents_ref[node] == node)
                    return seen | is_below.astype(jnp.int32)

                order = lax.fori_loop(0, NODE, below, zero)
                plan_ref[T_REL + d * FAST + count] = (row - source // NX + NZ) % NZ
                plan_ref[T_SEL + d * FAST + count] = order

            return count + hit.astype(jnp.int32)

        lax.fori_loop(0, NODE, peer_step, zero)

    def load_step(a, most):
        counts = [zero] * NX
        for j in range(NODE):
            slot = a * NODE + j
            parent = parents_ref[slot]
            c = jnp.where(parent != slot, (parent // NODE) % NX, NX)
            counts = [n + (c == i).astype(jnp.int32) for i, n in enumerate(counts)]
        for n in counts:
            most = jnp.maximum(most, n)
        return most

    plan_ref[T_LOAD] = lax.fori_loop(0, parents_ref.shape[0] // NODE, load_step, zero)


def make_plan(here, parents, blocks):
    smem = pl.BlockSpec(memory_space=pltpu.SMEM)
    return pl.pallas_call(
        plan_body,
        out_shape=jax.ShapeDtypeStruct((T_SIZE,), jnp.int32),
        in_specs=[smem, smem, smem],
        out_specs=smem,
        compiler_params=pltpu.CompilerParams(vmem_limit_bytes=1 << 20),
        name="plan",
    )(here, parents, blocks)


def pack_body(where_ref, mine_ref, other_ref, keys_ref, values_ref, first_ref, second_ref, sems):
    role = where_ref[0]
    base = where_ref[1] * NODE
    count = jnp.int32(0)
    first = jnp.int32(0)
    last = jnp.int32(0)
    for j in range(NODE):
        h, k = divmod(j, NODE // 2)
        parent = jnp.where(role == h, mine_ref[k], other_ref[k])
        keep = parent == base + j
        first = jnp.where(keep & (count == 0), j, first)
        last = jnp.where(keep, j, last)
        count = count + keep.astype(jnp.int32)
    copies = []
    for b, out in enumerate((first_ref, second_ref)):
        for s, node in enumerate((first, last)):
            for kv, src in enumerate((keys_ref, values_ref)):
                copies.append(
                    pltpu.make_async_copy(
                        src.at[node, :, pl.ds(b * BLK, BLK), :],
                        out.at[kv, s],
                        sems.at[len(copies)],
                    )
                )
    for c in copies:
        c.start()
    for c in copies:
        c.wait()


def pack(where, mine, other, keys, values):
    heads, _, dim = keys.shape[1:]
    shape = pltpu.VMEM((2, 2, heads, BLK, dim), keys.dtype)
    smem = pl.BlockSpec(memory_space=pltpu.SMEM)
    hbm = pl.BlockSpec(memory_space=pl.ANY)
    vmem = pl.BlockSpec(memory_space=pltpu.VMEM)
    return pl.pallas_call(
        pack_body,
        out_shape=(shape, shape),
        in_specs=[smem, smem, smem, hbm, hbm],
        out_specs=(vmem, vmem),
        scratch_shapes=[pltpu.SemaphoreType.DMA((8,))],
        compiler_params=pltpu.CompilerParams(vmem_limit_bytes=2 << 20),
        name="pack",
    )(where, mine, other, keys, values)


def ring_step(up, down):
    return lax.ppermute(up, "slot", zperm(1)), lax.ppermute(down, "slot", zperm(-1))


def ring_rest(own, up1, down1, up2, down2):
    up3, down3 = ring_step(up2, down2)
    half_up = lax.ppermute(up3[0:1], "slot", zperm(1))
    half_down = lax.ppermute(down3[1:2], "slot", zperm(-1))
    return [own, up1, up2, up3, half_up, half_down, down3, down2, down1], up3


def select_body(plan_ref, *refs):
    srcs = refs[:9]
    outs = refs[9 : 9 + NX]
    sems = refs[9 + NX]

    def source(rel, kv):
        if rel < 4:
            return srcs[rel], kv
        if rel == 4:
            return srcs[4 + kv], 0
        return srcs[rel + 1], kv

    def issue(start):
        for d in range(NX):
            for i in range(FAST):
                rel = plan_ref[T_REL + d * FAST + i]
                order = plan_ref[T_SEL + d * FAST + i]
                for kv in range(2):
                    sem = sems.at[(d * FAST + i) * 2 + kv]
                    if start:
                        for r in range(NZ):
                            ref, lead = source(r, kv)

                            @pl.when(rel == r)
                            def _(ref=ref, lead=lead):
                                pltpu.make_async_copy(
                                    ref.at[lead, order], outs[d].at[kv, i], sem
                                ).start()
                    else:
                        pltpu.make_async_copy(srcs[0].at[kv, 0], outs[d].at[kv, i], sem).wait()

    issue(True)
    issue(False)


def select(plan, srcs):
    own = srcs[0]
    shape = pltpu.VMEM((2, FAST) + own.shape[2:], own.dtype)
    hbm = pl.BlockSpec(memory_space=pl.ANY)
    vmem = pl.BlockSpec(memory_space=pltpu.VMEM)
    return pl.pallas_call(
        select_body,
        out_shape=(shape,) * NX,
        in_specs=[pl.BlockSpec(memory_space=pltpu.SMEM)] + [hbm] * 9,
        out_specs=(vmem,) * NX,
        scratch_shapes=[pltpu.SemaphoreType.DMA((NX * FAST * 2,))],
        compiler_params=pltpu.CompilerParams(vmem_limit_bytes=2 << 20),
        name="select",
    )(plan, *srcs)


def project_side(part, tile, att_ref, w_ref, outs, side):
    half = outs[0].shape[1]

    def step(c, carry):
        at = pl.multiple_of(c * tile, tile)
        cols = pl.ds(pl.multiple_of(side * half + at, tile), tile)
        res = jnp.dot(att_ref[...], w_ref[:, cols], preferred_element_type=jnp.float32)
        for d in range(NTP):
            outs[2 * d + side][:, pl.ds(at, tile)] = res[d * part : (d + 1) * part].astype(
                outs[0].dtype
            )
        return carry

    lax.fori_loop(0, half // tile, step, 0)


def attend_body(heads, group, dim, scale, tile, plan_ref, tp_ref, q_ref, nk_ref, nv_ref, *refs):
    caches = refs[0:2]
    moved = refs[2 : 2 + 2 * NX]
    refs = refs[2 + 2 * NX :]
    w_ref, att_ref, w1_ref = refs[:3]
    outs = refs[3 : 3 + 2 * NTP]
    kbuf, vbuf, w0_ref, sems, wsems = refs[3 + 2 * NTP :]
    bufs = (kbuf, vbuf)
    per = NODE // NTP
    part = per * STEP
    half = outs[0].shape[1]

    def fetch(j, kv, b, src):
        dst = bufs[kv].at[j, :, pl.ds(b * BLK, BLK), :]
        return pltpu.make_async_copy(src, dst, sems.at[j, kv * 2 + b])

    def own(j, kv, b):
        return fetch(j, kv, b, caches[kv].at[j, :, pl.ds(b * BLK, BLK), :])

    def start(j, carry):
        dist = plan_ref[T_FROM + j]
        rank = plan_ref[T_RANK + j]

        @pl.when(dist == NX)
        def _():
            for kv in range(2):
                for b in range(2):
                    own(j, kv, b).start()

        for d in range(NX):

            @pl.when(dist == d)
            def _(d=d):
                for kv in range(2):
                    for b in range(2):
                        fetch(j, kv, b, moved[b * NX + d].at[kv, rank]).start()

        return carry

    lax.fori_loop(0, NODE, start, 0)
    loads = []
    for i in range(4):
        dst = (w0_ref, w1_ref)[i // 2].at[:, pl.ds((i % 2) * half, half)]
        loads.append(
            pltpu.make_async_copy(w_ref.at[:, pl.ds(i * half, half)], dst, wsems.at[i])
        )
    for load in loads:
        load.start()

    rows = STEP * group
    tokens = kbuf.shape[2]
    nt = (((1,), (1,)), ((), ()))
    nn = (((1,), (0,)), ((), ()))
    step_of = lax.broadcasted_iota(jnp.int32, (rows, STEP), 0) % STEP
    step_ok = lax.broadcasted_iota(jnp.int32, (rows, STEP), 1) <= step_of
    token_at = lax.broadcasted_iota(jnp.int32, (rows, tokens), 1)

    def attend_node(n, carry):
        for kv in range(2):
            for b in range(2):
                own(n, kv, b).wait()
        at = pl.multiple_of(n * STEP, STEP)
        to = ((n // per - tp_ref[0] + NTP) % NTP) * per + n % per
        to = pl.multiple_of(to * STEP, STEP)
        cache_ok = token_at < plan_ref[T_LEN + n]
        for h in range(heads):
            base = h * group * dim
            q = jnp.concatenate(
                [q_ref[pl.ds(at, STEP), base + g * dim : base + (g + 1) * dim] for g in range(group)],
                axis=0,
            )
            nk = nk_ref[pl.ds(at, STEP), h * dim : (h + 1) * dim]
            nv = nv_ref[pl.ds(at, STEP), h * dim : (h + 1) * dim]
            sc = lax.dot_general(q, kbuf[n, h], nt, preferred_element_type=jnp.float32) * scale
            ss = lax.dot_general(q, nk, nt, preferred_element_type=jnp.float32) * scale
            sc = jnp.where(cache_ok, sc, -jnp.inf)
            ss = jnp.where(step_ok, ss, -jnp.inf)
            top = jnp.maximum(
                jnp.max(sc, axis=1, keepdims=True), jnp.max(ss, axis=1, keepdims=True)
            )
            pc = jnp.exp(sc - top)
            ps = jnp.exp(ss - top)
            total = jnp.sum(pc, axis=1, keepdims=True) + jnp.sum(ps, axis=1, keepdims=True)
            o = lax.dot_general(
                pc.astype(jnp.bfloat16), vbuf[n, h], nn, preferred_element_type=jnp.float32
            ) + lax.dot_general(
                ps.astype(jnp.bfloat16), nv, nn, preferred_element_type=jnp.float32
            )
            o = (o / total).astype(att_ref.dtype)
            for g in range(group):
                att_ref[pl.ds(to, STEP), base + g * dim : base + (g + 1) * dim] = o[
                    g * STEP : (g + 1) * STEP
                ]
        return carry

    lax.fori_loop(0, NODE, attend_node, 0)
    for side in range(2):
        loads[side].wait()
        project_side(part, tile, att_ref, w0_ref, outs, side)
    for load in loads[2:]:
        load.wait()


def attend(plan, tp, queries, new_keys, new_values, keys, values, moved, weight, tile):
    heads, _, dim = keys.shape[1:]
    rows, width = queries.shape
    group = width // (heads * dim)
    inner, cols = weight.shape
    dtype = queries.dtype
    smem = pl.BlockSpec(memory_space=pltpu.SMEM)
    vmem = pl.BlockSpec(memory_space=pltpu.VMEM)
    hbm = pl.BlockSpec(memory_space=pl.ANY)
    out = pltpu.VMEM((rows // NTP, cols // 4), dtype)
    return pl.pallas_call(
        functools.partial(attend_body, heads, group, dim, float(dim) ** -0.5, tile),
        out_shape=(pltpu.VMEM((rows, width), dtype), pltpu.VMEM((inner, cols // 2), dtype))
        + (out,) * (2 * NTP),
        in_specs=[smem, smem, vmem, vmem, vmem] + [hbm] * (3 + 2 * NX),
        out_specs=(vmem,) * (2 + 2 * NTP),
        scratch_shapes=[
            pltpu.VMEM(keys.shape, keys.dtype),
            pltpu.VMEM(keys.shape, keys.dtype),
            pltpu.VMEM((inner, cols // 2), dtype),
            pltpu.SemaphoreType.DMA((NODE, 4)),
            pltpu.SemaphoreType.DMA((4,)),
        ],
        compiler_params=pltpu.CompilerParams(vmem_limit_bytes=24 << 20),
        name="attend",
    )(plan, tp, queries, new_keys, new_values, keys, values, *moved, weight)


def project_body(tile, att_ref, w_ref, *outs):
    for side in range(2):
        project_side(outs[0].shape[0], tile, att_ref, w_ref, outs, side)


def project(att, weight, tile):
    out = pltpu.VMEM((att.shape[0] // NTP, weight.shape[1] // 2), att.dtype)
    vmem = pl.BlockSpec(memory_space=pltpu.VMEM)
    return pl.pallas_call(
        functools.partial(project_body, tile),
        out_shape=(out,) * (2 * NTP),
        in_specs=[vmem, vmem],
        out_specs=(vmem,) * (2 * NTP),
        compiler_params=pltpu.CompilerParams(vmem_limit_bytes=6 << 20),
        name="project",
    )(att, weight)


def add2(a, b):
    return (a.astype(jnp.float32) + b.astype(jnp.float32)).astype(a.dtype)


def scatter_sum(parts):
    r0a, r0b, r1a, r1b, r2a, r2b, r3a, r3b = parts
    up, down = yperm(1), yperm(-1)
    relay_a = lax.ppermute(r2a, "tp", up)
    relay_b = lax.ppermute(r2b, "tp", down)
    direct_b = lax.ppermute(r1b, "tp", up)
    direct_a = lax.ppermute(r3a, "tp", down)
    far_a = lax.ppermute(add2(r1a, relay_a), "tp", up)
    far_b = lax.ppermute(add2(r3b, relay_b), "tp", down)
    f32 = jnp.float32
    out_a = r0a.astype(f32) + far_a.astype(f32) + direct_a.astype(f32)
    out_b = r0b.astype(f32) + far_b.astype(f32) + direct_b.astype(f32)
    return [out_a.astype(r0a.dtype), out_b.astype(r0a.dtype)]


def general_fetch(parents, keys, values):
    slot_count = lax.axis_size("slot")
    slot_here = lax.axis_index("slot")
    moving_all = parents != jnp.arange(parents.shape[0], dtype=jnp.int32)
    from_here = (moving_all & (parents // NODE == slot_here)).reshape(slot_count, NODE)
    local = (parents % NODE).reshape(slot_count, NODE)
    send_node = jnp.sum(jnp.where(from_here, local, 0), axis=1)
    got_keys = lax.all_to_all(keys[send_node], "slot", 0, 0, tiled=True)
    got_values = lax.all_to_all(values[send_node], "slot", 0, 0, tiled=True)
    own = lax.dynamic_slice_in_dim(parents, slot_here * NODE, NODE)
    moving = (own != slot_here * NODE + jnp.arange(NODE, dtype=jnp.int32))[:, None, None, None]
    source = own // NODE
    both = jnp.stack(
        [jnp.where(moving, got_keys[source], keys), jnp.where(moving, got_values[source], values)]
    )
    both = both.reshape(2, NX, NODE // NX, keys.shape[1], 2, BLK, keys.shape[3])
    return [both[:, d, :, :, b] for b in range(2) for d in range(NX)]


def shards(
    queries, cache_keys, cache_values, new_keys, new_values, out_weight, fork_src, cache_blocks
):
    keys, values = cache_keys[0], cache_values[0]
    role_here = lax.axis_index("role").astype(jnp.int32)
    slot_here = lax.axis_index("slot").astype(jnp.int32)
    tp_here = lax.axis_index("tp").astype(jnp.int32).reshape(1)
    n_slot = lax.axis_size("slot")
    peers = lax.axis_size("role") * n_slot

    mine = lax.ppermute(fork_src, ("role", "slot"), halves_perm(0, n_slot))
    other = lax.ppermute(fork_src, ("role", "slot"), halves_perm(1, n_slot))
    where = jnp.stack([role_here, slot_here])
    first, second = pack(where, mine, other, keys, values)
    first1 = ring_step(first, first)
    second1 = ring_step(second, second)

    meta = jnp.concatenate([fork_src, cache_blocks])
    meta = jnp.broadcast_to(meta[None], (peers, meta.shape[0]))
    meta, _ = lax.optimization_barrier((meta, first[0, 0, 0, :8, :1]))
    meta = lax.all_to_all(meta, ("role", "slot"), 0, 0, tiled=True)
    n_src = fork_src.shape[0]
    parents = meta[:, :n_src].reshape(-1)
    blocks = meta[: peers // 2, n_src:].reshape(-1)
    plan = make_plan(slot_here.reshape(1), parents, blocks)
    fits = plan[T_LOAD] <= FAST

    def fast(_):
        first2 = ring_step(*first1)
        got_first, marker = ring_rest(first, *first1, *first2)
        start, _ = lax.optimization_barrier((second1, marker))
        second2 = ring_step(*start)
        got_second, _ = ring_rest(second, *second1, *second2)
        moved = []
        for got in (got_first, got_second):
            outs = select(plan, got)
            moved.append(outs[0])
            moved += [lax.ppermute(outs[d], "slot", xperm(d)) for d in (1, 2, 3)]
        return moved, plan

    def general(_):
        nodes = jnp.arange(NODE, dtype=jnp.int32)
        per = NODE // NX
        direct = jnp.concatenate([nodes // per, nodes % per, plan[T_LEN:]])
        return general_fetch(parents, keys, values), direct

    moved, plan = lax.cond(fits, fast, general, 0)
    att, weight1, *part0 = attend(
        plan,
        tp_here,
        queries[0],
        new_keys[0],
        new_values[0],
        keys,
        values,
        moved,
        out_weight[0],
        512,
    )
    part1 = project(att, weight1, 512)
    pieces = []
    for parts in (part0, part1):
        pieces += scatter_sum(parts)
    return jnp.concatenate(pieces, axis=1)[None]


def solution(mesh):
    in_specs = (
        P("role", "slot", "tp"),
        P("role", "slot", "tp", None, None),
        P("role", "slot", "tp", None, None),
        P("role", "slot", "tp"),
        P("role", "slot", "tp"),
        P("role", "tp", None),
        P(("role", "slot")),
        P("slot"),
    )
    out_specs = P("role", ("slot", "tp"), None)

    return jax.shard_map(shards, mesh=mesh, in_specs=in_specs, out_specs=out_specs, check_vma=False)
```

```python
import functools

import jax
import jax.numpy as jnp
from jax import lax
from jax.experimental import pallas as pl
from jax.experimental.pallas import tpu as pltpu
from jax.sharding import PartitionSpec as P


BLK = 128
NX = 4
NZ = 8
NTP = 4
NODE = 8
STEP = 32
FAST = 2
META = 16

T_FROM = 0
T_RANK = 8
T_LEN = 16
T_FIT = 24
T_SIZE = 32

SMEM = pl.BlockSpec(memory_space=pltpu.SMEM)
VMEM = pl.BlockSpec(memory_space=pltpu.VMEM)
ANY = pl.BlockSpec(memory_space=pl.ANY)


def params(mib):
    return pltpu.CompilerParams(vmem_limit_bytes=mib << 20)


def zperm(d):
    return [(s, (s + NX * d) % (NX * NZ)) for s in range(NX * NZ)]


def xperm(d):
    return [(s, (s // NX) * NX + (s % NX + d) % NX) for s in range(NX * NZ)]


def yperm(d):
    return [(t, (t + d) % NTP) for t in range(NTP)]


def halves_perm(other, n_slot):
    pairs = []
    for role in range(2):
        for k in range(n_slot // 2):
            for h in range(2):
                dest = (h ^ other) * n_slot + role * (n_slot // 2) + k
                pairs.append((role * n_slot + 2 * k + h, dest))
    return pairs


def lane_row(values):
    lane = lax.broadcasted_iota(jnp.int32, (META, 128), 1)
    tile = jnp.zeros((META, 128), jnp.float32)
    for i, value in enumerate(values):
        tile = jnp.where(lane == i, value.astype(jnp.float32), tile)
    return tile.astype(jnp.bfloat16)


def column_counts(here, list_ref, col):
    base = here * NODE
    counts = [jnp.int32(0)] * NX
    for j in range(NODE):
        parent = list_ref[j]
        dist = (col - (parent // NODE) % NX + NX) % NX
        dist = jnp.where(parent == base + j, NX, dist)
        counts = [c + (dist == d).astype(jnp.int32) for d, c in enumerate(counts)]
    return counts


def pack_body(
    where_ref, mine_ref, other_ref, blocks_ref, keys_ref, values_ref,
    first_ref, second_ref, list_ref, sems,
):
    role = where_ref[0]
    here = where_ref[1]
    base = here * NODE
    count = jnp.int32(0)
    low = jnp.int32(0)
    high = jnp.int32(0)
    for j in range(NODE):
        h, k = divmod(j, NODE // 2)
        parent = jnp.where(role == h, mine_ref[k], other_ref[k])
        list_ref[j] = parent
        keep = parent == base + j
        low = jnp.where(keep & (count == 0), j, low)
        high = jnp.where(keep, j, high)
        count = count + keep.astype(jnp.int32)
    heads = keys_ref.shape[1]
    copies = []
    for b, out in enumerate((first_ref, second_ref)):
        for s, node in enumerate((low, high)):
            for kv, src in enumerate((keys_ref, values_ref)):
                for h in range(heads):
                    row = ((kv * 2 + s) * heads + h) * BLK
                    copies.append(
                        pltpu.make_async_copy(
                            src.at[node, h, pl.ds(b * BLK, BLK), :],
                            out.at[pl.ds(row, BLK), :],
                            sems.at[len(copies)],
                        )
                    )
    for c in copies:
        c.start()
    counts = column_counts(here, list_ref, here % NX)
    most = jnp.maximum(jnp.maximum(counts[0], counts[1]), jnp.maximum(counts[2], counts[3]))
    fit = (most <= FAST).astype(jnp.int32)
    rows = second_ref.shape[0]
    first_ref[rows : rows + META, :] = lane_row(
        (low, high, blocks_ref[low], blocks_ref[high], fit)
    )
    for c in copies:
        c.wait()


def pack(where, mine, other, blocks, keys, values):
    heads, _, dim = keys.shape[1:]
    rows = 4 * heads * BLK
    return pl.pallas_call(
        pack_body,
        out_shape=(
            pltpu.VMEM((rows + META, dim), keys.dtype),
            pltpu.VMEM((rows, dim), keys.dtype),
            jax.ShapeDtypeStruct((NODE,), jnp.int32),
        ),
        in_specs=[SMEM, SMEM, SMEM, SMEM, ANY, ANY],
        out_specs=(VMEM, VMEM, SMEM),
        scratch_shapes=[pltpu.SemaphoreType.DMA((8 * heads,))],
        compiler_params=params(2),
        name="pack",
    )(where, mine, other, blocks, keys, values)


def ring_step(pair):
    up, down = pair
    return lax.ppermute(up, "slot", zperm(1)), lax.ppermute(down, "slot", zperm(-1))


def ring_last(pair):
    up, down = pair
    half = up.shape[0] // (2 * META) * META
    return (
        lax.ppermute(up[:half], "slot", zperm(1)),
        lax.ppermute(down[half:], "slot", zperm(-1)),
    )


def ring_list(own, one, two, three, last):
    return [own, one[0], two[0], three[0], last[0], last[1], three[1], two[1], one[1]]


def unit_source(srcs, rel, kv, rank, size):
    half = srcs[4].shape[0]
    at = (kv * 2 + rank) * size
    if rel < 4:
        return srcs[rel], at
    if rel == 4:
        return srcs[4 + kv], at - kv * half
    return srcs[rel + 1], at


def issue_units(picks, srcs, outs, size, sems):
    for u in range(NX * FAST):
        d, i = divmod(u, FAST)
        rel, rank = picks(u)
        for r in range(NZ):

            @pl.when(rel == r)
            def _(r=r, d=d, i=i, u=u, rank=rank):
                for kv in range(2):
                    ref, at = unit_source(srcs, r, kv, rank, size)
                    at = pl.multiple_of(at, META)
                    pltpu.make_async_copy(
                        ref.at[pl.ds(at, size), :],
                        outs[d].at[pl.ds((kv * 2 + i) * size, size), :],
                        sems.at[u * 2 + kv],
                    ).start()


def wait_units(srcs, outs, size, sems):
    for u in range(NX * FAST):
        d, i = divmod(u, FAST)
        for kv in range(2):
            pltpu.make_async_copy(
                srcs[0].at[pl.ds(0, size), :],
                outs[d].at[pl.ds((kv * 2 + i) * size, size), :],
                sems.at[u * 2 + kv],
            ).wait()


def select_first_body(where_ref, *refs):
    lists = refs[:NX]
    srcs = refs[NX : NX + 9]
    outs = refs[NX + 9 : 2 * NX + 9]
    pick_ref, meta_ref, wide_ref, ids_ref, sems, msem, ssem = refs[2 * NX + 9 :]
    size = outs[0].shape[0] // 4 // META * META
    here = where_ref[1]
    row = here // NX
    col = here % NX
    reads = []
    for rel in range(NZ):
        ref = srcs[rel] if rel < 4 else srcs[rel + 1]
        at = 4 * size - (srcs[4].shape[0] if rel == 4 else 0)
        reads.append(
            pltpu.make_async_copy(ref.at[pl.ds(at, META), :], meta_ref.at[rel], msem.at[rel])
        )
    for c in reads:
        c.start()
    for c in reads:
        c.wait()
    wide_ref[...] = meta_ref[...].astype(jnp.float32).astype(jnp.int32)
    spill = pltpu.make_async_copy(wide_ref, ids_ref, ssem)
    spill.start()
    spill.wait()
    for u in range(2 * NX * FAST):
        pick_ref[u] = 0
    for d in range(NX):
        base = (row * NX + (col + d) % NX) * NODE

        def scan(j, count, d=d, base=base):
            parent = lists[d][j]
            source = parent // NODE
            hit = (parent != base + j) & (source % NX == col)
            rel = (row - source // NX + NZ) % NZ

            @pl.when(hit & (count < FAST))
            def _():
                pick_ref[d * FAST + count] = rel
                pick_ref[NX * FAST + d * FAST + count] = (
                    parent % NODE == ids_ref[rel, 0, 1]
                ).astype(jnp.int32)

            return count + hit.astype(jnp.int32)

        lax.fori_loop(0, NODE, scan, jnp.int32(0))

    def picks(u):
        return pick_ref[u], pick_ref[NX * FAST + u]

    issue_units(picks, srcs, outs, size, sems)
    fit = ids_ref[0, 0, 4]
    for rel in range(1, NZ):
        fit = jnp.minimum(fit, ids_ref[rel, 0, 4])
    for d in range(NX):
        sizes = []
        for i in range(FAST):
            rel, rank = picks(d * FAST + i)
            sizes.append(ids_ref[rel, 0, 2 + rank])
        outs[d][4 * size : 4 * size + META, :] = lane_row((sizes[0], sizes[1], fit))
    wait_units(srcs, outs, size, sems)


def select_first(where, lists, srcs):
    own = srcs[0]
    out = pltpu.VMEM(own.shape, own.dtype)
    return pl.pallas_call(
        select_first_body,
        out_shape=(out,) * NX + (jax.ShapeDtypeStruct((2 * NX * FAST,), jnp.int32),),
        in_specs=[SMEM] * (1 + NX) + [ANY] * 9,
        out_specs=(VMEM,) * NX + (SMEM,),
        scratch_shapes=[
            pltpu.VMEM((NZ, META, 128), own.dtype),
            pltpu.VMEM((NZ, META, 128), jnp.int32),
            pltpu.SMEM((NZ, META, 128), jnp.int32),
            pltpu.SemaphoreType.DMA((NX * FAST * 2,)),
            pltpu.SemaphoreType.DMA((NZ,)),
            pltpu.SemaphoreType.DMA,
        ],
        compiler_params=params(2),
        name="select_first",
    )(where, *lists, *srcs)


def select_second_body(pick_ref, *refs):
    srcs = refs[:9]
    outs = refs[9 : 9 + NX]
    sems = refs[9 + NX]
    size = outs[0].shape[0] // 4

    def picks(u):
        return pick_ref[u], pick_ref[NX * FAST + u]

    issue_units(picks, srcs, outs, size, sems)
    wait_units(srcs, outs, size, sems)


def select_second(picks, srcs):
    own = srcs[0]
    out = pltpu.VMEM(own.shape, own.dtype)
    return pl.pallas_call(
        select_second_body,
        out_shape=(out,) * NX,
        in_specs=[SMEM] + [ANY] * 9,
        out_specs=(VMEM,) * NX,
        scratch_shapes=[pltpu.SemaphoreType.DMA((NX * FAST * 2,))],
        compiler_params=params(2),
        name="select_second",
    )(picks, *srcs)


def attend_unit(scale, q, k, v, nk, nv, step_ok):
    nt = (((1,), (1,)), ((), ()))
    nn = (((1,), (0,)), ((), ()))
    f32 = jnp.float32
    sc = lax.dot_general(q, k, nt, preferred_element_type=f32) * scale
    ss = lax.dot_general(q, nk, nt, preferred_element_type=f32) * scale
    ss = jnp.where(step_ok, ss, -jnp.inf)
    top = jnp.maximum(jnp.max(sc, axis=1, keepdims=True), jnp.max(ss, axis=1, keepdims=True))
    pc = jnp.exp(sc - top)
    ps = jnp.exp(ss - top)
    total = jnp.sum(pc, axis=1, keepdims=True) + jnp.sum(ps, axis=1, keepdims=True)
    o = lax.dot_general(pc.astype(v.dtype), v, nn, preferred_element_type=f32)
    o = o + lax.dot_general(ps.astype(v.dtype), nv, nn, preferred_element_type=f32)
    return (o / total).astype(v.dtype)


def attend_node(n, tokens, scale, tp, q_ref, nk_ref, nv_ref, kbuf, vbuf, att_ref):
    heads, _, dim = kbuf.shape[1:]
    group = q_ref.shape[1] // (heads * dim)
    per = NODE // NTP
    at = pl.multiple_of(n * STEP, STEP)
    to = ((n // per - tp + NTP) % NTP) * per + n % per
    to = pl.multiple_of(to * STEP, STEP)
    rows = STEP * group
    step_of = lax.broadcasted_iota(jnp.int32, (rows, STEP), 0) % STEP
    step_ok = lax.broadcasted_iota(jnp.int32, (rows, STEP), 1) <= step_of

    def head(h, carry):
        base = h * group * dim

        def cols(g):
            return pl.ds(pl.multiple_of(base + g * dim, dim), dim)

        mine = pl.ds(pl.multiple_of(h * dim, dim), dim)
        q = jnp.concatenate([q_ref[pl.ds(at, STEP), cols(g)] for g in range(group)], axis=0)
        o = attend_unit(
            scale,
            q,
            kbuf[n, h, :tokens],
            vbuf[n, h, :tokens],
            nk_ref[pl.ds(at, STEP), mine],
            nv_ref[pl.ds(at, STEP), mine],
            step_ok,
        )
        for g in range(group):
            att_ref[pl.ds(to, STEP), cols(g)] = o[g * STEP : (g + 1) * STEP]
        return carry

    lax.fori_loop(0, heads, head, 0)


def moved_copy(src, kv, rank, h, heads, j, b, buf, sem):
    at = pl.multiple_of(((kv * 2 + rank) * heads + h) * BLK, BLK)
    return pltpu.make_async_copy(
        src.at[pl.ds(at, BLK), :], buf.at[j, h, pl.ds(b * BLK, BLK), :], sem
    )


def early_body(scale, where_ref, list_ref, blocks_ref, q_ref, nk_ref, nv_ref, *refs):
    caches = refs[0:2]
    moved = refs[2 : 2 + NX]
    w_ref, att_ref, w0_ref, w1_ref, table_ref = refs[2 + NX : 7 + NX]
    kbuf, vbuf, meta_ref, wide_ref, ids_ref, sems, wsems, msem, ssem = refs[7 + NX :]
    bufs = (kbuf, vbuf)
    heads = kbuf.shape[1]
    here = where_ref[1]
    tp = where_ref[2]
    col = here % NX
    half = w0_ref.shape[1]
    reads = []
    for d in range(NX):
        at = moved[d].shape[0] - META
        reads.append(
            pltpu.make_async_copy(moved[d].at[pl.ds(at, META), :], meta_ref.at[d], msem.at[d])
        )
    for c in reads:
        c.start()
    counts = [jnp.int32(0)] * NX
    for j in range(NODE):
        parent = list_ref[j]
        moving = parent != here * NODE + j
        dist = jnp.where(moving, (col - (parent // NODE) % NX + NX) % NX, NX)
        rank = jnp.int32(0)
        for d in range(NX):
            hit = dist == d
            rank = jnp.where(hit, counts[d], rank)
            counts[d] = counts[d] + hit.astype(jnp.int32)
        rank = jnp.minimum(rank, FAST - 1)
        table_ref[T_FROM + j] = dist
        table_ref[T_RANK + j] = rank

        @pl.when(dist == NX)
        def _(j=j):
            for kv in range(2):
                pltpu.make_async_copy(caches[kv].at[j], bufs[kv].at[j], sems.at[j, kv]).start()

        for d in range(NX):

            @pl.when(dist == d)
            def _(j=j, d=d, rank=rank):
                for kv in range(2):
                    for h in range(heads):
                        moved_copy(
                            moved[d], kv, rank, h, heads, j, 0, bufs[kv], sems.at[j, kv * heads + h]
                        ).start()

    loads = [
        pltpu.make_async_copy(w_ref.at[:, pl.ds(i * half, half)], dst, wsems.at[i])
        for i, dst in enumerate((w0_ref, w1_ref))
    ]
    for load in loads:
        load.start()
    for c in reads:
        c.wait()
    wide_ref[...] = meta_ref[...].astype(jnp.float32).astype(jnp.int32)
    spill = pltpu.make_async_copy(wide_ref, ids_ref, ssem)
    spill.start()
    spill.wait()
    fit = ids_ref[0, 0, FAST]
    for d in range(1, NX):
        fit = jnp.minimum(fit, ids_ref[d, 0, FAST])
    for i in range(T_FIT, T_SIZE):
        table_ref[i] = fit
    for j in range(NODE):
        dist = table_ref[T_FROM + j]
        from_peer = ids_ref[jnp.minimum(dist, NX - 1), 0, table_ref[T_RANK + j]]
        table_ref[T_LEN + j] = jnp.where(dist == NX, blocks_ref[j], from_peer)

    def node(n, carry):
        local = table_ref[T_FROM + n] == NX
        blocks = table_ref[T_LEN + n]
        run = functools.partial(
            attend_node, n, scale=scale, tp=tp, q_ref=q_ref, nk_ref=nk_ref, nv_ref=nv_ref,
            kbuf=kbuf, vbuf=vbuf, att_ref=att_ref,
        )

        @pl.when(local)
        def _():
            for kv in range(2):
                pltpu.make_async_copy(caches[kv].at[n], bufs[kv].at[n], sems.at[n, kv]).wait()

        @pl.when(jnp.logical_not(local))
        def _():
            for kv in range(2):
                for h in range(heads):
                    moved_copy(
                        moved[0], kv, 0, h, heads, n, 0, bufs[kv], sems.at[n, kv * heads + h]
                    ).wait()

        @pl.when(local & (blocks == 2))
        def _():
            run(tokens=2 * BLK)

        @pl.when(blocks == 1)
        def _():
            run(tokens=BLK)

        return carry

    lax.fori_loop(0, NODE, node, 0)
    for load in loads:
        load.wait()


def early(where, own_list, blocks, queries, new_keys, new_values, keys, values, moved, weight):
    dim = keys.shape[3]
    inner, cols = weight.shape
    half = pltpu.VMEM((inner, cols // 2), weight.dtype)
    return pl.pallas_call(
        functools.partial(early_body, float(dim) ** -0.5),
        out_shape=(
            pltpu.VMEM(queries.shape, queries.dtype),
            half,
            half,
            jax.ShapeDtypeStruct((T_SIZE,), jnp.int32),
        ),
        in_specs=[SMEM, SMEM, SMEM, VMEM, VMEM, VMEM] + [ANY] * (3 + NX),
        out_specs=(VMEM, VMEM, VMEM, SMEM),
        scratch_shapes=[
            pltpu.VMEM(keys.shape, keys.dtype),
            pltpu.VMEM(keys.shape, keys.dtype),
            pltpu.VMEM((NX, META, 128), keys.dtype),
            pltpu.VMEM((NX, META, 128), jnp.int32),
            pltpu.SMEM((NX, META, 128), jnp.int32),
            pltpu.SemaphoreType.DMA((NODE, 2 * keys.shape[1])),
            pltpu.SemaphoreType.DMA((2,)),
            pltpu.SemaphoreType.DMA((NX,)),
            pltpu.SemaphoreType.DMA,
        ],
        compiler_params=params(8),
        name="early",
    )(where, own_list, blocks, queries, new_keys, new_values, keys, values, *moved, weight)


def project_side(part, tile, att_ref, w_ref, outs, side):
    half = outs[0].shape[1]

    def step(c, carry):
        at = pl.multiple_of(c * tile, tile)
        cols = pl.ds(pl.multiple_of(side * half + at, tile), tile)
        res = jnp.dot(att_ref[...], w_ref[:, cols], preferred_element_type=jnp.float32)
        for d in range(NTP):
            outs[2 * d + side][:, pl.ds(at, tile)] = res[d * part : (d + 1) * part].astype(
                outs[0].dtype
            )
        return carry

    lax.fori_loop(0, half // tile, step, 0)


def late_body(scale, tile, where_ref, table_ref, q_ref, nk_ref, nv_ref, *refs):
    firsts = refs[:NX]
    seconds = refs[NX : 2 * NX]
    old_ref, w_ref, att_ref = refs[2 * NX : 2 * NX + 3]
    outs = refs[2 * NX + 3 : 2 * NX + 3 + 2 * NTP]
    kbuf, vbuf, sems = refs[2 * NX + 3 + 2 * NTP :]
    del old_ref
    bufs = (kbuf, vbuf)
    heads = kbuf.shape[1]
    tp = where_ref[2]

    def is_late(n):
        return (table_ref[T_FROM + n] < NX) & (table_ref[T_LEN + n] == 2)

    def copies(n, d, rank):
        for b, group in enumerate((firsts, seconds)):
            for kv in range(2):
                for h in range(heads):
                    yield moved_copy(
                        group[d], kv, rank, h, heads, n, b, bufs[kv],
                        sems.at[n, (b * 2 + kv) * heads + h],
                    )

    def start(n, carry):
        for d in range(NX):

            @pl.when(is_late(n) & (table_ref[T_FROM + n] == d))
            def _(d=d):
                for c in copies(n, d, table_ref[T_RANK + n]):
                    c.start()

        return carry

    lax.fori_loop(0, NODE, start, 0)

    def node(n, carry):
        @pl.when(is_late(n))
        def _():
            for c in copies(n, 0, 0):
                c.wait()
            attend_node(n, 2 * BLK, scale, tp, q_ref, nk_ref, nv_ref, kbuf, vbuf, att_ref)

        return carry

    lax.fori_loop(0, NODE, node, 0)
    for side in range(2):
        project_side(outs[0].shape[0], tile, att_ref, w_ref, outs, side)


def late(where, table, queries, new_keys, new_values, firsts, seconds, att, weight, shape, tile):
    dim = shape[3]
    dtype = queries.dtype
    out = pltpu.VMEM((att.shape[0] // NTP, weight.shape[1] // 2), dtype)
    return pl.pallas_call(
        functools.partial(late_body, float(dim) ** -0.5, tile),
        out_shape=(pltpu.VMEM(att.shape, dtype),) + (out,) * (2 * NTP),
        in_specs=[SMEM, SMEM, VMEM, VMEM, VMEM] + [ANY] * (2 * NX) + [VMEM, VMEM],
        out_specs=(VMEM,) * (1 + 2 * NTP),
        scratch_shapes=[
            pltpu.VMEM(shape, dtype),
            pltpu.VMEM(shape, dtype),
            pltpu.SemaphoreType.DMA((NODE, 4 * shape[1])),
        ],
        input_output_aliases={5 + 2 * NX: 0},
        compiler_params=params(8),
        name="late",
    )(where, table, queries, new_keys, new_values, *firsts, *seconds, att, weight)


def project_body(tile, att_ref, w_ref, *outs):
    for side in range(2):
        project_side(outs[0].shape[0], tile, att_ref, w_ref, outs, side)


def project(att, weight, tile):
    out = pltpu.VMEM((att.shape[0] // NTP, weight.shape[1] // 2), att.dtype)
    return pl.pallas_call(
        functools.partial(project_body, tile),
        out_shape=(out,) * (2 * NTP),
        in_specs=[VMEM, VMEM],
        out_specs=(VMEM,) * (2 * NTP),
        compiler_params=params(6),
        name="project",
    )(att, weight)


def add2(a, b):
    return (a.astype(jnp.float32) + b.astype(jnp.float32)).astype(a.dtype)


def scatter_sum(parts):
    r0a, r0b, r1a, r1b, r2a, r2b, r3a, r3b = parts
    up, down = yperm(1), yperm(-1)
    relay_a = lax.ppermute(r2a, "tp", up)
    relay_b = lax.ppermute(r2b, "tp", down)
    direct_b = lax.ppermute(r1b, "tp", up)
    direct_a = lax.ppermute(r3a, "tp", down)
    far_a = lax.ppermute(add2(r1a, relay_a), "tp", up)
    far_b = lax.ppermute(add2(r3b, relay_b), "tp", down)
    f32 = jnp.float32
    out_a = r0a.astype(f32) + far_a.astype(f32) + direct_a.astype(f32)
    out_b = r0b.astype(f32) + far_b.astype(f32) + direct_b.astype(f32)
    return [out_a.astype(r0a.dtype), out_b.astype(r0a.dtype)]


def softmax_part(q, k, v, allowed, scale):
    logits = jnp.einsum("hqd,htd->hqt", q, k, preferred_element_type=jnp.float32) * scale
    logits = jnp.where(allowed[None], logits, -jnp.inf)
    top = jnp.max(logits, axis=-1)
    weights = jnp.exp(logits - top[..., None])
    total = jnp.sum(weights, axis=-1)
    out = jnp.einsum(
        "hqt,htd->hqd", weights.astype(v.dtype), v, preferred_element_type=jnp.float32
    )
    return out, top, total


def general(queries, keys, values, new_keys, new_values, weight, fork_src, cache_blocks):
    n_slot = lax.axis_size("slot")
    slot_here = lax.axis_index("slot")
    peers = lax.axis_size("role") * n_slot
    heads, tokens, dim = keys.shape[1:]
    group = queries.shape[1] // (heads * dim)
    scale = float(dim) ** -0.5
    n_src = fork_src.shape[0]
    meta = jnp.concatenate([fork_src, cache_blocks])
    meta = jnp.broadcast_to(meta[None], (peers, meta.shape[0]))
    meta = lax.all_to_all(meta, ("role", "slot"), 0, 0, tiled=True)
    parents = meta[:, :n_src].reshape(-1)
    blocks = meta[:n_slot, n_src:].reshape(-1)
    slots = jnp.arange(parents.shape[0], dtype=jnp.int32)
    from_here = ((parents != slots) & (parents // NODE == slot_here)).reshape(n_slot, NODE)
    local = (parents % NODE).reshape(n_slot, NODE)
    send = jnp.sum(jnp.where(from_here, local, 0), axis=1)
    own = lax.dynamic_slice_in_dim(parents, slot_here * NODE, NODE)
    moving = own != slot_here * NODE + jnp.arange(NODE, dtype=jnp.int32)
    source = own // NODE
    lengths = blocks[own] * BLK

    def gather(node, out):
        for kv, cache in enumerate((keys, values)):
            out = lax.dynamic_update_slice(
                out, cache[send[node]][None, None], (node, kv, 0, 0, 0)
            )
        return out

    both = lax.fori_loop(0, n_slot, gather, jnp.zeros((n_slot, 2) + keys.shape[1:], keys.dtype))
    both = lax.all_to_all(both, "slot", 0, 0, tiled=True)

    def node(j):
        def rows(a, n):
            a = lax.dynamic_slice_in_dim(a, j * STEP, STEP)
            a = a.reshape(STEP, heads, n, dim).transpose(1, 0, 2, 3)
            return a.reshape(heads, STEP * n, dim)

        got = jnp.where(moving[j], both[source[j]], jnp.stack([keys[j], values[j]]))
        q = rows(queries, group)
        step_of = jnp.arange(STEP * group) // group
        cache_ok = (jnp.arange(tokens) < lengths[j])[None, :]
        step_ok = jnp.arange(STEP)[None, :] <= step_of[:, None]
        co, cm, cs = softmax_part(q, got[0], got[1], cache_ok, scale)
        so, sm, ss = softmax_part(q, rows(new_keys, 1), rows(new_values, 1), step_ok, scale)
        top = jnp.maximum(cm, sm)
        cw = jnp.exp(cm - top)
        sw = jnp.exp(sm - top)
        out = (co * cw[..., None] + so * sw[..., None]) / (cs * cw + ss * sw)[..., None]
        out = out.astype(queries.dtype).reshape(heads, STEP, group, dim)
        return out.transpose(1, 0, 2, 3).reshape(STEP, heads * group * dim)

    att = lax.map(node, jnp.arange(NODE)).reshape(queries.shape)
    partial = jnp.dot(att, weight, preferred_element_type=jnp.float32).astype(att.dtype)
    partial = partial.reshape(NTP, -1, partial.shape[1])
    partial = lax.all_to_all(partial, "tp", 0, 0, tiled=True)
    return jnp.sum(partial.astype(jnp.float32), axis=0).astype(att.dtype)


def shards(
    queries, cache_keys, cache_values, new_keys, new_values, out_weight, fork_src, cache_blocks
):
    queries, keys, values = queries[0], cache_keys[0], cache_values[0]
    new_keys, new_values, weight = new_keys[0], new_values[0], out_weight[0]
    n_slot = lax.axis_size("slot")
    where = jnp.stack([lax.axis_index(name).astype(jnp.int32) for name in ("role", "slot", "tp")])

    mine = lax.ppermute(fork_src, ("role", "slot"), halves_perm(0, n_slot))
    other = lax.ppermute(fork_src, ("role", "slot"), halves_perm(1, n_slot))
    first, second, own_list = pack(where, mine, other, cache_blocks, keys, values)
    first1 = ring_step((first, first))
    second1 = ring_step((second, second))
    lists = [own_list]
    for d in (1, 2, 3):
        lists.append(lax.ppermute(own_list, "slot", xperm(-d)))
    first2 = ring_step(first1)
    first3 = ring_step(first2)
    second1b, _ = lax.optimization_barrier((second1, first3[0]))
    second2 = ring_step(second1b)
    got_first = ring_list(first, first1, first2, first3, ring_last(first3))
    *outs_first, picks = select_first(where, lists, got_first)
    moved_first = [outs_first[0]]
    for d in (1, 2, 3):
        moved_first.append(lax.ppermute(outs_first[d], "slot", xperm(d)))
    second2b, _ = lax.optimization_barrier((second2, outs_first[0]))
    second3 = ring_step(second2b)
    got_second = ring_list(second, second1, second2, second3, ring_last(second3))
    outs_second = select_second(picks, got_second)
    moved_second = [outs_second[0]]
    for d in (1, 2, 3):
        moved_second.append(lax.ppermute(outs_second[d], "slot", xperm(d)))
    att, weight0, weight1, table = early(
        where, own_list, cache_blocks, queries, new_keys, new_values, keys, values,
        moved_first, weight,
    )
    att, *part0 = late(
        where, table, queries, new_keys, new_values, moved_first, moved_second, att, weight0,
        keys.shape, 512,
    )
    part1 = project(att, weight1, 512)
    pieces = []
    for parts in (part0, part1):
        pieces += scatter_sum(parts)
    out = jnp.concatenate(pieces, axis=1)
    args = (queries, keys, values, new_keys, new_values, weight, fork_src, cache_blocks)
    out = lax.cond(table[T_FIT] == 1, lambda o, *_: o, lambda o, *a: general(*a), out, *args)
    return out[None]


def solution(mesh):
    in_specs = (
        P("role", "slot", "tp"),
        P("role", "slot", "tp", None, None),
        P("role", "slot", "tp", None, None),
        P("role", "slot", "tp"),
        P("role", "slot", "tp"),
        P("role", "tp", None),
        P(("role", "slot")),
        P("slot"),
    )
    out_specs = P("role", ("slot", "tp"), None)

    return jax.shard_map(shards, mesh=mesh, in_specs=in_specs, out_specs=out_specs, check_vma=False)
```

```python
import functools

import jax
import jax.numpy as jnp
from jax import lax
from jax.experimental import pallas as pl
from jax.experimental.pallas import tpu as pltpu
from jax.sharding import PartitionSpec as P


BLK = 128
NX = 4
NZ = 8
NTP = 4
NODE = 8
STEP = 32
FAST = 2
META = 16

T_FROM = 0
T_RANK = 8
T_LEN = 16
T_FIT = 24
T_SIZE = 32

SMEM = pl.BlockSpec(memory_space=pltpu.SMEM)
VMEM = pl.BlockSpec(memory_space=pltpu.VMEM)
ANY = pl.BlockSpec(memory_space=pl.ANY)


def params(mib):
    return pltpu.CompilerParams(vmem_limit_bytes=mib << 20)


def zperm(d):
    return [(s, (s + NX * d) % (NX * NZ)) for s in range(NX * NZ)]


def xperm(d):
    return [(s, (s // NX) * NX + (s % NX + d) % NX) for s in range(NX * NZ)]


def yperm(d):
    return [(t, (t + d) % NTP) for t in range(NTP)]


def halves_perm(other, n_slot):
    pairs = []
    for role in range(2):
        for k in range(n_slot // 2):
            for h in range(2):
                dest = (h ^ other) * n_slot + role * (n_slot // 2) + k
                pairs.append((role * n_slot + 2 * k + h, dest))
    return pairs


def lane_row(values):
    lane = lax.broadcasted_iota(jnp.int32, (META, 128), 1)
    tile = jnp.zeros((META, 128), jnp.float32)
    for i, value in enumerate(values):
        tile = jnp.where(lane == i, value.astype(jnp.float32), tile)
    return tile.astype(jnp.bfloat16)


def column_counts(here, list_ref, col):
    base = here * NODE
    counts = [jnp.int32(0)] * NX
    for j in range(NODE):
        parent = list_ref[j]
        dist = (col - (parent // NODE) % NX + NX) % NX
        dist = jnp.where(parent == base + j, NX, dist)
        counts = [c + (dist == d).astype(jnp.int32) for d, c in enumerate(counts)]
    return counts


def pack_body(
    where_ref, mine_ref, other_ref, blocks_ref, keys_ref, values_ref,
    first_ref, second_ref, list_ref, sems,
):
    role = where_ref[0]
    here = where_ref[1]
    base = here * NODE
    count = jnp.int32(0)
    low = jnp.int32(0)
    high = jnp.int32(0)
    for j in range(NODE):
        h, k = divmod(j, NODE // 2)
        parent = jnp.where(role == h, mine_ref[k], other_ref[k])
        list_ref[j] = parent
        keep = parent == base + j
        low = jnp.where(keep & (count == 0), j, low)
        high = jnp.where(keep, j, high)
        count = count + keep.astype(jnp.int32)
    heads = keys_ref.shape[1]
    copies = []
    for b, out in enumerate((first_ref, second_ref)):
        for s, node in enumerate((low, high)):
            for kv, src in enumerate((keys_ref, values_ref)):
                for h in range(heads):
                    row = ((kv * 2 + s) * heads + h) * BLK
                    copies.append(
                        pltpu.make_async_copy(
                            src.at[node, h, pl.ds(b * BLK, BLK), :],
                            out.at[pl.ds(row, BLK), :],
                            sems.at[len(copies)],
                        )
                    )
    for c in copies:
        c.start()
    counts = column_counts(here, list_ref, here % NX)
    most = jnp.maximum(jnp.maximum(counts[0], counts[1]), jnp.maximum(counts[2], counts[3]))
    fit = (most <= FAST).astype(jnp.int32)
    rows = second_ref.shape[0]
    first_ref[rows : rows + META, :] = lane_row(
        (low, high, blocks_ref[low], blocks_ref[high], fit)
    )
    for c in copies:
        c.wait()


def pack(where, mine, other, blocks, keys, values):
    heads, _, dim = keys.shape[1:]
    rows = 4 * heads * BLK
    return pl.pallas_call(
        pack_body,
        out_shape=(
            pltpu.VMEM((rows + META, dim), keys.dtype),
            pltpu.VMEM((rows, dim), keys.dtype),
            jax.ShapeDtypeStruct((NODE,), jnp.int32),
        ),
        in_specs=[SMEM, SMEM, SMEM, SMEM, ANY, ANY],
        out_specs=(VMEM, VMEM, SMEM),
        scratch_shapes=[pltpu.SemaphoreType.DMA((8 * heads,))],
        compiler_params=params(2),
        name="pack",
    )(where, mine, other, blocks, keys, values)


def ring_step(pair):
    up, down = pair
    return lax.ppermute(up, "slot", zperm(1)), lax.ppermute(down, "slot", zperm(-1))


def ring_last(pair, up):
    if up:
        return lax.ppermute(pair[0], "slot", zperm(1))
    return lax.ppermute(pair[1], "slot", zperm(-1))


def ring_list(own, one, two, three, last):
    return [own, one[0], two[0], three[0], last, three[1], two[1], one[1]]


def issue_units(pick_ref, srcs, outs, size, sems):
    for d in range(NX):

        def unit(i, carry, d=d):
            u = d * FAST + i
            rel = pick_ref[u]
            rank = pick_ref[NX * FAST + u]
            for r in range(NZ):

                @pl.when(rel == r)
                def _(r=r):
                    for kv in range(2):
                        at = pl.multiple_of((kv * 2 + rank) * size, META)
                        to = pl.multiple_of((kv * 2 + i) * size, META)
                        pltpu.make_async_copy(
                            srcs[r].at[pl.ds(at, size), :],
                            outs[d].at[pl.ds(to, size), :],
                            sems.at[u * 2 + kv],
                        ).start()

            return carry

        lax.fori_loop(0, FAST, unit, 0)


def wait_units(srcs, outs, size, sems):
    def unit(n, carry):
        pltpu.make_async_copy(
            srcs[0].at[pl.ds(0, size), :], outs[0].at[pl.ds(0, size), :], sems.at[n]
        ).wait()
        return carry

    lax.fori_loop(0, NX * FAST * 2, unit, 0)


def select_first_body(where_ref, *refs):
    lists = refs[:NX]
    srcs = refs[NX : NX + NZ]
    outs = refs[NX + NZ : 2 * NX + NZ]
    pick_ref, meta_ref, wide_ref, ids_ref, sems, msem, ssem = refs[2 * NX + NZ :]
    size = outs[0].shape[0] // 4 // META * META
    here = where_ref[1]
    row = here // NX
    col = here % NX
    reads = []
    for rel in range(NZ):
        tile = srcs[rel].at[pl.ds(4 * size, META), :]
        reads.append(pltpu.make_async_copy(tile, meta_ref.at[rel], msem.at[rel]))
    for c in reads:
        c.start()
    for c in reads:
        c.wait()
    wide_ref[...] = meta_ref[...].astype(jnp.float32).astype(jnp.int32)
    spill = pltpu.make_async_copy(wide_ref, ids_ref, ssem)
    spill.start()
    spill.wait()
    for u in range(2 * NX * FAST):
        pick_ref[u] = 0
    for d in range(NX):
        base = (row * NX + (col + d) % NX) * NODE

        def scan(j, count, d=d, base=base):
            parent = lists[d][j]
            source = parent // NODE
            hit = (parent != base + j) & (source % NX == col)
            rel = (row - source // NX + NZ) % NZ

            @pl.when(hit & (count < FAST))
            def _():
                pick_ref[d * FAST + count] = rel
                pick_ref[NX * FAST + d * FAST + count] = (
                    parent % NODE == ids_ref[rel, 0, 1]
                ).astype(jnp.int32)

            return count + hit.astype(jnp.int32)

        lax.fori_loop(0, NODE, scan, jnp.int32(0))

    issue_units(pick_ref, srcs, outs, size, sems)
    fit = ids_ref[0, 0, 4]
    for rel in range(1, NZ):
        fit = jnp.minimum(fit, ids_ref[rel, 0, 4])
    for d in range(NX):
        sizes = []
        for i in range(FAST):
            u = d * FAST + i
            sizes.append(ids_ref[pick_ref[u], 0, 2 + pick_ref[NX * FAST + u]])
        outs[d][4 * size : 4 * size + META, :] = lane_row((sizes[0], sizes[1], fit))
    wait_units(srcs, outs, size, sems)


def select_first(where, lists, srcs):
    own = srcs[0]
    out = pltpu.VMEM(own.shape, own.dtype)
    return pl.pallas_call(
        select_first_body,
        out_shape=(out,) * NX + (jax.ShapeDtypeStruct((2 * NX * FAST,), jnp.int32),),
        in_specs=[SMEM] * (1 + NX) + [ANY] * NZ,
        out_specs=(VMEM,) * NX + (SMEM,),
        scratch_shapes=[
            pltpu.VMEM((NZ, META, 128), own.dtype),
            pltpu.VMEM((NZ, META, 128), jnp.int32),
            pltpu.SMEM((NZ, META, 128), jnp.int32),
            pltpu.SemaphoreType.DMA((NX * FAST * 2,)),
            pltpu.SemaphoreType.DMA((NZ,)),
            pltpu.SemaphoreType.DMA,
        ],
        compiler_params=params(2),
        name="select_first",
    )(where, *lists, *srcs)


def select_second_body(pick_ref, *refs):
    srcs = refs[:NZ]
    outs = refs[NZ : NZ + NX]
    sems = refs[NZ + NX]
    size = outs[0].shape[0] // 4

    issue_units(pick_ref, srcs, outs, size, sems)
    wait_units(srcs, outs, size, sems)


def select_second(picks, srcs):
    own = srcs[0]
    out = pltpu.VMEM(own.shape, own.dtype)
    return pl.pallas_call(
        select_second_body,
        out_shape=(out,) * NX,
        in_specs=[SMEM] + [ANY] * NZ,
        out_specs=(VMEM,) * NX,
        scratch_shapes=[pltpu.SemaphoreType.DMA((NX * FAST * 2,))],
        compiler_params=params(2),
        name="select_second",
    )(picks, *srcs)


def attend_unit(scale, q, k, v, nk, nv, step_ok):
    nt = (((1,), (1,)), ((), ()))
    nn = (((1,), (0,)), ((), ()))
    f32 = jnp.float32
    sc = lax.dot_general(q, k, nt, preferred_element_type=f32) * scale
    ss = lax.dot_general(q, nk, nt, preferred_element_type=f32) * scale
    ss = jnp.where(step_ok, ss, -jnp.inf)
    top = jnp.maximum(jnp.max(sc, axis=1, keepdims=True), jnp.max(ss, axis=1, keepdims=True))
    pc = jnp.exp(sc - top)
    ps = jnp.exp(ss - top)
    total = jnp.sum(pc, axis=1, keepdims=True) + jnp.sum(ps, axis=1, keepdims=True)
    o = lax.dot_general(pc.astype(v.dtype), v, nn, preferred_element_type=f32)
    o = o + lax.dot_general(ps.astype(v.dtype), nv, nn, preferred_element_type=f32)
    return (o / total).astype(v.dtype)


def attend_node(n, tokens, scale, tp, q_ref, nk_ref, nv_ref, kbuf, vbuf, att_ref):
    heads, _, dim = kbuf.shape[1:]
    group = q_ref.shape[1] // (heads * dim)
    per = NODE // NTP
    at = pl.multiple_of(n * STEP, STEP)
    to = ((n // per - tp + NTP) % NTP) * per + n % per
    to = pl.multiple_of(to * STEP, STEP)
    rows = STEP * group
    step_of = lax.broadcasted_iota(jnp.int32, (rows, STEP), 0) % STEP
    step_ok = lax.broadcasted_iota(jnp.int32, (rows, STEP), 1) <= step_of

    def head(h, carry):
        base = h * group * dim

        def cols(g):
            return pl.ds(pl.multiple_of(base + g * dim, dim), dim)

        mine = pl.ds(pl.multiple_of(h * dim, dim), dim)
        q = jnp.concatenate([q_ref[pl.ds(at, STEP), cols(g)] for g in range(group)], axis=0)
        o = attend_unit(
            scale,
            q,
            kbuf[n, h, :tokens],
            vbuf[n, h, :tokens],
            nk_ref[pl.ds(at, STEP), mine],
            nv_ref[pl.ds(at, STEP), mine],
            step_ok,
        )
        for g in range(group):
            att_ref[pl.ds(to, STEP), cols(g)] = o[g * STEP : (g + 1) * STEP]
        return carry

    lax.fori_loop(0, heads, head, 0)


def moved_copy(src, kv, rank, h, heads, j, b, buf, sem):
    at = pl.multiple_of(((kv * 2 + rank) * heads + h) * BLK, BLK)
    return pltpu.make_async_copy(
        src.at[pl.ds(at, BLK), :], buf.at[j, h, pl.ds(b * BLK, BLK), :], sem
    )


def early_body(scale, where_ref, list_ref, blocks_ref, q_ref, nk_ref, nv_ref, *refs):
    caches = refs[0:2]
    moved = refs[2 : 2 + NX]
    w_ref, att_ref, w0_ref, table_ref = refs[2 + NX : 6 + NX]
    kbuf, vbuf, meta_ref, wide_ref, ids_ref, sems, wsem, msem, ssem = refs[6 + NX :]
    bufs = (kbuf, vbuf)
    heads = kbuf.shape[1]
    here = where_ref[1]
    tp = where_ref[2]
    col = here % NX
    half = w0_ref.shape[1]
    reads = []
    for d in range(NX):
        at = moved[d].shape[0] - META
        reads.append(
            pltpu.make_async_copy(moved[d].at[pl.ds(at, META), :], meta_ref.at[d], msem.at[d])
        )
    for c in reads:
        c.start()

    def place(j, counts):
        parent = list_ref[j]
        moving = parent != here * NODE + j
        dist = jnp.where(moving, (col - (parent // NODE) % NX + NX) % NX, NX)
        rank = jnp.int32(0)
        after = []
        for d in range(NX):
            hit = dist == d
            rank = jnp.where(hit, counts[d], rank)
            after.append(counts[d] + hit.astype(jnp.int32))
        rank = jnp.minimum(rank, FAST - 1)
        table_ref[T_FROM + j] = dist
        table_ref[T_RANK + j] = rank

        @pl.when(dist == NX)
        def _():
            for kv in range(2):
                pltpu.make_async_copy(caches[kv].at[j], bufs[kv].at[j], sems.at[j, kv]).start()

        for d in range(NX):

            @pl.when(dist == d)
            def _(d=d):
                for kv in range(2):
                    for h in range(heads):
                        moved_copy(
                            moved[d], kv, rank, h, heads, j, 0, bufs[kv], sems.at[j, kv * heads + h]
                        ).start()

        return tuple(after)

    lax.fori_loop(0, NODE, place, (jnp.int32(0),) * NX)
    load = pltpu.make_async_copy(w_ref.at[:, pl.ds(0, half)], w0_ref, wsem)
    load.start()
    for c in reads:
        c.wait()
    wide_ref[...] = meta_ref[...].astype(jnp.float32).astype(jnp.int32)
    spill = pltpu.make_async_copy(wide_ref, ids_ref, ssem)
    spill.start()
    spill.wait()
    fit = ids_ref[0, 0, FAST]
    for d in range(1, NX):
        fit = jnp.minimum(fit, ids_ref[d, 0, FAST])
    for i in range(T_FIT, T_SIZE):
        table_ref[i] = fit

    def measure(j, carry):
        dist = table_ref[T_FROM + j]
        from_peer = ids_ref[jnp.minimum(dist, NX - 1), 0, table_ref[T_RANK + j]]
        table_ref[T_LEN + j] = jnp.where(dist == NX, blocks_ref[j], from_peer)
        return carry

    lax.fori_loop(0, NODE, measure, 0)

    def node(n, carry):
        local = table_ref[T_FROM + n] == NX
        blocks = table_ref[T_LEN + n]
        run = functools.partial(
            attend_node, n, scale=scale, tp=tp, q_ref=q_ref, nk_ref=nk_ref, nv_ref=nv_ref,
            kbuf=kbuf, vbuf=vbuf, att_ref=att_ref,
        )

        @pl.when(local)
        def _():
            for kv in range(2):
                pltpu.make_async_copy(caches[kv].at[n], bufs[kv].at[n], sems.at[n, kv]).wait()

        @pl.when(jnp.logical_not(local))
        def _():
            for kv in range(2):
                for h in range(heads):
                    moved_copy(
                        moved[0], kv, 0, h, heads, n, 0, bufs[kv], sems.at[n, kv * heads + h]
                    ).wait()

        @pl.when(local & (blocks == 2))
        def _():
            run(tokens=2 * BLK)

        @pl.when(blocks == 1)
        def _():
            run(tokens=BLK)

        return carry

    lax.fori_loop(0, NODE, node, 0)
    load.wait()


def early(where, own_list, blocks, queries, new_keys, new_values, keys, values, moved, weight):
    dim = keys.shape[3]
    inner, cols = weight.shape
    half = pltpu.VMEM((inner, cols // 2), weight.dtype)
    return pl.pallas_call(
        functools.partial(early_body, float(dim) ** -0.5),
        out_shape=(
            pltpu.VMEM(queries.shape, queries.dtype),
            half,
            jax.ShapeDtypeStruct((T_SIZE,), jnp.int32),
        ),
        in_specs=[SMEM, SMEM, SMEM, VMEM, VMEM, VMEM] + [ANY] * (3 + NX),
        out_specs=(VMEM, VMEM, SMEM),
        scratch_shapes=[
            pltpu.VMEM(keys.shape, keys.dtype),
            pltpu.VMEM(keys.shape, keys.dtype),
            pltpu.VMEM((NX, META, 128), keys.dtype),
            pltpu.VMEM((NX, META, 128), jnp.int32),
            pltpu.SMEM((NX, META, 128), jnp.int32),
            pltpu.SemaphoreType.DMA((NODE, 2 * keys.shape[1])),
            pltpu.SemaphoreType.DMA,
            pltpu.SemaphoreType.DMA((NX,)),
            pltpu.SemaphoreType.DMA,
        ],
        compiler_params=params(8),
        name="early",
    )(where, own_list, blocks, queries, new_keys, new_values, keys, values, *moved, weight)


def project_half(chunk, tile, att_ref, w_ref, own_ref, relay_a, relay_b, da, db, ca, cb):
    part, half = relay_a.shape
    base = chunk * half

    def step(side, c, carry):
        at = pl.multiple_of(c * tile, tile)
        cols = pl.ds(pl.multiple_of(side * half + at, tile), tile)
        far = pl.ds(pl.multiple_of(base + at, tile), tile)
        res = jnp.dot(att_ref[...], w_ref[:, cols], preferred_element_type=jnp.float32)
        res = res.astype(own_ref.dtype)
        own_ref[:, cols] = res[:part]
        (ca, db)[side][:, far] = res[part : 2 * part]
        (relay_a, relay_b)[side][:, pl.ds(at, tile)] = res[2 * part : 3 * part]
        (da, cb)[side][:, far] = res[3 * part :]
        return carry

    for side in range(2):
        lax.fori_loop(0, half // tile, functools.partial(step, side), 0)


def late_body(scale, tile, where_ref, table_ref, q_ref, nk_ref, nv_ref, *refs):
    firsts = refs[:NX]
    seconds = refs[NX : 2 * NX]
    old_ref, w0_ref, w_ref, att_ref, w1_ref = refs[2 * NX : 2 * NX + 5]
    outs = refs[2 * NX + 5 : 2 * NX + 12]
    kbuf, vbuf, sems, wsem = refs[2 * NX + 12 :]
    del old_ref
    bufs = (kbuf, vbuf)
    heads = kbuf.shape[1]
    tp = where_ref[2]
    half = w1_ref.shape[1]

    def is_late(n):
        return (table_ref[T_FROM + n] < NX) & (table_ref[T_LEN + n] == 2)

    def copies(n, d, rank):
        for b, group in enumerate((firsts, seconds)):
            for kv in range(2):
                for h in range(heads):
                    yield moved_copy(
                        group[d], kv, rank, h, heads, n, b, bufs[kv],
                        sems.at[n, (b * 2 + kv) * heads + h],
                    )

    def start(n, carry):
        for d in range(NX):

            @pl.when(is_late(n) & (table_ref[T_FROM + n] == d))
            def _(d=d):
                for c in copies(n, d, table_ref[T_RANK + n]):
                    c.start()

        return carry

    lax.fori_loop(0, NODE, start, 0)
    load = pltpu.make_async_copy(w_ref.at[:, pl.ds(half, half)], w1_ref, wsem)
    load.start()

    def node(n, carry):
        @pl.when(is_late(n))
        def _():
            for c in copies(n, 0, 0):
                c.wait()
            attend_node(n, 2 * BLK, scale, tp, q_ref, nk_ref, nv_ref, kbuf, vbuf, att_ref)

        return carry

    lax.fori_loop(0, NODE, node, 0)
    project_half(0, tile, att_ref, w0_ref, *outs)
    load.wait()


def late(where, table, queries, new_keys, new_values, moved, att, weight0, weight, shape, tile):
    dtype = queries.dtype
    part = att.shape[0] // NTP
    inner, half = weight0.shape
    wide = pltpu.VMEM((part, half), dtype)
    slim = pltpu.VMEM((part, half // 2), dtype)
    return pl.pallas_call(
        functools.partial(late_body, float(shape[3]) ** -0.5, tile),
        out_shape=(pltpu.VMEM(att.shape, dtype), pltpu.VMEM((inner, half), dtype))
        + (wide, slim, slim, wide, wide, wide, wide),
        in_specs=[SMEM, SMEM, VMEM, VMEM, VMEM] + [ANY] * (2 * NX) + [VMEM, VMEM, ANY],
        out_specs=(VMEM,) * 9,
        scratch_shapes=[
            pltpu.VMEM(shape, dtype),
            pltpu.VMEM(shape, dtype),
            pltpu.SemaphoreType.DMA((NODE, 4 * shape[1])),
            pltpu.SemaphoreType.DMA,
        ],
        input_output_aliases={5 + 2 * NX: 0},
        compiler_params=params(8),
        name="late",
    )(where, table, queries, new_keys, new_values, *moved, att, weight0, weight)


def project_body(tile, att_ref, w_ref, da0, db0, ca0, cb0, own_ref, ra, rb, da, db, ca, cb):
    del da0, db0, ca0, cb0
    project_half(1, tile, att_ref, w_ref, own_ref, ra, rb, da, db, ca, cb)


def project(att, weight, shared, tile):
    part = att.shape[0] // NTP
    half = weight.shape[1]
    wide = pltpu.VMEM((part, half), att.dtype)
    slim = pltpu.VMEM((part, half // 2), att.dtype)
    return pl.pallas_call(
        functools.partial(project_body, tile),
        out_shape=(wide, slim, slim, wide, wide, wide, wide),
        in_specs=[VMEM] * 6,
        out_specs=(VMEM,) * 7,
        input_output_aliases={2 + i: 3 + i for i in range(4)},
        compiler_params=params(6),
        name="project",
    )(att, weight, *shared)


def combine_body(base_ref, low_ref, high_ref, out_ref):
    half = low_ref.shape[1]
    for i, ref in enumerate((low_ref, high_ref)):
        cols = slice(i * half, (i + 1) * half)
        total = base_ref[:, cols].astype(jnp.float32) + ref[...].astype(jnp.float32)
        out_ref[:, cols] = total.astype(out_ref.dtype)


def combine(base, low, high):
    return pl.pallas_call(
        combine_body,
        out_shape=pltpu.VMEM(base.shape, base.dtype),
        in_specs=[VMEM] * 3,
        out_specs=VMEM,
        compiler_params=params(2),
        name="combine",
    )(base, low, high)


def finish_body(own0, own1, da, db, fa, fb, out_ref):
    half = own0.shape[1] // 2
    for c, own in enumerate((own0, own1)):
        here = slice(c * half, (c + 1) * half)
        for side, (near, far) in enumerate(((da, fa), (db, fb))):
            cols = slice(side * half, (side + 1) * half)
            total = own[:, cols].astype(jnp.float32) + near[:, here].astype(jnp.float32)
            total = total + far[:, here].astype(jnp.float32)
            at = 2 * c * half + side * half
            out_ref[:, at : at + half] = total.astype(out_ref.dtype)


def finish(*args):
    part, half = args[0].shape
    return pl.pallas_call(
        finish_body,
        out_shape=jax.ShapeDtypeStruct((part, 2 * half), args[0].dtype),
        in_specs=[VMEM] * 6,
        out_specs=VMEM,
        compiler_params=params(4),
        name="finish",
    )(*args)


def softmax_part(q, k, v, allowed, scale):
    logits = jnp.einsum("hqd,htd->hqt", q, k, preferred_element_type=jnp.float32) * scale
    logits = jnp.where(allowed[None], logits, -jnp.inf)
    top = jnp.max(logits, axis=-1)
    weights = jnp.exp(logits - top[..., None])
    total = jnp.sum(weights, axis=-1)
    out = jnp.einsum(
        "hqt,htd->hqd", weights.astype(v.dtype), v, preferred_element_type=jnp.float32
    )
    return out, top, total


def general(
    where, mine, other, queries, keys, values, new_keys, new_values, weight, cache_blocks
):
    n_slot = lax.axis_size("slot")
    slot_here = lax.axis_index("slot")
    tp_here = lax.axis_index("tp")
    heads, tokens, dim = keys.shape[1:]
    group = queries.shape[1] // (heads * dim)
    scale = float(dim) ** -0.5
    first, second, own = pack(where, mine, other, cache_blocks, keys, values)
    rows = second.shape[0]
    moving = own != slot_here * NODE + jnp.arange(NODE, dtype=jnp.int32)
    source = own // NODE

    def turn(t, carry):
        near, far, got, blocks = carry
        from_slot = (slot_here - t + n_slot) % n_slot
        ids = near[rows].astype(jnp.int32)
        shape = (2, 2, heads, BLK, dim)
        both = jnp.concatenate([near[:rows].reshape(shape), far.reshape(shape)], axis=3)
        hit = moving & (source == from_slot)
        rank = own % NODE == ids[1]
        new = jnp.where(rank[:, None, None, None, None], both[None, :, 1], both[None, :, 0])
        got = jnp.where(hit[:, None, None, None, None], new, got)
        blocks = jnp.where(hit, jnp.where(rank, ids[3], ids[2]), blocks)
        pairs = [(s, (s + 1) % n_slot) for s in range(n_slot)]
        joined = lax.ppermute(jnp.concatenate([near, far]), "slot", pairs)
        return joined[: rows + META], joined[rows + META :], got, blocks

    local = jnp.stack([keys, values], axis=1)
    got, blocks = lax.fori_loop(0, n_slot, turn, (first, second, local, cache_blocks))[2:]

    def node(j):
        def rows_of(a, n):
            a = lax.dynamic_slice_in_dim(a, j * STEP, STEP)
            a = a.reshape(STEP, heads, n, dim).transpose(1, 0, 2, 3)
            return a.reshape(heads, STEP * n, dim)

        q = rows_of(queries, group)
        step_of = jnp.arange(STEP * group) // group
        cache_ok = (jnp.arange(tokens) < blocks[j] * BLK)[None, :]
        step_ok = jnp.arange(STEP)[None, :] <= step_of[:, None]
        co, cm, cs = softmax_part(q, got[j, 0], got[j, 1], cache_ok, scale)
        so, sm, ss = softmax_part(q, rows_of(new_keys, 1), rows_of(new_values, 1), step_ok, scale)
        top = jnp.maximum(cm, sm)
        cw = jnp.exp(cm - top)
        sw = jnp.exp(sm - top)
        out = (co * cw[..., None] + so * sw[..., None]) / (cs * cw + ss * sw)[..., None]
        out = out.astype(queries.dtype).reshape(heads, STEP, group, dim)
        return out.transpose(1, 0, 2, 3).reshape(STEP, heads * group * dim)

    att = lax.map(node, jnp.arange(NODE)).reshape(queries.shape)
    partial = jnp.dot(att, weight, preferred_element_type=jnp.float32)
    partial = partial.reshape(NTP, -1, partial.shape[1])

    def piece(i):
        return lax.dynamic_index_in_dim(partial, (tp_here + i) % NTP, 0, keepdims=False)

    def pass_on(k, total):
        return lax.ppermute(total, "tp", yperm(1)) + piece(NTP - 2 - k)

    return lax.fori_loop(0, NTP - 1, pass_on, piece(NTP - 1)).astype(att.dtype)


def shards(
    queries, cache_keys, cache_values, new_keys, new_values, out_weight, fork_src, cache_blocks
):
    queries, keys, values = queries[0], cache_keys[0], cache_values[0]
    new_keys, new_values, weight = new_keys[0], new_values[0], out_weight[0]
    n_slot = lax.axis_size("slot")
    where = jnp.stack([lax.axis_index(name).astype(jnp.int32) for name in ("role", "slot", "tp")])

    mine = lax.ppermute(fork_src, ("role", "slot"), halves_perm(0, n_slot))
    other = lax.ppermute(fork_src, ("role", "slot"), halves_perm(1, n_slot))
    first, second, own_list = pack(where, mine, other, cache_blocks, keys, values)
    first1 = ring_step((first, first))
    second1 = ring_step((second, second))
    lists = [own_list]
    for d in (1, 2, 3):
        lists.append(lax.ppermute(own_list, "slot", xperm(-d)))
    first2 = ring_step(first1)
    second2 = ring_step(second1)
    first3 = ring_step(first2)
    second3 = ring_step(second2)
    got_first = ring_list(first, first1, first2, first3, ring_last(first3, True))
    got_second = ring_list(second, second1, second2, second3, ring_last(second3, False))
    *outs_first, picks = select_first(where, lists, got_first)
    moved = [outs_first[0]]
    for d in (1, 2, 3):
        moved.append(lax.ppermute(outs_first[d], "slot", xperm(d)))
    outs_second = select_second(picks, got_second)
    att, weight0, table = early(
        where, own_list, cache_blocks, queries, new_keys, new_values, keys, values, moved,
        weight,
    )
    moved = moved + [outs_second[0]]
    for d in (1, 2, 3):
        moved.append(lax.ppermute(outs_second[d], "slot", xperm(d)))
    att, weight1, own0, relay_a0, relay_b0, *shared = late(
        where, table, queries, new_keys, new_values, moved, att, weight0, weight, keys.shape, 512
    )
    up, down = yperm(1), yperm(-1)
    relay_a0 = lax.ppermute(relay_a0, "tp", up)
    relay_b0 = lax.ppermute(relay_b0, "tp", down)
    own1, relay_a1, relay_b1, da, db, ca, cb = project(att, weight1, shared, 512)
    relay_a1 = lax.ppermute(relay_a1, "tp", up)
    relay_b1 = lax.ppermute(relay_b1, "tp", down)
    da = lax.ppermute(da, "tp", down)
    db = lax.ppermute(db, "tp", up)
    far_a = lax.ppermute(combine(ca, relay_a0, relay_a1), "tp", up)
    far_b = lax.ppermute(combine(cb, relay_b0, relay_b1), "tp", down)
    out = finish(own0, own1, da, db, far_a, far_b)
    args = (where, mine, other, queries, keys, values, new_keys, new_values, weight, cache_blocks)
    out = lax.cond(table[T_FIT] == 1, lambda o, *_: o, lambda o, *a: general(*a), out, *args)
    return out[None]


def solution(mesh):
    in_specs = (
        P("role", "slot", "tp"),
        P("role", "slot", "tp", None, None),
        P("role", "slot", "tp", None, None),
        P("role", "slot", "tp"),
        P("role", "slot", "tp"),
        P("role", "tp", None),
        P(("role", "slot")),
        P("slot"),
    )
    out_specs = P("role", ("slot", "tp"), None)

    return jax.shard_map(shards, mesh=mesh, in_specs=in_specs, out_specs=out_specs, check_vma=False)
```

```python
import functools
import math

import jax
import jax.numpy as jnp
from jax import lax
from jax.experimental import pallas as pl
from jax.experimental.pallas import tpu as pltpu
from jax.sharding import PartitionSpec as P


BLK = 128
NX = 4
NZ = 8
NTP = 4
NODE = 8
STEP = 32
FAST = 2
META = 16

T_FROM = 0
T_RANK = 8
T_LEN = 16
T_FIT = 24
T_SIZE = 32

SMEM = pl.BlockSpec(memory_space=pltpu.SMEM)
VMEM = pl.BlockSpec(memory_space=pltpu.VMEM)
ANY = pl.BlockSpec(memory_space=pl.ANY)


def params(mib):
    return pltpu.CompilerParams(vmem_limit_bytes=mib << 20)


def zperm(d):
    return [(s, (s + NX * d) % (NX * NZ)) for s in range(NX * NZ)]


def xperm(d):
    return [(s, (s // NX) * NX + (s % NX + d) % NX) for s in range(NX * NZ)]


def yperm(d):
    return [(t, (t + d) % NTP) for t in range(NTP)]


def halves_perm(other, n_slot):
    pairs = []
    for role in range(2):
        for k in range(n_slot // 2):
            for h in range(2):
                dest = (h ^ other) * n_slot + role * (n_slot // 2) + k
                pairs.append((role * n_slot + 2 * k + h, dest))
    return pairs


def lane_row(values):
    lane = lax.broadcasted_iota(jnp.int32, (META, 128), 1)
    tile = jnp.zeros((META, 128), jnp.float32)
    for i, value in enumerate(values):
        tile = jnp.where(lane == i, value.astype(jnp.float32), tile)
    return tile.astype(jnp.bfloat16)


def column_counts(here, list_ref, col):
    base = here * NODE
    counts = [jnp.int32(0)] * NX
    for j in range(NODE):
        parent = list_ref[j]
        dist = (col - (parent // NODE) % NX + NX) % NX
        dist = jnp.where(parent == base + j, NX, dist)
        counts = [c + (dist == d).astype(jnp.int32) for d, c in enumerate(counts)]
    return counts


def pack_body(
    where_ref, mine_ref, other_ref, blocks_ref, keys_ref, values_ref,
    first_ref, second_ref, list_ref, sems,
):
    role = where_ref[0]
    here = where_ref[1]
    base = here * NODE
    count = jnp.int32(0)
    low = jnp.int32(0)
    high = jnp.int32(0)
    for j in range(NODE):
        h, k = divmod(j, NODE // 2)
        parent = jnp.where(role == h, mine_ref[k], other_ref[k])
        list_ref[j] = parent
        keep = parent == base + j
        low = jnp.where(keep & (count == 0), j, low)
        high = jnp.where(keep, j, high)
        count = count + keep.astype(jnp.int32)
    heads = keys_ref.shape[1]
    copies = []
    for b, out in enumerate((first_ref, second_ref)):
        for s, node in enumerate((low, high)):
            for kv, src in enumerate((keys_ref, values_ref)):
                for h in range(heads):
                    row = ((kv * 2 + s) * heads + h) * BLK
                    copies.append(
                        pltpu.make_async_copy(
                            src.at[node, h, pl.ds(b * BLK, BLK), :],
                            out.at[pl.ds(row, BLK), :],
                            sems.at[len(copies)],
                        )
                    )
    for c in copies:
        c.start()
    counts = column_counts(here, list_ref, here % NX)
    most = jnp.maximum(jnp.maximum(counts[0], counts[1]), jnp.maximum(counts[2], counts[3]))
    fit = (most <= FAST).astype(jnp.int32)
    rows = second_ref.shape[0]
    first_ref[rows : rows + META, :] = lane_row(
        (low, high, blocks_ref[low], blocks_ref[high], fit)
    )
    for c in copies:
        c.wait()


def pack(where, mine, other, blocks, keys, values):
    heads, _, dim = keys.shape[1:]
    rows = 4 * heads * BLK
    return pl.pallas_call(
        pack_body,
        out_shape=(
            pltpu.VMEM((rows + META, dim), keys.dtype),
            pltpu.VMEM((rows, dim), keys.dtype),
            jax.ShapeDtypeStruct((NODE,), jnp.int32),
        ),
        in_specs=[SMEM, SMEM, SMEM, SMEM, ANY, ANY],
        out_specs=(VMEM, VMEM, SMEM),
        scratch_shapes=[pltpu.SemaphoreType.DMA((8 * heads,))],
        compiler_params=params(2),
        name="pack",
    )(where, mine, other, blocks, keys, values)


def ring_step(pair):
    up, down = pair
    return lax.ppermute(up, "slot", zperm(1)), lax.ppermute(down, "slot", zperm(-1))


def ring_last(pair, up):
    if up:
        return lax.ppermute(pair[0], "slot", zperm(1))
    return lax.ppermute(pair[1], "slot", zperm(-1))


def ring_list(own, one, two, three, last):
    return [own, one[0], two[0], three[0], last, three[1], two[1], one[1]]


def issue_units(pick_ref, srcs, outs, size, sems):
    for d in range(NX):

        def unit(i, carry, d=d):
            u = d * FAST + i
            rel = pick_ref[u]
            rank = pick_ref[NX * FAST + u]
            for r in range(NZ):

                @pl.when(rel == r)
                def _(r=r):
                    for kv in range(2):
                        at = pl.multiple_of((kv * 2 + rank) * size, META)
                        to = pl.multiple_of((kv * 2 + i) * size, META)
                        pltpu.make_async_copy(
                            srcs[r].at[pl.ds(at, size), :],
                            outs[d].at[pl.ds(to, size), :],
                            sems.at[u * 2 + kv],
                        ).start()

            return carry

        lax.fori_loop(0, FAST, unit, 0)


def wait_units(srcs, outs, size, sems):
    def unit(n, carry):
        pltpu.make_async_copy(
            srcs[0].at[pl.ds(0, size), :], outs[0].at[pl.ds(0, size), :], sems.at[n]
        ).wait()
        return carry

    lax.fori_loop(0, NX * FAST * 2, unit, 0)


def select_first_body(where_ref, *refs):
    lists = refs[:NX]
    srcs = refs[NX : NX + NZ]
    outs = refs[NX + NZ : 2 * NX + NZ]
    pick_ref, meta_ref, wide_ref, ids_ref, sems, msem, ssem = refs[2 * NX + NZ :]
    size = outs[0].shape[0] // 4 // META * META
    here = where_ref[1]
    row = here // NX
    col = here % NX
    reads = []
    for rel in range(NZ):
        tile = srcs[rel].at[pl.ds(4 * size, META), :]
        reads.append(pltpu.make_async_copy(tile, meta_ref.at[rel], msem.at[rel]))
    for c in reads:
        c.start()
    for c in reads:
        c.wait()
    wide_ref[...] = meta_ref[...].astype(jnp.float32).astype(jnp.int32)
    spill = pltpu.make_async_copy(wide_ref, ids_ref, ssem)
    spill.start()
    spill.wait()
    for u in range(2 * NX * FAST):
        pick_ref[u] = 0
    for d in range(NX):
        base = (row * NX + (col + d) % NX) * NODE

        def scan(j, count, d=d, base=base):
            parent = lists[d][j]
            source = parent // NODE
            hit = (parent != base + j) & (source % NX == col)
            rel = (row - source // NX + NZ) % NZ

            @pl.when(hit & (count < FAST))
            def _():
                pick_ref[d * FAST + count] = rel
                pick_ref[NX * FAST + d * FAST + count] = (
                    parent % NODE == ids_ref[rel, 0, 1]
                ).astype(jnp.int32)

            return count + hit.astype(jnp.int32)

        lax.fori_loop(0, NODE, scan, jnp.int32(0))

    issue_units(pick_ref, srcs, outs, size, sems)
    fit = ids_ref[0, 0, 4]
    for rel in range(1, NZ):
        fit = jnp.minimum(fit, ids_ref[rel, 0, 4])
    for d in range(NX):
        sizes = []
        for i in range(FAST):
            u = d * FAST + i
            sizes.append(ids_ref[pick_ref[u], 0, 2 + pick_ref[NX * FAST + u]])
        outs[d][4 * size : 4 * size + META, :] = lane_row((sizes[0], sizes[1], fit))
    wait_units(srcs, outs, size, sems)


def select_first(where, lists, srcs):
    own = srcs[0]
    out = pltpu.VMEM(own.shape, own.dtype)
    return pl.pallas_call(
        select_first_body,
        out_shape=(out,) * NX + (jax.ShapeDtypeStruct((2 * NX * FAST,), jnp.int32),),
        in_specs=[SMEM] * (1 + NX) + [ANY] * NZ,
        out_specs=(VMEM,) * NX + (SMEM,),
        scratch_shapes=[
            pltpu.VMEM((NZ, META, 128), own.dtype),
            pltpu.VMEM((NZ, META, 128), jnp.int32),
            pltpu.SMEM((NZ, META, 128), jnp.int32),
            pltpu.SemaphoreType.DMA((NX * FAST * 2,)),
            pltpu.SemaphoreType.DMA((NZ,)),
            pltpu.SemaphoreType.DMA,
        ],
        compiler_params=params(2),
        name="select_first",
    )(where, *lists, *srcs)


def select_second_body(pick_ref, *refs):
    srcs = refs[:NZ]
    outs = refs[NZ : NZ + NX]
    sems = refs[NZ + NX]
    size = outs[0].shape[0] // 4

    issue_units(pick_ref, srcs, outs, size, sems)
    wait_units(srcs, outs, size, sems)


def select_second(picks, srcs):
    own = srcs[0]
    out = pltpu.VMEM(own.shape, own.dtype)
    return pl.pallas_call(
        select_second_body,
        out_shape=(out,) * NX,
        in_specs=[SMEM] + [ANY] * NZ,
        out_specs=(VMEM,) * NX,
        scratch_shapes=[pltpu.SemaphoreType.DMA((NX * FAST * 2,))],
        compiler_params=params(2),
        name="select_second",
    )(picks, *srcs)


def attend_node(n, tokens, scale, tp, q_ref, nk_ref, nv_ref, kbuf, vbuf, att_ref):
    heads, _, dim = kbuf.shape[1:]
    group = q_ref.shape[1] // (heads * dim)
    per = NODE // NTP
    at = pl.multiple_of(n * STEP, STEP)
    to = ((n // per - tp + NTP) % NTP) * per + n % per
    to = pl.multiple_of(to * STEP, STEP)
    rows = STEP * group
    f32 = jnp.float32
    nt = (((1,), (1,)), ((), ()))
    nn = (((1,), (0,)), ((), ()))
    step_of = lax.broadcasted_iota(jnp.int32, (rows, BLK), 0) % STEP
    step_ok = lax.broadcasted_iota(jnp.int32, (rows, BLK), 1) <= step_of
    pad = jnp.zeros((BLK - STEP, dim), kbuf.dtype)
    rate = scale * math.log2(math.e)
    logits = []
    for h in range(heads):
        base = h * group * dim
        q = jnp.concatenate(
            [q_ref[pl.ds(at, STEP), base + g * dim : base + (g + 1) * dim] for g in range(group)],
            axis=0,
        )
        nk = nk_ref[pl.ds(at, STEP), h * dim : (h + 1) * dim]
        k = jnp.concatenate([kbuf[n, h, :tokens], nk, pad], axis=0)
        logits.append(lax.dot_general(q, k, nt, preferred_element_type=f32))
    weights = []
    totals = []
    for h in range(heads):
        tiles = [logits[h][:, i : i + BLK] for i in range(0, tokens, BLK)]
        tiles.append(jnp.where(step_ok, logits[h][:, tokens:], -jnp.inf))
        top = tiles[0]
        for tile in tiles[1:]:
            top = jnp.maximum(top, tile)
        top = jnp.max(top, axis=1, keepdims=True)
        tiles = [jnp.exp2((tile - top) * rate) for tile in tiles]
        total = tiles[0]
        for tile in tiles[1:]:
            total = total + tile
        totals.append(jnp.sum(total, axis=1, keepdims=True))
        weights.append(jnp.concatenate([tile.astype(kbuf.dtype) for tile in tiles], axis=1))
    for h in range(heads):
        base = h * group * dim
        nv = nv_ref[pl.ds(at, STEP), h * dim : (h + 1) * dim]
        v = jnp.concatenate([vbuf[n, h, :tokens], nv, pad], axis=0)
        o = lax.dot_general(weights[h], v, nn, preferred_element_type=f32)
        o = (o * (1.0 / totals[h])).astype(att_ref.dtype)
        for g in range(group):
            att_ref[pl.ds(to, STEP), base + g * dim : base + (g + 1) * dim] = o[
                g * STEP : (g + 1) * STEP
            ]


def moved_copy(src, kv, rank, h, heads, j, b, buf, sem):
    at = pl.multiple_of(((kv * 2 + rank) * heads + h) * BLK, BLK)
    return pltpu.make_async_copy(
        src.at[pl.ds(at, BLK), :], buf.at[j, h, pl.ds(b * BLK, BLK), :], sem
    )


def early_body(scale, where_ref, list_ref, blocks_ref, q_ref, nk_ref, nv_ref, *refs):
    caches = refs[0:2]
    moved = refs[2 : 2 + NX]
    w_ref, att_ref, w0_ref, table_ref = refs[2 + NX : 6 + NX]
    kbuf, vbuf, meta_ref, wide_ref, ids_ref, sems, wsem, msem, ssem = refs[6 + NX :]
    bufs = (kbuf, vbuf)
    heads = kbuf.shape[1]
    here = where_ref[1]
    tp = where_ref[2]
    col = here % NX
    half = w0_ref.shape[1]
    reads = []
    for d in range(NX):
        at = moved[d].shape[0] - META
        reads.append(
            pltpu.make_async_copy(moved[d].at[pl.ds(at, META), :], meta_ref.at[d], msem.at[d])
        )
    for c in reads:
        c.start()

    def place(j, counts):
        parent = list_ref[j]
        moving = parent != here * NODE + j
        dist = jnp.where(moving, (col - (parent // NODE) % NX + NX) % NX, NX)
        rank = jnp.int32(0)
        after = []
        for d in range(NX):
            hit = dist == d
            rank = jnp.where(hit, counts[d], rank)
            after.append(counts[d] + hit.astype(jnp.int32))
        rank = jnp.minimum(rank, FAST - 1)
        table_ref[T_FROM + j] = dist
        table_ref[T_RANK + j] = rank

        @pl.when(dist == NX)
        def _():
            for kv in range(2):
                pltpu.make_async_copy(caches[kv].at[j], bufs[kv].at[j], sems.at[j, kv]).start()

        for d in range(NX):

            @pl.when(dist == d)
            def _(d=d):
                for kv in range(2):
                    for h in range(heads):
                        moved_copy(
                            moved[d], kv, rank, h, heads, j, 0, bufs[kv], sems.at[j, kv * heads + h]
                        ).start()

        return tuple(after)

    lax.fori_loop(0, NODE, place, (jnp.int32(0),) * NX)
    load = pltpu.make_async_copy(w_ref.at[:, pl.ds(0, half)], w0_ref, wsem)
    load.start()
    for c in reads:
        c.wait()
    wide_ref[...] = meta_ref[...].astype(jnp.float32).astype(jnp.int32)
    spill = pltpu.make_async_copy(wide_ref, ids_ref, ssem)
    spill.start()
    spill.wait()
    fit = ids_ref[0, 0, FAST]
    for d in range(1, NX):
        fit = jnp.minimum(fit, ids_ref[d, 0, FAST])
    for i in range(T_FIT, T_SIZE):
        table_ref[i] = fit

    def measure(j, carry):
        dist = table_ref[T_FROM + j]
        from_peer = ids_ref[jnp.minimum(dist, NX - 1), 0, table_ref[T_RANK + j]]
        table_ref[T_LEN + j] = jnp.where(dist == NX, blocks_ref[j], from_peer)
        return carry

    lax.fori_loop(0, NODE, measure, 0)

    def node(n, carry):
        local = table_ref[T_FROM + n] == NX
        blocks = table_ref[T_LEN + n]
        run = functools.partial(
            attend_node, n, scale=scale, tp=tp, q_ref=q_ref, nk_ref=nk_ref, nv_ref=nv_ref,
            kbuf=kbuf, vbuf=vbuf, att_ref=att_ref,
        )

        @pl.when(local)
        def _():
            for kv in range(2):
                pltpu.make_async_copy(caches[kv].at[n], bufs[kv].at[n], sems.at[n, kv]).wait()

        @pl.when(jnp.logical_not(local))
        def _():
            for kv in range(2):
                for h in range(heads):
                    moved_copy(
                        moved[0], kv, 0, h, heads, n, 0, bufs[kv], sems.at[n, kv * heads + h]
                    ).wait()

        @pl.when(local & (blocks == 2))
        def _():
            run(tokens=2 * BLK)

        @pl.when(blocks == 1)
        def _():
            run(tokens=BLK)

        return carry

    lax.fori_loop(0, NODE, node, 0)
    load.wait()


def early(where, own_list, blocks, queries, new_keys, new_values, keys, values, moved, weight):
    dim = keys.shape[3]
    inner, cols = weight.shape
    half = pltpu.VMEM((inner, cols // 2), weight.dtype)
    return pl.pallas_call(
        functools.partial(early_body, float(dim) ** -0.5),
        out_shape=(
            pltpu.VMEM(queries.shape, queries.dtype),
            half,
            jax.ShapeDtypeStruct((T_SIZE,), jnp.int32),
        ),
        in_specs=[SMEM, SMEM, SMEM, VMEM, VMEM, VMEM] + [ANY] * (3 + NX),
        out_specs=(VMEM, VMEM, SMEM),
        scratch_shapes=[
            pltpu.VMEM(keys.shape, keys.dtype),
            pltpu.VMEM(keys.shape, keys.dtype),
            pltpu.VMEM((NX, META, 128), keys.dtype),
            pltpu.VMEM((NX, META, 128), jnp.int32),
            pltpu.SMEM((NX, META, 128), jnp.int32),
            pltpu.SemaphoreType.DMA((NODE, 2 * keys.shape[1])),
            pltpu.SemaphoreType.DMA,
            pltpu.SemaphoreType.DMA((NX,)),
            pltpu.SemaphoreType.DMA,
        ],
        compiler_params=params(8),
        name="early",
    )(where, own_list, blocks, queries, new_keys, new_values, keys, values, *moved, weight)


def project_half(chunk, tile, att_ref, w_ref, own_ref, relay_a, relay_b, da, db, ca, cb):
    part, half = relay_a.shape
    base = chunk * half

    def step(side, c, carry):
        at = pl.multiple_of(c * tile, tile)
        cols = pl.ds(pl.multiple_of(side * half + at, tile), tile)
        far = pl.ds(pl.multiple_of(base + at, tile), tile)
        res = jnp.dot(att_ref[...], w_ref[:, cols], preferred_element_type=jnp.float32)
        res = res.astype(own_ref.dtype)
        own_ref[:, cols] = res[:part]
        (ca, db)[side][:, far] = res[part : 2 * part]
        (relay_a, relay_b)[side][:, pl.ds(at, tile)] = res[2 * part : 3 * part]
        (da, cb)[side][:, far] = res[3 * part :]
        return carry

    for side in range(2):
        lax.fori_loop(0, half // tile, functools.partial(step, side), 0)


def late_body(scale, tile, where_ref, table_ref, q_ref, nk_ref, nv_ref, *refs):
    firsts = refs[:NX]
    seconds = refs[NX : 2 * NX]
    old_ref, w0_ref, w_ref, att_ref, w1_ref = refs[2 * NX : 2 * NX + 5]
    outs = refs[2 * NX + 5 : 2 * NX + 12]
    kbuf, vbuf, sems, wsem = refs[2 * NX + 12 :]
    del old_ref
    bufs = (kbuf, vbuf)
    heads = kbuf.shape[1]
    tp = where_ref[2]
    half = w1_ref.shape[1]

    def is_late(n):
        return (table_ref[T_FROM + n] < NX) & (table_ref[T_LEN + n] == 2)

    def copies(n, d, rank):
        for b, group in enumerate((firsts, seconds)):
            for kv in range(2):
                for h in range(heads):
                    yield moved_copy(
                        group[d], kv, rank, h, heads, n, b, bufs[kv],
                        sems.at[n, (b * 2 + kv) * heads + h],
                    )

    def start(n, carry):
        for d in range(NX):

            @pl.when(is_late(n) & (table_ref[T_FROM + n] == d))
            def _(d=d):
                for c in copies(n, d, table_ref[T_RANK + n]):
                    c.start()

        return carry

    lax.fori_loop(0, NODE, start, 0)
    load = pltpu.make_async_copy(w_ref.at[:, pl.ds(half, half)], w1_ref, wsem)
    load.start()

    def node(n, carry):
        @pl.when(is_late(n))
        def _():
            for c in copies(n, 0, 0):
                c.wait()
            attend_node(n, 2 * BLK, scale, tp, q_ref, nk_ref, nv_ref, kbuf, vbuf, att_ref)

        return carry

    lax.fori_loop(0, NODE, node, 0)
    project_half(0, tile, att_ref, w0_ref, *outs)
    load.wait()


def late(where, table, queries, new_keys, new_values, moved, att, weight0, weight, shape, tile):
    dtype = queries.dtype
    part = att.shape[0] // NTP
    inner, half = weight0.shape
    wide = pltpu.VMEM((part, half), dtype)
    slim = pltpu.VMEM((part, half // 2), dtype)
    return pl.pallas_call(
        functools.partial(late_body, float(shape[3]) ** -0.5, tile),
        out_shape=(pltpu.VMEM(att.shape, dtype), pltpu.VMEM((inner, half), dtype))
        + (wide, slim, slim, wide, wide, wide, wide),
        in_specs=[SMEM, SMEM, VMEM, VMEM, VMEM] + [ANY] * (2 * NX) + [VMEM, VMEM, ANY],
        out_specs=(VMEM,) * 9,
        scratch_shapes=[
            pltpu.VMEM(shape, dtype),
            pltpu.VMEM(shape, dtype),
            pltpu.SemaphoreType.DMA((NODE, 4 * shape[1])),
            pltpu.SemaphoreType.DMA,
        ],
        input_output_aliases={5 + 2 * NX: 0},
        compiler_params=params(8),
        name="late",
    )(where, table, queries, new_keys, new_values, *moved, att, weight0, weight)


def project_body(tile, att_ref, w_ref, da0, db0, ca0, cb0, own_ref, ra, rb, da, db, ca, cb):
    del da0, db0, ca0, cb0
    project_half(1, tile, att_ref, w_ref, own_ref, ra, rb, da, db, ca, cb)


def project(att, weight, shared, tile):
    part = att.shape[0] // NTP
    half = weight.shape[1]
    wide = pltpu.VMEM((part, half), att.dtype)
    slim = pltpu.VMEM((part, half // 2), att.dtype)
    return pl.pallas_call(
        functools.partial(project_body, tile),
        out_shape=(wide, slim, slim, wide, wide, wide, wide),
        in_specs=[VMEM] * 6,
        out_specs=(VMEM,) * 7,
        input_output_aliases={2 + i: 3 + i for i in range(4)},
        compiler_params=params(6),
        name="project",
    )(att, weight, *shared)


def combine_body(base_ref, low_ref, high_ref, out_ref):
    half = low_ref.shape[1]
    for i, ref in enumerate((low_ref, high_ref)):
        cols = slice(i * half, (i + 1) * half)
        total = base_ref[:, cols].astype(jnp.float32) + ref[...].astype(jnp.float32)
        out_ref[:, cols] = total.astype(out_ref.dtype)


def combine(base, low, high):
    return pl.pallas_call(
        combine_body,
        out_shape=pltpu.VMEM(base.shape, base.dtype),
        in_specs=[VMEM] * 3,
        out_specs=VMEM,
        compiler_params=params(2),
        name="combine",
    )(base, low, high)


def finish_body(own0, own1, da, db, fa, fb, out_ref):
    half = own0.shape[1] // 2
    for c, own in enumerate((own0, own1)):
        here = slice(c * half, (c + 1) * half)
        for side, (near, far) in enumerate(((da, fa), (db, fb))):
            cols = slice(side * half, (side + 1) * half)
            total = own[:, cols].astype(jnp.float32) + near[:, here].astype(jnp.float32)
            total = total + far[:, here].astype(jnp.float32)
            at = 2 * c * half + side * half
            out_ref[:, at : at + half] = total.astype(out_ref.dtype)


def finish(*args):
    part, half = args[0].shape
    return pl.pallas_call(
        finish_body,
        out_shape=jax.ShapeDtypeStruct((part, 2 * half), args[0].dtype),
        in_specs=[VMEM] * 6,
        out_specs=VMEM,
        compiler_params=params(4),
        name="finish",
    )(*args)


def general(
    where, mine, other, queries, keys, values, new_keys, new_values, weight, cache_blocks
):
    n_slot = lax.axis_size("slot")
    slot_here = lax.axis_index("slot")
    tp_here = lax.axis_index("tp")
    heads, tokens, dim = keys.shape[1:]
    rows, width = queries.shape
    group = width // (heads * dim)
    scale = float(dim) ** -0.5
    f32 = jnp.float32
    first, second, own = pack(where, mine, other, cache_blocks, keys, values)
    size = second.shape[0]
    each = heads * BLK

    def turn(t, carry):
        buf, got, blocks = carry
        from_slot = (slot_here - t + n_slot) % n_slot
        ids = buf[size].astype(jnp.int32)

        def take(j, state):
            got, blocks = state
            hit = (own[j] != slot_here * NODE + j) & (own[j] // NODE == from_slot)
            rank = (own[j] % NODE == ids[1]).astype(jnp.int32)

            def put(state):
                got, blocks = state
                for b in range(2):
                    for kv in range(2):
                        start = b * (size + META) + (kv * 2 + rank) * each
                        unit = lax.dynamic_slice_in_dim(buf, start, each)
                        got = lax.dynamic_update_slice(got, unit[None, None, None], (j, kv, b, 0, 0))
                return got, lax.dynamic_update_slice(blocks, ids[2 + rank][None], (j,))

            return lax.cond(hit, put, lambda state: state, (got, blocks))

        got, blocks = lax.fori_loop(0, NODE, take, (got, blocks))
        pairs = [(s, (s + 1) % n_slot) for s in range(n_slot)]
        return lax.ppermute(buf, "slot", pairs), got, blocks

    local = jnp.stack([keys, values], axis=1).reshape(NODE, 2, heads, 2, BLK, dim)
    local = local.transpose(0, 1, 3, 2, 4, 5).reshape(NODE, 2, 2, each, dim)
    carry = (jnp.concatenate([first, second]), local, cache_blocks)
    got, blocks = lax.fori_loop(0, n_slot, turn, carry)[1:]
    row_at = lax.broadcasted_iota(jnp.int32, (STEP * group, 1), 0) // group
    step_ok = lax.broadcasted_iota(jnp.int32, (1, STEP), 1) <= row_at
    token_at = lax.broadcasted_iota(jnp.int32, (1, tokens), 1)

    def unit(n, att):
        j, h = n // heads, n % heads

        def cut(a, wide):
            return lax.dynamic_slice(a, (j * STEP, h * wide), (STEP, wide))

        def cache(kv):
            return lax.dynamic_slice(got, (j, kv, 0, h * BLK, 0), (1, 1, 2, BLK, dim)).reshape(
                tokens, dim
            )

        q = cut(queries, group * dim).reshape(STEP * group, dim)
        k = jnp.concatenate([cache(0), cut(new_keys, dim)])
        v = jnp.concatenate([cache(1), cut(new_values, dim)])
        ok = jnp.concatenate(
            [jnp.broadcast_to(token_at < blocks[j] * BLK, (STEP * group, tokens)), step_ok], axis=1
        )
        logits = jnp.dot(q, k.T, preferred_element_type=f32) * scale
        logits = jnp.where(ok, logits, -jnp.inf)
        weights = jnp.exp(logits - jnp.max(logits, axis=1, keepdims=True))
        out = jnp.dot(weights.astype(v.dtype), v, preferred_element_type=f32)
        out = out / jnp.sum(weights, axis=1, keepdims=True)
        out = out.astype(att.dtype).reshape(STEP, group * dim)
        return lax.dynamic_update_slice(att, out, (j * STEP, h * group * dim))

    att = lax.fori_loop(0, NODE * heads, unit, jnp.zeros_like(queries))
    part = rows // NTP
    cols = weight.shape[1]
    tile = 512

    def piece(i):
        mine = lax.dynamic_slice_in_dim(att, (tp_here + i) % NTP * part, part)

        def column(c, total):
            w = lax.dynamic_slice_in_dim(weight, c * tile, tile, axis=1)
            res = jnp.dot(mine, w, preferred_element_type=f32)
            return lax.dynamic_update_slice(total, res, (0, c * tile))

        return lax.fori_loop(0, cols // tile, column, jnp.zeros((part, cols), f32))

    def pass_on(k, total):
        return lax.ppermute(total, "tp", yperm(1)) + piece(2 * NTP - 1 - k)

    total = lax.fori_loop(0, NTP, pass_on, jnp.zeros((part, cols), f32))
    return total.astype(att.dtype)


def shards(
    queries, cache_keys, cache_values, new_keys, new_values, out_weight, fork_src, cache_blocks
):
    queries, keys, values = queries[0], cache_keys[0], cache_values[0]
    new_keys, new_values, weight = new_keys[0], new_values[0], out_weight[0]
    n_slot = lax.axis_size("slot")
    where = jnp.stack([lax.axis_index(name).astype(jnp.int32) for name in ("role", "slot", "tp")])

    mine = lax.ppermute(fork_src, ("role", "slot"), halves_perm(0, n_slot))
    other = lax.ppermute(fork_src, ("role", "slot"), halves_perm(1, n_slot))
    first, second, own_list = pack(where, mine, other, cache_blocks, keys, values)
    first1 = ring_step((first, first))
    second1 = ring_step((second, second))
    lists = [own_list]
    for d in (1, 2, 3):
        lists.append(lax.ppermute(own_list, "slot", xperm(-d)))
    first2 = ring_step(first1)
    second2 = ring_step(second1)
    first3 = ring_step(first2)
    second3 = ring_step(second2)
    got_first = ring_list(first, first1, first2, first3, ring_last(first3, True))
    got_second = ring_list(second, second1, second2, second3, ring_last(second3, False))
    *outs_first, picks = select_first(where, lists, got_first)
    moved = [outs_first[0]]
    for d in (1, 2, 3):
        moved.append(lax.ppermute(outs_first[d], "slot", xperm(d)))
    outs_second = select_second(picks, got_second)
    att, weight0, table = early(
        where, own_list, cache_blocks, queries, new_keys, new_values, keys, values, moved,
        weight,
    )
    moved = moved + [outs_second[0]]
    for d in (1, 2, 3):
        moved.append(lax.ppermute(outs_second[d], "slot", xperm(d)))
    att, weight1, own0, relay_a0, relay_b0, *shared = late(
        where, table, queries, new_keys, new_values, moved, att, weight0, weight, keys.shape, 512
    )
    up, down = yperm(1), yperm(-1)
    relay_a0 = lax.ppermute(relay_a0, "tp", up)
    relay_b0 = lax.ppermute(relay_b0, "tp", down)
    own1, relay_a1, relay_b1, da, db, ca, cb = project(att, weight1, shared, 512)
    relay_a1 = lax.ppermute(relay_a1, "tp", up)
    relay_b1 = lax.ppermute(relay_b1, "tp", down)
    da = lax.ppermute(da, "tp", down)
    db = lax.ppermute(db, "tp", up)
    far_a = lax.ppermute(combine(ca, relay_a0, relay_a1), "tp", up)
    far_b = lax.ppermute(combine(cb, relay_b0, relay_b1), "tp", down)
    out = finish(own0, own1, da, db, far_a, far_b)
    args = (where, mine, other, queries, keys, values, new_keys, new_values, weight, cache_blocks)
    out = lax.cond(table[T_FIT] == 1, lambda o, *_: o, lambda o, *a: general(*a), out, *args)
    return out[None]


def solution(mesh):
    in_specs = (
        P("role", "slot", "tp"),
        P("role", "slot", "tp", None, None),
        P("role", "slot", "tp", None, None),
        P("role", "slot", "tp"),
        P("role", "slot", "tp"),
        P("role", "tp", None),
        P(("role", "slot")),
        P("slot"),
    )
    out_specs = P("role", ("slot", "tp"), None)

    return jax.shard_map(shards, mesh=mesh, in_specs=in_specs, out_specs=out_specs, check_vma=False)
```

```python
import functools
import math

import jax
import jax.numpy as jnp
from jax import lax
from jax.experimental import pallas as pl
from jax.experimental.pallas import tpu as pltpu
from jax.sharding import PartitionSpec as P


BLK = 128
NX = 4
NZ = 8
NTP = 4
NODE = 8
STEP = 32
FAST = 2
META = 16

T_FROM = 0
T_RANK = 8
T_LEN = 16
T_FIT = 24
T_SIZE = 32

SMEM = pl.BlockSpec(memory_space=pltpu.SMEM)
VMEM = pl.BlockSpec(memory_space=pltpu.VMEM)
ANY = pl.BlockSpec(memory_space=pl.ANY)


def params(mib):
    return pltpu.CompilerParams(vmem_limit_bytes=mib << 20)


def zperm(d):
    return [(s, (s + NX * d) % (NX * NZ)) for s in range(NX * NZ)]


def xperm(d):
    return [(s, (s // NX) * NX + (s % NX + d) % NX) for s in range(NX * NZ)]


def yperm(d):
    return [(t, (t + d) % NTP) for t in range(NTP)]


def halves_perm(other, n_slot):
    pairs = []
    for role in range(2):
        for k in range(n_slot // 2):
            for h in range(2):
                dest = (h ^ other) * n_slot + role * (n_slot // 2) + k
                pairs.append((role * n_slot + 2 * k + h, dest))
    return pairs


def lane_row(values):
    lane = lax.broadcasted_iota(jnp.int32, (META, 128), 1)
    tile = jnp.zeros((META, 128), jnp.float32)
    for i, value in enumerate(values):
        tile = jnp.where(lane == i, value.astype(jnp.float32), tile)
    return tile.astype(jnp.bfloat16)


def column_counts(here, list_ref, col):
    base = here * NODE
    counts = [jnp.int32(0)] * NX
    for j in range(NODE):
        parent = list_ref[j]
        dist = (col - (parent // NODE) % NX + NX) % NX
        dist = jnp.where(parent == base + j, NX, dist)
        counts = [c + (dist == d).astype(jnp.int32) for d, c in enumerate(counts)]
    return counts


def pack_body(
    where_ref, mine_ref, other_ref, blocks_ref, keys_ref, values_ref,
    first_ref, second_ref, list_ref, sems,
):
    role = where_ref[0]
    here = where_ref[1]
    base = here * NODE
    count = jnp.int32(0)
    low = jnp.int32(0)
    high = jnp.int32(0)
    for j in range(NODE):
        h, k = divmod(j, NODE // 2)
        parent = jnp.where(role == h, mine_ref[k], other_ref[k])
        list_ref[j] = parent
        keep = parent == base + j
        low = jnp.where(keep & (count == 0), j, low)
        high = jnp.where(keep, j, high)
        count = count + keep.astype(jnp.int32)
    heads = keys_ref.shape[1]
    copies = []
    for b, out in enumerate((first_ref, second_ref)):
        for s, node in enumerate((low, high)):
            for kv, src in enumerate((keys_ref, values_ref)):
                for h in range(heads):
                    row = ((kv * 2 + s) * heads + h) * BLK
                    copies.append(
                        pltpu.make_async_copy(
                            src.at[node, h, pl.ds(b * BLK, BLK), :],
                            out.at[pl.ds(row, BLK), :],
                            sems.at[len(copies)],
                        )
                    )
    for c in copies:
        c.start()
    counts = column_counts(here, list_ref, here % NX)
    most = jnp.maximum(jnp.maximum(counts[0], counts[1]), jnp.maximum(counts[2], counts[3]))
    fit = (most <= FAST).astype(jnp.int32)
    rows = second_ref.shape[0]
    first_ref[rows : rows + META, :] = lane_row(
        (low, high, blocks_ref[low], blocks_ref[high], fit)
    )
    for c in copies:
        c.wait()


def pack(where, mine, other, blocks, keys, values):
    heads, _, dim = keys.shape[1:]
    rows = 4 * heads * BLK
    return pl.pallas_call(
        pack_body,
        out_shape=(
            pltpu.VMEM((rows + META, dim), keys.dtype),
            pltpu.VMEM((rows, dim), keys.dtype),
            jax.ShapeDtypeStruct((NODE,), jnp.int32),
        ),
        in_specs=[SMEM, SMEM, SMEM, SMEM, ANY, ANY],
        out_specs=(VMEM, VMEM, SMEM),
        scratch_shapes=[pltpu.SemaphoreType.DMA((8 * heads,))],
        compiler_params=params(2),
        name="pack",
    )(where, mine, other, blocks, keys, values)


def ring_step(pair):
    up, down = pair
    return lax.ppermute(up, "slot", zperm(1)), lax.ppermute(down, "slot", zperm(-1))


def ring_last(pair, up):
    if up:
        return lax.ppermute(pair[0], "slot", zperm(1))
    return lax.ppermute(pair[1], "slot", zperm(-1))


def ring_list(own, one, two, three, last):
    return [own, one[0], two[0], three[0], last, three[1], two[1], one[1]]


def copy_units(pick_ref, srcs, outs, size):
    for d in range(NX):

        def unit(i, carry, d=d):
            u = d * FAST + i
            rel = pick_ref[u]
            rank = pick_ref[NX * FAST + u]
            for r in range(NZ):

                @pl.when(rel == r)
                def _(r=r):
                    for kv in range(2):
                        at = pl.multiple_of((kv * 2 + rank) * size, META)
                        to = pl.multiple_of((kv * 2 + i) * size, META)
                        outs[d][pl.ds(to, size), :] = srcs[r][pl.ds(at, size), :]

            return carry

        lax.fori_loop(0, FAST, unit, 0)


def spill(tiles, wide_ref, ids_ref, sem):
    for i, tile in enumerate(tiles):
        row = jnp.max(tile.astype(jnp.float32), axis=0, keepdims=True)
        wide_ref[i : i + 1, :] = row.astype(jnp.int32)
    copy = pltpu.make_async_copy(wide_ref, ids_ref, sem)
    copy.start()
    copy.wait()


def select_first_body(where_ref, *refs):
    lists = refs[:NX]
    srcs = refs[NX : NX + NZ]
    outs = refs[NX + NZ : 2 * NX + NZ]
    pick_ref, wide_ref, ids_ref, sem = refs[2 * NX + NZ :]
    size = outs[0].shape[0] // 4 // META * META
    here = where_ref[1]
    row = here // NX
    col = here % NX
    tiles = [src[4 * size : 4 * size + META, :] for src in srcs]
    spill(tiles, wide_ref, ids_ref, sem)
    for u in range(2 * NX * FAST):
        pick_ref[u] = 0
    for d in range(NX):
        base = (row * NX + (col + d) % NX) * NODE

        def scan(j, count, d=d, base=base):
            parent = lists[d][j]
            source = parent // NODE
            hit = (parent != base + j) & (source % NX == col)
            rel = (row - source // NX + NZ) % NZ

            @pl.when(hit & (count < FAST))
            def _():
                pick_ref[d * FAST + count] = rel
                pick_ref[NX * FAST + d * FAST + count] = (
                    parent % NODE == ids_ref[rel, 1]
                ).astype(jnp.int32)

            return count + hit.astype(jnp.int32)

        lax.fori_loop(0, NODE, scan, jnp.int32(0))

    copy_units(pick_ref, srcs, outs, size)
    fit = ids_ref[0, 4]
    for rel in range(1, NZ):
        fit = jnp.minimum(fit, ids_ref[rel, 4])
    for d in range(NX):
        sizes = []
        for i in range(FAST):
            u = d * FAST + i
            sizes.append(ids_ref[pick_ref[u], 2 + pick_ref[NX * FAST + u]])
        outs[d][4 * size : 4 * size + META, :] = lane_row((sizes[0], sizes[1], fit))


def select_first(where, lists, srcs):
    own = srcs[0]
    out = pltpu.VMEM(own.shape, own.dtype)
    return pl.pallas_call(
        select_first_body,
        out_shape=(out,) * NX + (jax.ShapeDtypeStruct((2 * NX * FAST,), jnp.int32),),
        in_specs=[SMEM] * (1 + NX) + [VMEM] * NZ,
        out_specs=(VMEM,) * NX + (SMEM,),
        scratch_shapes=[
            pltpu.VMEM((NZ, 128), jnp.int32),
            pltpu.SMEM((NZ, 128), jnp.int32),
            pltpu.SemaphoreType.DMA,
        ],
        compiler_params=params(2),
        name="select_first",
    )(where, *lists, *srcs)


def select_second_body(pick_ref, *refs):
    copy_units(pick_ref, refs[:NZ], refs[NZ:], refs[NZ].shape[0] // 4)


def select_second(picks, srcs):
    own = srcs[0]
    out = pltpu.VMEM(own.shape, own.dtype)
    return pl.pallas_call(
        select_second_body,
        out_shape=(out,) * NX,
        in_specs=[SMEM] + [VMEM] * NZ,
        out_specs=(VMEM,) * NX,
        compiler_params=params(2),
        name="select_second",
    )(picks, *srcs)


def attend_node(n, tokens, scale, tp, q_ref, nk_ref, nv_ref, kbuf, vbuf, att_ref):
    heads, _, dim = kbuf.shape[1:]
    group = q_ref.shape[1] // (heads * dim)
    per = NODE // NTP
    at = pl.multiple_of(n * STEP, STEP)
    to = ((n // per - tp + NTP) % NTP) * per + n % per
    to = pl.multiple_of(to * STEP, STEP)
    rows = STEP * group
    f32 = jnp.float32
    nt = (((1,), (1,)), ((), ()))
    nn = (((1,), (0,)), ((), ()))
    step_of = lax.broadcasted_iota(jnp.int32, (rows, BLK), 0) % STEP
    step_ok = lax.broadcasted_iota(jnp.int32, (rows, BLK), 1) <= step_of
    pad = jnp.zeros((BLK - STEP, dim), kbuf.dtype)
    rate = scale * math.log2(math.e)
    logits = []
    for h in range(heads):
        base = h * group * dim
        q = jnp.concatenate(
            [q_ref[pl.ds(at, STEP), base + g * dim : base + (g + 1) * dim] for g in range(group)],
            axis=0,
        )
        nk = nk_ref[pl.ds(at, STEP), h * dim : (h + 1) * dim]
        k = jnp.concatenate([kbuf[n, h, :tokens], nk, pad], axis=0)
        logits.append(lax.dot_general(q, k, nt, preferred_element_type=f32))
    weights = []
    totals = []
    for h in range(heads):
        tiles = [logits[h][:, i : i + BLK] for i in range(0, tokens, BLK)]
        tiles.append(jnp.where(step_ok, logits[h][:, tokens:], -jnp.inf))
        top = tiles[0]
        for tile in tiles[1:]:
            top = jnp.maximum(top, tile)
        top = jnp.max(top, axis=1, keepdims=True)
        tiles = [jnp.exp2((tile - top) * rate) for tile in tiles]
        total = tiles[0]
        for tile in tiles[1:]:
            total = total + tile
        totals.append(jnp.sum(total, axis=1, keepdims=True))
        weights.append(jnp.concatenate([tile.astype(kbuf.dtype) for tile in tiles], axis=1))
    for h in range(heads):
        base = h * group * dim
        nv = nv_ref[pl.ds(at, STEP), h * dim : (h + 1) * dim]
        v = jnp.concatenate([vbuf[n, h, :tokens], nv, pad], axis=0)
        o = lax.dot_general(weights[h], v, nn, preferred_element_type=f32)
        o = (o * (1.0 / totals[h])).astype(att_ref.dtype)
        for g in range(group):
            att_ref[pl.ds(to, STEP), base + g * dim : base + (g + 1) * dim] = o[
                g * STEP : (g + 1) * STEP
            ]


def cache_copies(src, j, bufs, sems):
    heads = bufs[0].shape[1]
    return [
        pltpu.make_async_copy(src[kv].at[j, h], bufs[kv].at[j, h], sems.at[j, kv * heads + h])
        for kv in range(2)
        for h in range(heads)
    ]


def moved_copies(blocks, rank, j, bufs, sems):
    heads = bufs[0].shape[1]
    copies = []
    for b, src in enumerate(blocks):
        for kv in range(2):
            for h in range(heads):
                at = pl.multiple_of(((kv * 2 + rank) * heads + h) * BLK, BLK)
                copies.append(
                    pltpu.make_async_copy(
                        src.at[pl.ds(at, BLK), :],
                        bufs[kv].at[j, h, pl.ds(b * BLK, BLK), :],
                        sems.at[j, len(copies)],
                    )
                )
    return copies


def each_node(body):
    def step(n, carry):
        body(n)
        return carry

    lax.fori_loop(0, NODE, step, 0)


def local_body(scale, where_ref, list_ref, blocks_ref, q_ref, nk_ref, nv_ref, *refs):
    caches = refs[0:2]
    moved = refs[2:4]
    w_ref, att_ref, w0_ref, table_ref, kbuf, vbuf, wide_ref, ids_ref, sems, sem, wsem = refs[4:]
    bufs = (kbuf, vbuf)
    here = where_ref[1]
    tp = where_ref[2]
    col = here % NX

    def place(j, counts):
        parent = list_ref[j]
        moving = parent != here * NODE + j
        dist = jnp.where(moving, (col - (parent // NODE) % NX + NX) % NX, NX)
        rank = jnp.int32(0)
        after = []
        for d in range(NX):
            hit = dist == d
            rank = jnp.where(hit, counts[d], rank)
            after.append(counts[d] + hit.astype(jnp.int32))
        rank = jnp.minimum(rank, FAST - 1)
        table_ref[T_FROM + j] = dist
        table_ref[T_RANK + j] = rank

        @pl.when(dist == NX)
        def _():
            for c in cache_copies(caches, j, bufs, sems):
                c.start()

        @pl.when(dist == 0)
        def _():
            for c in moved_copies(moved, rank, j, bufs, sems):
                c.start()

        return tuple(after)

    lax.fori_loop(0, NODE, place, (jnp.int32(0),) * NX)
    load = pltpu.make_async_copy(w_ref.at[:, pl.ds(0, w0_ref.shape[1])], w0_ref, wsem)
    load.start()
    rows = moved[0].shape[0]
    spill([moved[0][rows - META :, :]], wide_ref, ids_ref, sem)
    for i in range(T_FIT, T_SIZE):
        table_ref[i] = ids_ref[0, FAST]

    def node(n):
        dist = table_ref[T_FROM + n]
        blocks = jnp.where(dist == NX, blocks_ref[n], ids_ref[0, table_ref[T_RANK + n]])
        table_ref[T_LEN + n] = blocks
        mine = (dist == NX) | (dist == 0)
        run = functools.partial(
            attend_node, n, scale=scale, tp=tp, q_ref=q_ref, nk_ref=nk_ref, nv_ref=nv_ref,
            kbuf=kbuf, vbuf=vbuf, att_ref=att_ref,
        )

        @pl.when(dist == NX)
        def _():
            for c in cache_copies(caches, n, bufs, sems):
                c.wait()

        @pl.when(dist == 0)
        def _():
            for c in moved_copies(moved, 0, n, bufs, sems):
                c.wait()

        @pl.when(mine & (blocks == 2))
        def _():
            run(tokens=2 * BLK)

        @pl.when(mine & (blocks == 1))
        def _():
            run(tokens=BLK)

    each_node(node)
    load.wait()


def half_weight(weight):
    return pltpu.VMEM((weight.shape[0], weight.shape[1] // 2), weight.dtype)


def node_scratch(keys, per_node):
    return [
        pltpu.VMEM(keys.shape, keys.dtype),
        pltpu.VMEM(keys.shape, keys.dtype),
        pltpu.VMEM((NX, 128), jnp.int32),
        pltpu.SMEM((NX, 128), jnp.int32),
        pltpu.SemaphoreType.DMA((NODE, per_node)),
        pltpu.SemaphoreType.DMA,
        pltpu.SemaphoreType.DMA,
    ]


def local(where, own_list, blocks, queries, new_keys, new_values, keys, values, moved, weight):
    return pl.pallas_call(
        functools.partial(local_body, float(keys.shape[3]) ** -0.5),
        out_shape=(
            pltpu.VMEM(queries.shape, queries.dtype),
            half_weight(weight),
            jax.ShapeDtypeStruct((T_SIZE,), jnp.int32),
        ),
        in_specs=[SMEM, SMEM, SMEM, VMEM, VMEM, VMEM, ANY, ANY, VMEM, VMEM, ANY],
        out_specs=(VMEM, VMEM, SMEM),
        scratch_shapes=node_scratch(keys, 4 * keys.shape[1]),
        compiler_params=params(8),
        name="local",
    )(where, own_list, blocks, queries, new_keys, new_values, keys, values, *moved, weight)


def early_body(scale, where_ref, old_table, q_ref, nk_ref, nv_ref, *refs):
    moved = refs[: NX - 1]
    refs = refs[NX - 1 :]
    w_ref, old_ref, att_ref, w1_ref, table_ref, kbuf, vbuf, wide_ref, ids_ref, sems, sem, wsem = refs
    del old_ref
    bufs = (kbuf, vbuf)

    def start(n):
        for d in range(1, NX):

            @pl.when(old_table[T_FROM + n] == d)
            def _(d=d):
                for c in moved_copies(moved[d - 1 : d], old_table[T_RANK + n], n, bufs, sems):
                    c.start()

    each_node(start)
    half = w1_ref.shape[1]
    load = pltpu.make_async_copy(w_ref.at[:, pl.ds(half, half)], w1_ref, wsem)
    load.start()
    spill([m[m.shape[0] - META :, :] for m in moved], wide_ref, ids_ref, sem)
    for i in range(T_LEN):
        table_ref[i] = old_table[i]
    fit = old_table[T_FIT]
    for d in range(1, NX):
        fit = jnp.minimum(fit, ids_ref[d - 1, FAST])
    for i in range(T_FIT, T_SIZE):
        table_ref[i] = fit

    def node(n):
        dist = old_table[T_FROM + n]
        far = (dist > 0) & (dist < NX)
        at = jnp.clip(dist - 1, 0, NX - 2)
        blocks = jnp.where(far, ids_ref[at, old_table[T_RANK + n]], old_table[T_LEN + n])
        table_ref[T_LEN + n] = blocks

        @pl.when(far)
        def _():
            for c in moved_copies(moved[:1], 0, n, bufs, sems):
                c.wait()

        @pl.when(far & (blocks == 1))
        def _():
            attend_node(
                n, BLK, scale, where_ref[2], q_ref, nk_ref, nv_ref, kbuf, vbuf, att_ref
            )

    each_node(node)
    load.wait()


def early(where, table, queries, new_keys, new_values, moved, weight, att, keys):
    return pl.pallas_call(
        functools.partial(early_body, float(keys.shape[3]) ** -0.5),
        out_shape=(
            pltpu.VMEM(queries.shape, queries.dtype),
            half_weight(weight),
            jax.ShapeDtypeStruct((T_SIZE,), jnp.int32),
        ),
        in_specs=[SMEM, SMEM, VMEM, VMEM, VMEM] + [VMEM] * (NX - 1) + [ANY, VMEM],
        out_specs=(VMEM, VMEM, SMEM),
        scratch_shapes=node_scratch(keys, 2 * keys.shape[1]),
        input_output_aliases={5 + NX: 0},
        compiler_params=params(8),
        name="early",
    )(where, table, queries, new_keys, new_values, *moved, weight, att)


def project_half(chunk, tile, att_ref, w_ref, own_ref, relay_a, relay_b, da, db, ca, cb):
    part, half = relay_a.shape
    base = chunk * half

    def step(side, c, carry):
        at = pl.multiple_of(c * tile, tile)
        cols = pl.ds(pl.multiple_of(side * half + at, tile), tile)
        far = pl.ds(pl.multiple_of(base + at, tile), tile)
        res = jnp.dot(att_ref[...], w_ref[:, cols], preferred_element_type=jnp.float32)
        res = res.astype(own_ref.dtype)
        own_ref[:, cols] = res[:part]
        (ca, db)[side][:, far] = res[part : 2 * part]
        (relay_a, relay_b)[side][:, pl.ds(at, tile)] = res[2 * part : 3 * part]
        (da, cb)[side][:, far] = res[3 * part :]
        return carry

    for side in range(2):
        lax.fori_loop(0, half // tile, functools.partial(step, side), 0)


def late_body(scale, tile, where_ref, table_ref, q_ref, nk_ref, nv_ref, *refs):
    far = NX - 1
    firsts = refs[:far]
    seconds = refs[far : 2 * far]
    old_ref, w_ref, att_ref = refs[2 * far : 2 * far + 3]
    outs = refs[2 * far + 3 : 2 * far + 10]
    kbuf, vbuf, sems = refs[2 * far + 10 :]
    del old_ref
    bufs = (kbuf, vbuf)

    def is_late(n):
        dist = table_ref[T_FROM + n]
        return (dist > 0) & (dist < NX) & (table_ref[T_LEN + n] == 2)

    def start(n):
        for d in range(1, NX):

            @pl.when(is_late(n) & (table_ref[T_FROM + n] == d))
            def _(d=d):
                pair = (firsts[d - 1], seconds[d - 1])
                for c in moved_copies(pair, table_ref[T_RANK + n], n, bufs, sems):
                    c.start()

    each_node(start)

    def node(n):
        @pl.when(is_late(n))
        def _():
            for c in moved_copies((firsts[0], seconds[0]), 0, n, bufs, sems):
                c.wait()
            attend_node(
                n, 2 * BLK, scale, where_ref[2], q_ref, nk_ref, nv_ref, kbuf, vbuf, att_ref
            )

    each_node(node)
    project_half(0, tile, att_ref, w_ref, *outs)


def late(where, table, queries, new_keys, new_values, firsts, seconds, att, weight0, shape, tile):
    dtype = queries.dtype
    part = att.shape[0] // NTP
    half = weight0.shape[1]
    wide = pltpu.VMEM((part, half), dtype)
    slim = pltpu.VMEM((part, half // 2), dtype)
    far = NX - 1
    return pl.pallas_call(
        functools.partial(late_body, float(shape[3]) ** -0.5, tile),
        out_shape=(pltpu.VMEM(att.shape, dtype), wide, slim, slim, wide, wide, wide, wide),
        in_specs=[SMEM, SMEM, VMEM, VMEM, VMEM] + [ANY] * (2 * far) + [VMEM, VMEM],
        out_specs=(VMEM,) * 8,
        scratch_shapes=[
            pltpu.VMEM(shape, dtype),
            pltpu.VMEM(shape, dtype),
            pltpu.SemaphoreType.DMA((NODE, 4 * shape[1])),
        ],
        input_output_aliases={5 + 2 * far: 0},
        compiler_params=params(8),
        name="late",
    )(where, table, queries, new_keys, new_values, *firsts, *seconds, att, weight0)


def project_body(tile, att_ref, w_ref, da0, db0, ca0, cb0, own_ref, ra, rb, da, db, ca, cb):
    del da0, db0, ca0, cb0
    project_half(1, tile, att_ref, w_ref, own_ref, ra, rb, da, db, ca, cb)


def project(att, weight, shared, tile):
    part = att.shape[0] // NTP
    half = weight.shape[1]
    wide = pltpu.VMEM((part, half), att.dtype)
    slim = pltpu.VMEM((part, half // 2), att.dtype)
    return pl.pallas_call(
        functools.partial(project_body, tile),
        out_shape=(wide, slim, slim, wide, wide, wide, wide),
        in_specs=[VMEM] * 6,
        out_specs=(VMEM,) * 7,
        input_output_aliases={2 + i: 3 + i for i in range(4)},
        compiler_params=params(6),
        name="project",
    )(att, weight, *shared)


def combine_body(base_ref, low_ref, high_ref, out_ref):
    half = low_ref.shape[1]
    for i, ref in enumerate((low_ref, high_ref)):
        cols = slice(i * half, (i + 1) * half)
        total = base_ref[:, cols].astype(jnp.float32) + ref[...].astype(jnp.float32)
        out_ref[:, cols] = total.astype(out_ref.dtype)


def combine(base, low, high):
    return pl.pallas_call(
        combine_body,
        out_shape=pltpu.VMEM(base.shape, base.dtype),
        in_specs=[VMEM] * 3,
        out_specs=VMEM,
        compiler_params=params(2),
        name="combine",
    )(base, low, high)


def finish_body(own0, own1, da, db, fa, fb, out_ref):
    half = own0.shape[1] // 2
    for c, own in enumerate((own0, own1)):
        here = slice(c * half, (c + 1) * half)
        for side, (near, far) in enumerate(((da, fa), (db, fb))):
            cols = slice(side * half, (side + 1) * half)
            total = own[:, cols].astype(jnp.float32) + near[:, here].astype(jnp.float32)
            total = total + far[:, here].astype(jnp.float32)
            at = 2 * c * half + side * half
            out_ref[:, at : at + half] = total.astype(out_ref.dtype)


def finish(*args):
    part, half = args[0].shape
    return pl.pallas_call(
        finish_body,
        out_shape=jax.ShapeDtypeStruct((part, 2 * half), args[0].dtype),
        in_specs=[VMEM] * 6,
        out_specs=VMEM,
        compiler_params=params(4),
        name="finish",
    )(*args)


def general(
    where, mine, other, queries, keys, values, new_keys, new_values, weight, cache_blocks
):
    n_slot = lax.axis_size("slot")
    slot_here = lax.axis_index("slot")
    tp_here = lax.axis_index("tp")
    heads, tokens, dim = keys.shape[1:]
    rows, width = queries.shape
    group = width // (heads * dim)
    scale = float(dim) ** -0.5
    f32 = jnp.float32
    first, second, own = pack(where, mine, other, cache_blocks, keys, values)
    size = second.shape[0]
    each = heads * BLK

    def turn(t, carry):
        buf, got, blocks = carry
        from_slot = (slot_here - t + n_slot) % n_slot
        ids = buf[size].astype(jnp.int32)

        def take(j, state):
            got, blocks = state
            hit = (own[j] != slot_here * NODE + j) & (own[j] // NODE == from_slot)
            rank = (own[j] % NODE == ids[1]).astype(jnp.int32)

            def put(state):
                got, blocks = state
                for b in range(2):
                    for kv in range(2):
                        start = b * (size + META) + (kv * 2 + rank) * each
                        unit = lax.dynamic_slice_in_dim(buf, start, each)
                        got = lax.dynamic_update_slice(got, unit[None, None, None], (j, kv, b, 0, 0))
                return got, lax.dynamic_update_slice(blocks, ids[2 + rank][None], (j,))

            return lax.cond(hit, put, lambda state: state, (got, blocks))

        got, blocks = lax.fori_loop(0, NODE, take, (got, blocks))
        pairs = [(s, (s + 1) % n_slot) for s in range(n_slot)]
        return lax.ppermute(buf, "slot", pairs), got, blocks

    local = jnp.stack([keys, values], axis=1).reshape(NODE, 2, heads, 2, BLK, dim)
    local = local.transpose(0, 1, 3, 2, 4, 5).reshape(NODE, 2, 2, each, dim)
    carry = (jnp.concatenate([first, second]), local, cache_blocks)
    got, blocks = lax.fori_loop(0, n_slot, turn, carry)[1:]
    row_at = lax.broadcasted_iota(jnp.int32, (STEP * group, 1), 0) // group
    step_ok = lax.broadcasted_iota(jnp.int32, (1, STEP), 1) <= row_at
    token_at = lax.broadcasted_iota(jnp.int32, (1, tokens), 1)

    def unit(n, att):
        j, h = n // heads, n % heads

        def cut(a, wide):
            return lax.dynamic_slice(a, (j * STEP, h * wide), (STEP, wide))

        def cache(kv):
            return lax.dynamic_slice(got, (j, kv, 0, h * BLK, 0), (1, 1, 2, BLK, dim)).reshape(
                tokens, dim
            )

        q = cut(queries, group * dim).reshape(STEP * group, dim)
        k = jnp.concatenate([cache(0), cut(new_keys, dim)])
        v = jnp.concatenate([cache(1), cut(new_values, dim)])
        ok = jnp.concatenate(
            [jnp.broadcast_to(token_at < blocks[j] * BLK, (STEP * group, tokens)), step_ok], axis=1
        )
        logits = jnp.dot(q, k.T, preferred_element_type=f32) * scale
        logits = jnp.where(ok, logits, -jnp.inf)
        weights = jnp.exp(logits - jnp.max(logits, axis=1, keepdims=True))
        out = jnp.dot(weights.astype(v.dtype), v, preferred_element_type=f32)
        out = out / jnp.sum(weights, axis=1, keepdims=True)
        out = out.astype(att.dtype).reshape(STEP, group * dim)
        return lax.dynamic_update_slice(att, out, (j * STEP, h * group * dim))

    att = lax.fori_loop(0, NODE * heads, unit, jnp.zeros_like(queries))
    part = rows // NTP
    cols = weight.shape[1]
    tile = 512

    def piece(i):
        mine = lax.dynamic_slice_in_dim(att, (tp_here + i) % NTP * part, part)

        def column(c, total):
            w = lax.dynamic_slice_in_dim(weight, c * tile, tile, axis=1)
            res = jnp.dot(mine, w, preferred_element_type=f32)
            return lax.dynamic_update_slice(total, res, (0, c * tile))

        return lax.fori_loop(0, cols // tile, column, jnp.zeros((part, cols), f32))

    def pass_on(k, total):
        return lax.ppermute(total, "tp", yperm(1)) + piece(2 * NTP - 1 - k)

    total = lax.fori_loop(0, NTP, pass_on, jnp.zeros((part, cols), f32))
    return total.astype(att.dtype)


def shards(
    queries, cache_keys, cache_values, new_keys, new_values, out_weight, fork_src, cache_blocks
):
    queries, keys, values = queries[0], cache_keys[0], cache_values[0]
    new_keys, new_values, weight = new_keys[0], new_values[0], out_weight[0]
    n_slot = lax.axis_size("slot")
    where = jnp.stack([lax.axis_index(name).astype(jnp.int32) for name in ("role", "slot", "tp")])

    mine = lax.ppermute(fork_src, ("role", "slot"), halves_perm(0, n_slot))
    other = lax.ppermute(fork_src, ("role", "slot"), halves_perm(1, n_slot))
    first, second, own_list = pack(where, mine, other, cache_blocks, keys, values)
    first1 = ring_step((first, first))
    second1 = ring_step((second, second))
    lists = [own_list]
    for d in (1, 2, 3):
        lists.append(lax.ppermute(own_list, "slot", xperm(-d)))
    first2 = ring_step(first1)
    second2 = ring_step(second1)
    first3 = ring_step(first2)
    second3 = ring_step(second2)
    got_first = ring_list(first, first1, first2, first3, ring_last(first3, True))
    got_second = ring_list(second, second1, second2, second3, ring_last(second3, False))
    *outs_first, picks = select_first(where, lists, got_first)
    firsts = []
    for d in (1, 2, 3):
        firsts.append(lax.ppermute(outs_first[d], "slot", xperm(d)))
    outs_second = select_second(picks, got_second)
    seconds = []
    for d in (1, 2, 3):
        seconds.append(lax.ppermute(outs_second[d], "slot", xperm(d)))
    att, weight0, table = local(
        where, own_list, cache_blocks, queries, new_keys, new_values, keys, values,
        (outs_first[0], outs_second[0]), weight,
    )
    att, weight1, table = early(
        where, table, queries, new_keys, new_values, firsts, weight, att, keys
    )
    att, own0, relay_a0, relay_b0, *shared = late(
        where, table, queries, new_keys, new_values, firsts, seconds, att, weight0, keys.shape, 512
    )
    up, down = yperm(1), yperm(-1)
    relay_a0 = lax.ppermute(relay_a0, "tp", up)
    relay_b0 = lax.ppermute(relay_b0, "tp", down)
    own1, relay_a1, relay_b1, da, db, ca, cb = project(att, weight1, shared, 512)
    relay_a1 = lax.ppermute(relay_a1, "tp", up)
    relay_b1 = lax.ppermute(relay_b1, "tp", down)
    da = lax.ppermute(da, "tp", down)
    db = lax.ppermute(db, "tp", up)
    far_a = lax.ppermute(combine(ca, relay_a0, relay_a1), "tp", up)
    far_b = lax.ppermute(combine(cb, relay_b0, relay_b1), "tp", down)
    out = finish(own0, own1, da, db, far_a, far_b)
    args = (where, mine, other, queries, keys, values, new_keys, new_values, weight, cache_blocks)
    out = lax.cond(table[T_FIT] == 1, lambda o, *_: o, lambda o, *a: general(*a), out, *args)
    return out[None]


def solution(mesh):
    in_specs = (
        P("role", "slot", "tp"),
        P("role", "slot", "tp", None, None),
        P("role", "slot", "tp", None, None),
        P("role", "slot", "tp"),
        P("role", "slot", "tp"),
        P("role", "tp", None),
        P(("role", "slot")),
        P("slot"),
    )
    out_specs = P("role", ("slot", "tp"), None)

    return jax.shard_map(shards, mesh=mesh, in_specs=in_specs, out_specs=out_specs, check_vma=False)
```

```python
import functools
import math

import jax
import jax.numpy as jnp
from jax import lax
from jax.experimental import pallas as pl
from jax.experimental.pallas import tpu as pltpu
from jax.sharding import PartitionSpec as P


BLK = 128
NX = 4
NZ = 8
NTP = 4
NODE = 8
STEP = 32
FAST = 2
META = 16

T_FROM = 0
T_RANK = 8
T_LEN = 16
T_FIT = 24
T_SIZE = 32

SMEM = pl.BlockSpec(memory_space=pltpu.SMEM)
VMEM = pl.BlockSpec(memory_space=pltpu.VMEM)
ANY = pl.BlockSpec(memory_space=pl.ANY)


def params(mib):
    return pltpu.CompilerParams(vmem_limit_bytes=mib << 20)


def zperm(d):
    return [(s, (s + NX * d) % (NX * NZ)) for s in range(NX * NZ)]


def xperm(d):
    return [(s, (s // NX) * NX + (s % NX + d) % NX) for s in range(NX * NZ)]


def yperm(d):
    return [(t, (t + d) % NTP) for t in range(NTP)]


def halves_perm(other, n_slot):
    pairs = []
    for role in range(2):
        for k in range(n_slot // 2):
            for h in range(2):
                dest = (h ^ other) * n_slot + role * (n_slot // 2) + k
                pairs.append((role * n_slot + 2 * k + h, dest))
    return pairs


def lane_row(values):
    lane = lax.broadcasted_iota(jnp.int32, (META, 128), 1)
    tile = jnp.zeros((META, 128), jnp.float32)
    for i, value in enumerate(values):
        tile = jnp.where(lane == i, value.astype(jnp.float32), tile)
    return tile.astype(jnp.bfloat16)


def column_counts(here, list_ref, col):
    base = here * NODE
    counts = [jnp.int32(0)] * NX
    for j in range(NODE):
        parent = list_ref[j]
        dist = (col - (parent // NODE) % NX + NX) % NX
        dist = jnp.where(parent == base + j, NX, dist)
        counts = [c + (dist == d).astype(jnp.int32) for d, c in enumerate(counts)]
    return counts


def pack_body(
    where_ref, mine_ref, other_ref, blocks_ref, keys_ref, values_ref,
    first_ref, second_ref, list_ref, sems,
):
    role = where_ref[0]
    here = where_ref[1]
    base = here * NODE
    count = jnp.int32(0)
    low = jnp.int32(0)
    high = jnp.int32(0)
    for j in range(NODE):
        h, k = divmod(j, NODE // 2)
        parent = jnp.where(role == h, mine_ref[k], other_ref[k])
        list_ref[j] = parent
        keep = parent == base + j
        low = jnp.where(keep & (count == 0), j, low)
        high = jnp.where(keep, j, high)
        count = count + keep.astype(jnp.int32)
    heads = keys_ref.shape[1]
    copies = []
    for b, out in enumerate((first_ref, second_ref)):
        for s, node in enumerate((low, high)):
            for kv, src in enumerate((keys_ref, values_ref)):
                for h in range(heads):
                    row = ((kv * 2 + s) * heads + h) * BLK
                    copies.append(
                        pltpu.make_async_copy(
                            src.at[node, h, pl.ds(b * BLK, BLK), :],
                            out.at[pl.ds(row, BLK), :],
                            sems.at[len(copies)],
                        )
                    )
    for c in copies:
        c.start()
    counts = column_counts(here, list_ref, here % NX)
    most = jnp.maximum(jnp.maximum(counts[0], counts[1]), jnp.maximum(counts[2], counts[3]))
    fit = (most <= FAST).astype(jnp.int32)
    rows = second_ref.shape[0]
    first_ref[rows : rows + META, :] = lane_row(
        (low, high, blocks_ref[low], blocks_ref[high], fit)
    )
    for c in copies:
        c.wait()


def pack(where, mine, other, blocks, keys, values):
    heads, _, dim = keys.shape[1:]
    rows = 4 * heads * BLK
    return pl.pallas_call(
        pack_body,
        out_shape=(
            pltpu.VMEM((rows + META, dim), keys.dtype),
            pltpu.VMEM((rows, dim), keys.dtype),
            jax.ShapeDtypeStruct((NODE,), jnp.int32),
        ),
        in_specs=[SMEM, SMEM, SMEM, SMEM, ANY, ANY],
        out_specs=(VMEM, VMEM, SMEM),
        scratch_shapes=[pltpu.SemaphoreType.DMA((8 * heads,))],
        compiler_params=params(2),
        name="pack",
    )(where, mine, other, blocks, keys, values)


def ring_step(pair):
    up, down = pair
    return lax.ppermute(up, "slot", zperm(1)), lax.ppermute(down, "slot", zperm(-1))


def ring_last(pair, up):
    if up:
        return lax.ppermute(pair[0], "slot", zperm(1))
    return lax.ppermute(pair[1], "slot", zperm(-1))


def ring_list(own, one, two, three, last):
    return [own, one[0], two[0], three[0], last, three[1], two[1], one[1]]


def copy_units(pick_ref, srcs, outs, size):
    for d in range(NX):

        def unit(i, carry, d=d):
            u = d * FAST + i
            rel = pick_ref[u]
            rank = pick_ref[NX * FAST + u]
            for r in range(NZ):

                @pl.when(rel == r)
                def _(r=r):
                    for kv in range(2):
                        at = pl.multiple_of((kv * 2 + rank) * size, META)
                        to = pl.multiple_of((kv * 2 + i) * size, META)
                        outs[d][pl.ds(to, size), :] = srcs[r][pl.ds(at, size), :]

            return carry

        lax.fori_loop(0, FAST, unit, 0)


def spill(tiles, wide_ref, ids_ref, sem):
    for i, tile in enumerate(tiles):
        row = jnp.max(tile.astype(jnp.float32), axis=0, keepdims=True)
        wide_ref[i : i + 1, :] = row.astype(jnp.int32)
    copy = pltpu.make_async_copy(wide_ref, ids_ref, sem)
    copy.start()
    copy.wait()


def select_first_body(where_ref, *refs):
    lists = refs[:NX]
    srcs = refs[NX : NX + NZ]
    outs = refs[NX + NZ : 2 * NX + NZ]
    pick_ref, wide_ref, ids_ref, sem = refs[2 * NX + NZ :]
    size = outs[0].shape[0] // 4 // META * META
    here = where_ref[1]
    row = here // NX
    col = here % NX
    tiles = [src[4 * size : 4 * size + META, :] for src in srcs]
    spill(tiles, wide_ref, ids_ref, sem)
    for u in range(2 * NX * FAST):
        pick_ref[u] = 0
    for d in range(NX):
        base = (row * NX + (col + d) % NX) * NODE

        def scan(j, count, d=d, base=base):
            parent = lists[d][j]
            source = parent // NODE
            hit = (parent != base + j) & (source % NX == col)
            rel = (row - source // NX + NZ) % NZ

            @pl.when(hit & (count < FAST))
            def _():
                pick_ref[d * FAST + count] = rel
                pick_ref[NX * FAST + d * FAST + count] = (
                    parent % NODE == ids_ref[rel, 1]
                ).astype(jnp.int32)

            return count + hit.astype(jnp.int32)

        lax.fori_loop(0, NODE, scan, jnp.int32(0))

    copy_units(pick_ref, srcs, outs, size)
    fit = ids_ref[0, 4]
    for rel in range(1, NZ):
        fit = jnp.minimum(fit, ids_ref[rel, 4])
    for d in range(NX):
        sizes = []
        for i in range(FAST):
            u = d * FAST + i
            sizes.append(ids_ref[pick_ref[u], 2 + pick_ref[NX * FAST + u]])
        outs[d][4 * size : 4 * size + META, :] = lane_row((sizes[0], sizes[1], fit))


def select_first(where, lists, srcs):
    own = srcs[0]
    out = pltpu.VMEM(own.shape, own.dtype)
    return pl.pallas_call(
        select_first_body,
        out_shape=(out,) * NX + (jax.ShapeDtypeStruct((2 * NX * FAST,), jnp.int32),),
        in_specs=[SMEM] * (1 + NX) + [VMEM] * NZ,
        out_specs=(VMEM,) * NX + (SMEM,),
        scratch_shapes=[
            pltpu.VMEM((NZ, 128), jnp.int32),
            pltpu.SMEM((NZ, 128), jnp.int32),
            pltpu.SemaphoreType.DMA,
        ],
        compiler_params=params(2),
        name="select_first",
    )(where, *lists, *srcs)


def select_second_body(pick_ref, *refs):
    copy_units(pick_ref, refs[:NZ], refs[NZ:], refs[NZ].shape[0] // 4)


def select_second(picks, srcs):
    own = srcs[0]
    out = pltpu.VMEM(own.shape, own.dtype)
    return pl.pallas_call(
        select_second_body,
        out_shape=(out,) * NX,
        in_specs=[SMEM] + [VMEM] * NZ,
        out_specs=(VMEM,) * NX,
        compiler_params=params(2),
        name="select_second",
    )(picks, *srcs)


def attend_nodes(nodes, blocks, tokens, scale, tp, q_ref, nk_ref, nv_ref, kbuf, vbuf, att_ref):
    heads, _, dim = kbuf.shape[1:]
    group = q_ref.shape[1] // (heads * dim)
    per = NODE // NTP
    rows = STEP * group
    f32 = jnp.float32
    nt = (((1,), (1,)), ((), ()))
    nn = (((1,), (0,)), ((), ()))
    step_of = lax.broadcasted_iota(jnp.int32, (rows, BLK), 0) % STEP
    step_ok = lax.broadcasted_iota(jnp.int32, (rows, BLK), 1) <= step_of
    pad = jnp.zeros((BLK - STEP, dim), kbuf.dtype)
    rate = scale * math.log2(math.e)
    chains = [(i, h) for i in range(len(nodes)) for h in range(heads)]
    at = [pl.multiple_of(n * STEP, STEP) for n in nodes]
    logits = []
    for i, h in chains:
        base = h * group * dim
        step = pl.ds(at[i], STEP)
        q = jnp.concatenate(
            [q_ref[step, base + g * dim : base + (g + 1) * dim] for g in range(group)], axis=0
        )
        nk = nk_ref[step, h * dim : (h + 1) * dim]
        k = jnp.concatenate([kbuf[nodes[i], h, :tokens], nk, pad], axis=0)
        logits.append(lax.dot_general(q, k, nt, preferred_element_type=f32))
    weights = []
    totals = []
    for (i, h), logit in zip(chains, logits):
        tiles = [logit[:, :BLK]]
        for b in range(1, tokens // BLK):
            tile = logit[:, b * BLK : (b + 1) * BLK]
            tiles.append(tile if blocks is None else jnp.where(blocks[i] > b, tile, -jnp.inf))
        tiles.append(jnp.where(step_ok, logit[:, tokens:], -jnp.inf))
        top = tiles[0]
        for tile in tiles[1:]:
            top = jnp.maximum(top, tile)
        top = jnp.max(top, axis=1, keepdims=True)
        tiles = [jnp.exp2((tile - top) * rate) for tile in tiles]
        total = tiles[0]
        for tile in tiles[1:]:
            total = total + tile
        totals.append(jnp.sum(total, axis=1, keepdims=True))
        weights.append(jnp.concatenate([tile.astype(kbuf.dtype) for tile in tiles], axis=1))
    for c, (i, h) in enumerate(chains):
        base = h * group * dim
        nv = nv_ref[pl.ds(at[i], STEP), h * dim : (h + 1) * dim]
        v = jnp.concatenate([vbuf[nodes[i], h, :tokens], nv, pad], axis=0)
        o = lax.dot_general(weights[c], v, nn, preferred_element_type=f32)
        o = (o * (1.0 / totals[c])).astype(att_ref.dtype)
        to = ((nodes[i] // per - tp + NTP) % NTP) * per + nodes[i] % per
        to = pl.ds(pl.multiple_of(to * STEP, STEP), STEP)
        for g in range(group):
            att_ref[to, base + g * dim : base + (g + 1) * dim] = o[g * STEP : (g + 1) * STEP]


def attend_pairs(chosen, wait, todo_ref, run):
    def collect(n, count):
        take = chosen(n)

        @pl.when(take)
        def _():
            todo_ref[count] = n
            todo_ref[count + 1] = n

        return count + take.astype(jnp.int32)

    count = lax.fori_loop(0, NODE, collect, jnp.int32(0))

    def pair(p, carry):
        one = todo_ref[2 * p]
        two = todo_ref[2 * p + 1]
        wait(one)

        @pl.when(two != one)
        def _():
            wait(two)

        run((one, two))
        return carry

    lax.fori_loop(0, (count + 1) // 2, pair, 0)


def cache_copies(src, j, bufs, sems):
    heads = bufs[0].shape[1]
    return [
        pltpu.make_async_copy(src[kv].at[j, h], bufs[kv].at[j, h], sems.at[j, kv * heads + h])
        for kv in range(2)
        for h in range(heads)
    ]


def moved_copies(blocks, rank, j, bufs, sems):
    heads = bufs[0].shape[1]
    copies = []
    for b, src in enumerate(blocks):
        for kv in range(2):
            for h in range(heads):
                at = pl.multiple_of(((kv * 2 + rank) * heads + h) * BLK, BLK)
                copies.append(
                    pltpu.make_async_copy(
                        src.at[pl.ds(at, BLK), :],
                        bufs[kv].at[j, h, pl.ds(b * BLK, BLK), :],
                        sems.at[j, len(copies)],
                    )
                )
    return copies


def each_node(body):
    def step(n, carry):
        body(n)
        return carry

    lax.fori_loop(0, NODE, step, 0)


def local_body(scale, where_ref, list_ref, blocks_ref, q_ref, nk_ref, nv_ref, *refs):
    caches = refs[0:2]
    moved = refs[2:4]
    w_ref, att_ref, w0_ref, table_ref = refs[4:8]
    kbuf, vbuf, wide_ref, ids_ref, todo_ref, sems, sem, wsem = refs[8:]
    bufs = (kbuf, vbuf)
    here = where_ref[1]
    tp = where_ref[2]
    col = here % NX

    def place(j, counts):
        parent = list_ref[j]
        moving = parent != here * NODE + j
        dist = jnp.where(moving, (col - (parent // NODE) % NX + NX) % NX, NX)
        rank = jnp.int32(0)
        after = []
        for d in range(NX):
            hit = dist == d
            rank = jnp.where(hit, counts[d], rank)
            after.append(counts[d] + hit.astype(jnp.int32))
        rank = jnp.minimum(rank, FAST - 1)
        table_ref[T_FROM + j] = dist
        table_ref[T_RANK + j] = rank

        @pl.when(dist == NX)
        def _():
            for c in cache_copies(caches, j, bufs, sems):
                c.start()

        @pl.when(dist == 0)
        def _():
            for c in moved_copies(moved, rank, j, bufs, sems):
                c.start()

        return tuple(after)

    lax.fori_loop(0, NODE, place, (jnp.int32(0),) * NX)
    load = pltpu.make_async_copy(w_ref.at[:, pl.ds(0, w0_ref.shape[1])], w0_ref, wsem)
    load.start()
    rows = moved[0].shape[0]
    spill([moved[0][rows - META :, :]], wide_ref, ids_ref, sem)
    for i in range(T_FIT, T_SIZE):
        table_ref[i] = ids_ref[0, FAST]

    def measure(n):
        blocks = jnp.where(
            table_ref[T_FROM + n] == NX, blocks_ref[n], ids_ref[0, table_ref[T_RANK + n]]
        )
        table_ref[T_LEN + n] = blocks

    each_node(measure)

    def chosen(n):
        return (table_ref[T_FROM + n] == NX) | (table_ref[T_FROM + n] == 0)

    def wait(n):
        @pl.when(table_ref[T_FROM + n] == NX)
        def _():
            for c in cache_copies(caches, n, bufs, sems):
                c.wait()

        @pl.when(table_ref[T_FROM + n] == 0)
        def _():
            for c in moved_copies(moved, 0, n, bufs, sems):
                c.wait()

    def run(nodes):
        blocks = [table_ref[T_LEN + n] for n in nodes]
        attend_nodes(
            nodes, blocks, 2 * BLK, scale, tp, q_ref, nk_ref, nv_ref, kbuf, vbuf, att_ref
        )

    attend_pairs(chosen, wait, todo_ref, run)
    load.wait()


def half_weight(weight):
    return pltpu.VMEM((weight.shape[0], weight.shape[1] // 2), weight.dtype)


def node_scratch(keys, per_node):
    return [
        pltpu.VMEM(keys.shape, keys.dtype),
        pltpu.VMEM(keys.shape, keys.dtype),
        pltpu.VMEM((NX, 128), jnp.int32),
        pltpu.SMEM((NX, 128), jnp.int32),
        pltpu.SMEM((NODE + 2,), jnp.int32),
        pltpu.SemaphoreType.DMA((NODE, per_node)),
        pltpu.SemaphoreType.DMA,
        pltpu.SemaphoreType.DMA,
    ]


def local(where, own_list, blocks, queries, new_keys, new_values, keys, values, moved, weight):
    return pl.pallas_call(
        functools.partial(local_body, float(keys.shape[3]) ** -0.5),
        out_shape=(
            pltpu.VMEM(queries.shape, queries.dtype),
            half_weight(weight),
            jax.ShapeDtypeStruct((T_SIZE,), jnp.int32),
        ),
        in_specs=[SMEM, SMEM, SMEM, VMEM, VMEM, VMEM, ANY, ANY, VMEM, VMEM, ANY],
        out_specs=(VMEM, VMEM, SMEM),
        scratch_shapes=node_scratch(keys, 4 * keys.shape[1]),
        compiler_params=params(8),
        name="local",
    )(where, own_list, blocks, queries, new_keys, new_values, keys, values, *moved, weight)


def early_body(scale, where_ref, old_table, q_ref, nk_ref, nv_ref, *refs):
    moved = refs[: NX - 1]
    refs = refs[NX - 1 :]
    w_ref, old_ref, att_ref, w1_ref, table_ref = refs[:5]
    kbuf, vbuf, wide_ref, ids_ref, todo_ref, sems, sem, wsem = refs[5:]
    del old_ref
    bufs = (kbuf, vbuf)

    def start(n):
        for d in range(1, NX):

            @pl.when(old_table[T_FROM + n] == d)
            def _(d=d):
                for c in moved_copies(moved[d - 1 : d], old_table[T_RANK + n], n, bufs, sems):
                    c.start()

    each_node(start)
    half = w1_ref.shape[1]
    load = pltpu.make_async_copy(w_ref.at[:, pl.ds(half, half)], w1_ref, wsem)
    load.start()
    spill([m[m.shape[0] - META :, :] for m in moved], wide_ref, ids_ref, sem)
    for i in range(T_LEN):
        table_ref[i] = old_table[i]
    fit = old_table[T_FIT]
    for d in range(1, NX):
        fit = jnp.minimum(fit, ids_ref[d - 1, FAST])
    for i in range(T_FIT, T_SIZE):
        table_ref[i] = fit

    def is_far(n):
        return (old_table[T_FROM + n] > 0) & (old_table[T_FROM + n] < NX)

    def wait(n):
        for c in moved_copies(moved[:1], 0, n, bufs, sems):
            c.wait()

    def measure(n):
        at = jnp.clip(old_table[T_FROM + n] - 1, 0, NX - 2)
        blocks = jnp.where(
            is_far(n), ids_ref[at, old_table[T_RANK + n]], old_table[T_LEN + n]
        )
        table_ref[T_LEN + n] = blocks

        @pl.when(is_far(n) & (blocks == 2))
        def _():
            wait(n)

    each_node(measure)

    def chosen(n):
        return is_far(n) & (table_ref[T_LEN + n] == 1)

    def run(nodes):
        attend_nodes(
            nodes, None, BLK, scale, where_ref[2], q_ref, nk_ref, nv_ref, kbuf, vbuf, att_ref
        )

    attend_pairs(chosen, wait, todo_ref, run)
    load.wait()


def early(where, table, queries, new_keys, new_values, moved, weight, att, keys):
    return pl.pallas_call(
        functools.partial(early_body, float(keys.shape[3]) ** -0.5),
        out_shape=(
            pltpu.VMEM(queries.shape, queries.dtype),
            half_weight(weight),
            jax.ShapeDtypeStruct((T_SIZE,), jnp.int32),
        ),
        in_specs=[SMEM, SMEM, VMEM, VMEM, VMEM] + [VMEM] * (NX - 1) + [ANY, VMEM],
        out_specs=(VMEM, VMEM, SMEM),
        scratch_shapes=node_scratch(keys, 2 * keys.shape[1]),
        input_output_aliases={5 + NX: 0},
        compiler_params=params(8),
        name="early",
    )(where, table, queries, new_keys, new_values, *moved, weight, att)


def project_half(chunk, tile, att_ref, w_ref, own_ref, relay_a, relay_b, da, db, ca, cb):
    part, half = relay_a.shape
    base = chunk * half

    def step(side, c, carry):
        at = pl.multiple_of(c * tile, tile)
        cols = pl.ds(pl.multiple_of(side * half + at, tile), tile)
        far = pl.ds(pl.multiple_of(base + at, tile), tile)
        res = jnp.dot(att_ref[...], w_ref[:, cols], preferred_element_type=jnp.float32)
        res = res.astype(own_ref.dtype)
        own_ref[:, cols] = res[:part]
        (ca, db)[side][:, far] = res[part : 2 * part]
        (relay_a, relay_b)[side][:, pl.ds(at, tile)] = res[2 * part : 3 * part]
        (da, cb)[side][:, far] = res[3 * part :]
        return carry

    for side in range(2):
        lax.fori_loop(0, half // tile, functools.partial(step, side), 0)


def late_body(scale, tile, where_ref, table_ref, q_ref, nk_ref, nv_ref, *refs):
    far = NX - 1
    firsts = refs[:far]
    seconds = refs[far : 2 * far]
    old_ref, w_ref, att_ref = refs[2 * far : 2 * far + 3]
    outs = refs[2 * far + 3 : 2 * far + 10]
    kbuf, vbuf, todo_ref, sems = refs[2 * far + 10 :]
    del old_ref
    bufs = (kbuf, vbuf)

    def is_late(n):
        dist = table_ref[T_FROM + n]
        return (dist > 0) & (dist < NX) & (table_ref[T_LEN + n] == 2)

    def start(n):
        for d in range(1, NX):

            @pl.when(is_late(n) & (table_ref[T_FROM + n] == d))
            def _(d=d):
                pair = (firsts[d - 1], seconds[d - 1])
                for c in moved_copies(pair, table_ref[T_RANK + n], n, bufs, sems):
                    c.start()

    each_node(start)

    def wait(n):
        for c in moved_copies((firsts[0], seconds[0]), 0, n, bufs, sems):
            c.wait()

    def run(nodes):
        attend_nodes(
            nodes, None, 2 * BLK, scale, where_ref[2], q_ref, nk_ref, nv_ref, kbuf, vbuf, att_ref
        )

    attend_pairs(is_late, wait, todo_ref, run)
    project_half(0, tile, att_ref, w_ref, *outs)


def late(where, table, queries, new_keys, new_values, firsts, seconds, att, weight0, shape, tile):
    dtype = queries.dtype
    part = att.shape[0] // NTP
    half = weight0.shape[1]
    wide = pltpu.VMEM((part, half), dtype)
    slim = pltpu.VMEM((part, half // 2), dtype)
    far = NX - 1
    return pl.pallas_call(
        functools.partial(late_body, float(shape[3]) ** -0.5, tile),
        out_shape=(pltpu.VMEM(att.shape, dtype), wide, slim, slim, wide, wide, wide, wide),
        in_specs=[SMEM, SMEM, VMEM, VMEM, VMEM] + [ANY] * (2 * far) + [VMEM, VMEM],
        out_specs=(VMEM,) * 8,
        scratch_shapes=[
            pltpu.VMEM(shape, dtype),
            pltpu.VMEM(shape, dtype),
            pltpu.SMEM((NODE + 2,), jnp.int32),
            pltpu.SemaphoreType.DMA((NODE, 4 * shape[1])),
        ],
        input_output_aliases={5 + 2 * far: 0},
        compiler_params=params(8),
        name="late",
    )(where, table, queries, new_keys, new_values, *firsts, *seconds, att, weight0)


def project_body(tile, att_ref, w_ref, da0, db0, ca0, cb0, own_ref, ra, rb, da, db, ca, cb):
    del da0, db0, ca0, cb0
    project_half(1, tile, att_ref, w_ref, own_ref, ra, rb, da, db, ca, cb)


def project(att, weight, shared, tile):
    part = att.shape[0] // NTP
    half = weight.shape[1]
    wide = pltpu.VMEM((part, half), att.dtype)
    slim = pltpu.VMEM((part, half // 2), att.dtype)
    return pl.pallas_call(
        functools.partial(project_body, tile),
        out_shape=(wide, slim, slim, wide, wide, wide, wide),
        in_specs=[VMEM] * 6,
        out_specs=(VMEM,) * 7,
        input_output_aliases={2 + i: 3 + i for i in range(4)},
        compiler_params=params(6),
        name="project",
    )(att, weight, *shared)


def combine_body(base_ref, low_ref, high_ref, out_ref):
    half = low_ref.shape[1]
    for i, ref in enumerate((low_ref, high_ref)):
        cols = slice(i * half, (i + 1) * half)
        total = base_ref[:, cols].astype(jnp.float32) + ref[...].astype(jnp.float32)
        out_ref[:, cols] = total.astype(out_ref.dtype)


def combine(base, low, high):
    return pl.pallas_call(
        combine_body,
        out_shape=pltpu.VMEM(base.shape, base.dtype),
        in_specs=[VMEM] * 3,
        out_specs=VMEM,
        compiler_params=params(2),
        name="combine",
    )(base, low, high)


def finish_body(own0, own1, da, db, fa, fb, out_ref):
    half = own0.shape[1] // 2
    for c, own in enumerate((own0, own1)):
        here = slice(c * half, (c + 1) * half)
        for side, (near, far) in enumerate(((da, fa), (db, fb))):
            cols = slice(side * half, (side + 1) * half)
            total = own[:, cols].astype(jnp.float32) + near[:, here].astype(jnp.float32)
            total = total + far[:, here].astype(jnp.float32)
            at = 2 * c * half + side * half
            out_ref[:, at : at + half] = total.astype(out_ref.dtype)


def finish(*args):
    part, half = args[0].shape
    return pl.pallas_call(
        finish_body,
        out_shape=jax.ShapeDtypeStruct((part, 2 * half), args[0].dtype),
        in_specs=[VMEM] * 6,
        out_specs=VMEM,
        compiler_params=params(4),
        name="finish",
    )(*args)


def general(
    where, mine, other, queries, keys, values, new_keys, new_values, weight, cache_blocks
):
    n_slot = lax.axis_size("slot")
    slot_here = lax.axis_index("slot")
    tp_here = lax.axis_index("tp")
    heads, tokens, dim = keys.shape[1:]
    rows, width = queries.shape
    group = width // (heads * dim)
    scale = float(dim) ** -0.5
    f32 = jnp.float32
    first, second, own = pack(where, mine, other, cache_blocks, keys, values)
    size = second.shape[0]
    each = heads * BLK

    def turn(t, carry):
        buf, got, blocks = carry
        from_slot = (slot_here - t + n_slot) % n_slot
        ids = buf[size].astype(jnp.int32)

        def take(j, state):
            got, blocks = state
            hit = (own[j] != slot_here * NODE + j) & (own[j] // NODE == from_slot)
            rank = (own[j] % NODE == ids[1]).astype(jnp.int32)

            def put(state):
                got, blocks = state
                for b in range(2):
                    for kv in range(2):
                        start = b * (size + META) + (kv * 2 + rank) * each
                        unit = lax.dynamic_slice_in_dim(buf, start, each)
                        got = lax.dynamic_update_slice(got, unit[None, None, None], (j, kv, b, 0, 0))
                return got, lax.dynamic_update_slice(blocks, ids[2 + rank][None], (j,))

            return lax.cond(hit, put, lambda state: state, (got, blocks))

        got, blocks = lax.fori_loop(0, NODE, take, (got, blocks))
        pairs = [(s, (s + 1) % n_slot) for s in range(n_slot)]
        return lax.ppermute(buf, "slot", pairs), got, blocks

    local = jnp.stack([keys, values], axis=1).reshape(NODE, 2, heads, 2, BLK, dim)
    local = local.transpose(0, 1, 3, 2, 4, 5).reshape(NODE, 2, 2, each, dim)
    carry = (jnp.concatenate([first, second]), local, cache_blocks)
    got, blocks = lax.fori_loop(0, n_slot, turn, carry)[1:]
    row_at = lax.broadcasted_iota(jnp.int32, (STEP * group, 1), 0) // group
    step_ok = lax.broadcasted_iota(jnp.int32, (1, STEP), 1) <= row_at
    token_at = lax.broadcasted_iota(jnp.int32, (1, tokens), 1)

    def unit(n, att):
        j, h = n // heads, n % heads

        def cut(a, wide):
            return lax.dynamic_slice(a, (j * STEP, h * wide), (STEP, wide))

        def cache(kv):
            return lax.dynamic_slice(got, (j, kv, 0, h * BLK, 0), (1, 1, 2, BLK, dim)).reshape(
                tokens, dim
            )

        q = cut(queries, group * dim).reshape(STEP * group, dim)
        k = jnp.concatenate([cache(0), cut(new_keys, dim)])
        v = jnp.concatenate([cache(1), cut(new_values, dim)])
        ok = jnp.concatenate(
            [jnp.broadcast_to(token_at < blocks[j] * BLK, (STEP * group, tokens)), step_ok], axis=1
        )
        logits = jnp.dot(q, k.T, preferred_element_type=f32) * scale
        logits = jnp.where(ok, logits, -jnp.inf)
        weights = jnp.exp(logits - jnp.max(logits, axis=1, keepdims=True))
        out = jnp.dot(weights.astype(v.dtype), v, preferred_element_type=f32)
        out = out / jnp.sum(weights, axis=1, keepdims=True)
        out = out.astype(att.dtype).reshape(STEP, group * dim)
        return lax.dynamic_update_slice(att, out, (j * STEP, h * group * dim))

    att = lax.fori_loop(0, NODE * heads, unit, jnp.zeros_like(queries))
    part = rows // NTP
    cols = weight.shape[1]
    tile = 512

    def piece(i):
        mine = lax.dynamic_slice_in_dim(att, (tp_here + i) % NTP * part, part)

        def column(c, total):
            w = lax.dynamic_slice_in_dim(weight, c * tile, tile, axis=1)
            res = jnp.dot(mine, w, preferred_element_type=f32)
            return lax.dynamic_update_slice(total, res, (0, c * tile))

        return lax.fori_loop(0, cols // tile, column, jnp.zeros((part, cols), f32))

    def pass_on(k, total):
        return lax.ppermute(total, "tp", yperm(1)) + piece(2 * NTP - 1 - k)

    total = lax.fori_loop(0, NTP, pass_on, jnp.zeros((part, cols), f32))
    return total.astype(att.dtype)


def shards(
    queries, cache_keys, cache_values, new_keys, new_values, out_weight, fork_src, cache_blocks
):
    queries, keys, values = queries[0], cache_keys[0], cache_values[0]
    new_keys, new_values, weight = new_keys[0], new_values[0], out_weight[0]
    n_slot = lax.axis_size("slot")
    where = jnp.stack([lax.axis_index(name).astype(jnp.int32) for name in ("role", "slot", "tp")])

    mine = lax.ppermute(fork_src, ("role", "slot"), halves_perm(0, n_slot))
    other = lax.ppermute(fork_src, ("role", "slot"), halves_perm(1, n_slot))
    first, second, own_list = pack(where, mine, other, cache_blocks, keys, values)
    first1 = ring_step((first, first))
    second1 = ring_step((second, second))
    lists = [own_list]
    for d in (1, 2, 3):
        lists.append(lax.ppermute(own_list, "slot", xperm(-d)))
    first2 = ring_step(first1)
    second2 = ring_step(second1)
    first3 = ring_step(first2)
    second3 = ring_step(second2)
    got_first = ring_list(first, first1, first2, first3, ring_last(first3, True))
    got_second = ring_list(second, second1, second2, second3, ring_last(second3, False))
    *outs_first, picks = select_first(where, lists, got_first)
    firsts = []
    for d in (1, 2, 3):
        firsts.append(lax.ppermute(outs_first[d], "slot", xperm(d)))
    outs_second = select_second(picks, got_second)
    seconds = []
    for d in (1, 2, 3):
        seconds.append(lax.ppermute(outs_second[d], "slot", xperm(d)))
    att, weight0, table = local(
        where, own_list, cache_blocks, queries, new_keys, new_values, keys, values,
        (outs_first[0], outs_second[0]), weight,
    )
    att, weight1, table = early(
        where, table, queries, new_keys, new_values, firsts, weight, att, keys
    )
    att, own0, relay_a0, relay_b0, *shared = late(
        where, table, queries, new_keys, new_values, firsts, seconds, att, weight0, keys.shape, 512
    )
    up, down = yperm(1), yperm(-1)
    relay_a0 = lax.ppermute(relay_a0, "tp", up)
    relay_b0 = lax.ppermute(relay_b0, "tp", down)
    own1, relay_a1, relay_b1, da, db, ca, cb = project(att, weight1, shared, 512)
    relay_a1 = lax.ppermute(relay_a1, "tp", up)
    relay_b1 = lax.ppermute(relay_b1, "tp", down)
    da = lax.ppermute(da, "tp", down)
    db = lax.ppermute(db, "tp", up)
    far_a = lax.ppermute(combine(ca, relay_a0, relay_a1), "tp", up)
    far_b = lax.ppermute(combine(cb, relay_b0, relay_b1), "tp", down)
    out = finish(own0, own1, da, db, far_a, far_b)
    args = (where, mine, other, queries, keys, values, new_keys, new_values, weight, cache_blocks)
    out = lax.cond(table[T_FIT] == 1, lambda o, *_: o, lambda o, *a: general(*a), out, *args)
    return out[None]


def solution(mesh):
    in_specs = (
        P("role", "slot", "tp"),
        P("role", "slot", "tp", None, None),
        P("role", "slot", "tp", None, None),
        P("role", "slot", "tp"),
        P("role", "slot", "tp"),
        P("role", "tp", None),
        P(("role", "slot")),
        P("slot"),
    )
    out_specs = P("role", ("slot", "tp"), None)

    return jax.shard_map(shards, mesh=mesh, in_specs=in_specs, out_specs=out_specs, check_vma=False)
```

```python
import functools
import math

import jax
import jax.numpy as jnp
from jax import lax
from jax.experimental import pallas as pl
from jax.experimental.pallas import tpu as pltpu
from jax.sharding import PartitionSpec as P


BLK = 128
NX = 4
NZ = 8
NTP = 4
NODE = 8
STEP = 32
FAST = 2
META = 16
LOADS = 8

T_FROM = 0
T_RANK = 8
T_LEN = 16
T_FIT = 24
T_SIZE = 32

SMEM = pl.BlockSpec(memory_space=pltpu.SMEM)
VMEM = pl.BlockSpec(memory_space=pltpu.VMEM)
ANY = pl.BlockSpec(memory_space=pl.ANY)


def params(mib):
    return pltpu.CompilerParams(vmem_limit_bytes=mib << 20)


def zperm(d):
    return [(s, (s + NX * d) % (NX * NZ)) for s in range(NX * NZ)]


def xperm(d):
    return [(s, (s // NX) * NX + (s % NX + d) % NX) for s in range(NX * NZ)]


def yperm(d):
    return [(t, (t + d) % NTP) for t in range(NTP)]


def halves_perm(other, n_slot):
    pairs = []
    for role in range(2):
        for k in range(n_slot // 2):
            for h in range(2):
                dest = (h ^ other) * n_slot + role * (n_slot // 2) + k
                pairs.append((role * n_slot + 2 * k + h, dest))
    return pairs


def lane_row(values):
    lane = lax.broadcasted_iota(jnp.int32, (META, 128), 1)
    tile = jnp.zeros((META, 128), jnp.float32)
    for i, value in enumerate(values):
        tile = jnp.where(lane == i, value.astype(jnp.float32), tile)
    return tile.astype(jnp.bfloat16)


def column_counts(here, list_ref, col):
    base = here * NODE
    counts = [jnp.int32(0)] * NX
    for j in range(NODE):
        parent = list_ref[j]
        dist = (col - (parent // NODE) % NX + NX) % NX
        dist = jnp.where(parent == base + j, NX, dist)
        counts = [c + (dist == d).astype(jnp.int32) for d, c in enumerate(counts)]
    return counts


def pack_body(
    where_ref, mine_ref, other_ref, blocks_ref, keys_ref, values_ref,
    first_ref, second_ref, list_ref, sems,
):
    role = where_ref[0]
    here = where_ref[1]
    base = here * NODE
    count = jnp.int32(0)
    low = jnp.int32(0)
    high = jnp.int32(0)
    for j in range(NODE):
        h, k = divmod(j, NODE // 2)
        parent = jnp.where(role == h, mine_ref[k], other_ref[k])
        list_ref[j] = parent
        keep = parent == base + j
        low = jnp.where(keep & (count == 0), j, low)
        high = jnp.where(keep, j, high)
        count = count + keep.astype(jnp.int32)
    heads = keys_ref.shape[1]
    copies = []
    for b, out in enumerate((first_ref, second_ref)):
        for s, node in enumerate((low, high)):
            for kv, src in enumerate((keys_ref, values_ref)):
                for h in range(heads):
                    row = ((kv * 2 + s) * heads + h) * BLK
                    copies.append(
                        pltpu.make_async_copy(
                            src.at[node, h, pl.ds(b * BLK, BLK), :],
                            out.at[pl.ds(row, BLK), :],
                            sems.at[len(copies)],
                        )
                    )
    for c in copies:
        c.start()
    counts = column_counts(here, list_ref, here % NX)
    most = jnp.maximum(jnp.maximum(counts[0], counts[1]), jnp.maximum(counts[2], counts[3]))
    fit = (most <= FAST).astype(jnp.int32)
    rows = second_ref.shape[0]
    first_ref[rows : rows + META, :] = lane_row(
        (low, high, blocks_ref[low], blocks_ref[high], fit)
    )
    for c in copies:
        c.wait()


def pack(where, mine, other, blocks, keys, values):
    heads, _, dim = keys.shape[1:]
    rows = 4 * heads * BLK
    return pl.pallas_call(
        pack_body,
        out_shape=(
            pltpu.VMEM((rows + META, dim), keys.dtype),
            pltpu.VMEM((rows, dim), keys.dtype),
            jax.ShapeDtypeStruct((NODE,), jnp.int32),
        ),
        in_specs=[SMEM, SMEM, SMEM, SMEM, ANY, ANY],
        out_specs=(VMEM, VMEM, SMEM),
        scratch_shapes=[pltpu.SemaphoreType.DMA((8 * heads,))],
        compiler_params=params(2),
        name="pack",
    )(where, mine, other, blocks, keys, values)


def ring_step(pair):
    up, down = pair
    return lax.ppermute(up, "slot", zperm(1)), lax.ppermute(down, "slot", zperm(-1))


def ring_last(pair, up):
    if up:
        return lax.ppermute(pair[0], "slot", zperm(1))
    return lax.ppermute(pair[1], "slot", zperm(-1))


def ring_list(own, one, two, three, last):
    return [own, one[0], two[0], three[0], last, three[1], two[1], one[1]]


def copy_units(pick_ref, srcs, outs, size):
    for d in range(NX):

        def unit(i, carry, d=d):
            u = d * FAST + i
            rel = pick_ref[u]
            rank = pick_ref[NX * FAST + u]
            for r in range(NZ):

                @pl.when(rel == r)
                def _(r=r):
                    for kv in range(2):
                        at = pl.multiple_of((kv * 2 + rank) * size, META)
                        to = pl.multiple_of((kv * 2 + i) * size, META)
                        outs[d][pl.ds(to, size), :] = srcs[r][pl.ds(at, size), :]

            return carry

        lax.fori_loop(0, FAST, unit, 0)


def spill(tiles, wide_ref, ids_ref, sem):
    for i, tile in enumerate(tiles):
        row = jnp.max(tile.astype(jnp.float32), axis=0, keepdims=True)
        wide_ref[i : i + 1, :] = row.astype(jnp.int32)
    copy = pltpu.make_async_copy(wide_ref, ids_ref, sem)
    copy.start()
    copy.wait()


def select_first_body(where_ref, *refs):
    lists = refs[:NX]
    srcs = refs[NX : NX + NZ]
    outs = refs[NX + NZ : 2 * NX + NZ]
    pick_ref, wide_ref, ids_ref, sem = refs[2 * NX + NZ :]
    size = outs[0].shape[0] // 4 // META * META
    here = where_ref[1]
    row = here // NX
    col = here % NX
    tiles = [src[4 * size : 4 * size + META, :] for src in srcs]
    spill(tiles, wide_ref, ids_ref, sem)
    for u in range(2 * NX * FAST):
        pick_ref[u] = 0
    for d in range(NX):
        base = (row * NX + (col + d) % NX) * NODE

        def scan(j, count, d=d, base=base):
            parent = lists[d][j]
            source = parent // NODE
            hit = (parent != base + j) & (source % NX == col)
            rel = (row - source // NX + NZ) % NZ

            @pl.when(hit & (count < FAST))
            def _():
                pick_ref[d * FAST + count] = rel
                pick_ref[NX * FAST + d * FAST + count] = (
                    parent % NODE == ids_ref[rel, 1]
                ).astype(jnp.int32)

            return count + hit.astype(jnp.int32)

        lax.fori_loop(0, NODE, scan, jnp.int32(0))

    copy_units(pick_ref, srcs, outs, size)
    fit = ids_ref[0, 4]
    for rel in range(1, NZ):
        fit = jnp.minimum(fit, ids_ref[rel, 4])
    for d in range(NX):
        sizes = []
        for i in range(FAST):
            u = d * FAST + i
            sizes.append(ids_ref[pick_ref[u], 2 + pick_ref[NX * FAST + u]])
        outs[d][4 * size : 4 * size + META, :] = lane_row((sizes[0], sizes[1], fit))


def select_first(where, lists, srcs):
    own = srcs[0]
    out = pltpu.VMEM(own.shape, own.dtype)
    return pl.pallas_call(
        select_first_body,
        out_shape=(out,) * NX + (jax.ShapeDtypeStruct((2 * NX * FAST,), jnp.int32),),
        in_specs=[SMEM] * (1 + NX) + [VMEM] * NZ,
        out_specs=(VMEM,) * NX + (SMEM,),
        scratch_shapes=[
            pltpu.VMEM((NZ, 128), jnp.int32),
            pltpu.SMEM((NZ, 128), jnp.int32),
            pltpu.SemaphoreType.DMA,
        ],
        compiler_params=params(2),
        name="select_first",
    )(where, *lists, *srcs)


def select_second_body(pick_ref, *refs):
    copy_units(pick_ref, refs[:NZ], refs[NZ:], refs[NZ].shape[0] // 4)


def select_second(picks, srcs):
    own = srcs[0]
    out = pltpu.VMEM(own.shape, own.dtype)
    return pl.pallas_call(
        select_second_body,
        out_shape=(out,) * NX,
        in_specs=[SMEM] + [VMEM] * NZ,
        out_specs=(VMEM,) * NX,
        compiler_params=params(2),
        name="select_second",
    )(picks, *srcs)


def attend_nodes(nodes, blocks, tokens, scale, tp, q_ref, nk_ref, nv_ref, kbuf, vbuf, att_ref):
    heads, _, dim = kbuf.shape[1:]
    group = q_ref.shape[1] // (heads * dim)
    per = NODE // NTP
    rows = STEP * group
    f32 = jnp.float32
    nt = (((1,), (1,)), ((), ()))
    nn = (((1,), (0,)), ((), ()))
    step_of = lax.broadcasted_iota(jnp.int32, (rows, BLK), 0) % STEP
    step_ok = lax.broadcasted_iota(jnp.int32, (rows, BLK), 1) <= step_of
    pad = jnp.zeros((BLK - STEP, dim), kbuf.dtype)
    rate = scale * math.log2(math.e)
    chains = [(i, h) for i in range(len(nodes)) for h in range(heads)]
    at = [pl.multiple_of(n * STEP, STEP) for n in nodes]
    logits = []
    for i, h in chains:
        base = h * group * dim
        step = pl.ds(at[i], STEP)
        q = jnp.concatenate(
            [q_ref[step, base + g * dim : base + (g + 1) * dim] for g in range(group)], axis=0
        )
        nk = nk_ref[step, h * dim : (h + 1) * dim]
        k = jnp.concatenate([kbuf[nodes[i], h, :tokens], nk, pad], axis=0)
        logits.append(lax.dot_general(q, k, nt, preferred_element_type=f32))
    weights = []
    totals = []
    for (i, h), logit in zip(chains, logits):
        tiles = [logit[:, :BLK]]
        for b in range(1, tokens // BLK):
            tile = logit[:, b * BLK : (b + 1) * BLK]
            tiles.append(tile if blocks is None else jnp.where(blocks[i] > b, tile, -jnp.inf))
        tiles.append(jnp.where(step_ok, logit[:, tokens:], -jnp.inf))
        top = tiles[0]
        for tile in tiles[1:]:
            top = jnp.maximum(top, tile)
        top = jnp.max(top, axis=1, keepdims=True)
        tiles = [jnp.exp2((tile - top) * rate) for tile in tiles]
        total = tiles[0]
        for tile in tiles[1:]:
            total = total + tile
        totals.append(jnp.sum(total, axis=1, keepdims=True))
        weights.append(jnp.concatenate([tile.astype(kbuf.dtype) for tile in tiles], axis=1))
    for c, (i, h) in enumerate(chains):
        base = h * group * dim
        nv = nv_ref[pl.ds(at[i], STEP), h * dim : (h + 1) * dim]
        v = jnp.concatenate([vbuf[nodes[i], h, :tokens], nv, pad], axis=0)
        o = lax.dot_general(weights[c], v, nn, preferred_element_type=f32)
        o = (o * (1.0 / totals[c])).astype(att_ref.dtype)
        to = ((nodes[i] // per - tp + NTP) % NTP) * per + nodes[i] % per
        to = pl.ds(pl.multiple_of(to * STEP, STEP), STEP)
        for g in range(group):
            att_ref[to, base + g * dim : base + (g + 1) * dim] = o[g * STEP : (g + 1) * STEP]


def attend_pairs(chosen, wait, todo_ref, run):
    def collect(n, count):
        take = chosen(n)

        @pl.when(take)
        def _():
            todo_ref[count] = n
            todo_ref[count + 1] = n

        return count + take.astype(jnp.int32)

    count = lax.fori_loop(0, NODE, collect, jnp.int32(0))

    def pair(p, carry):
        one = todo_ref[2 * p]
        two = todo_ref[2 * p + 1]
        wait(one)

        @pl.when(two != one)
        def _():
            wait(two)

        run((one, two))
        return carry

    lax.fori_loop(0, (count + 1) // 2, pair, 0)


def cache_copies(src, j, bufs, sems):
    heads = bufs[0].shape[1]
    return [
        pltpu.make_async_copy(src[kv].at[j, h], bufs[kv].at[j, h], sems.at[j, kv * heads + h])
        for kv in range(2)
        for h in range(heads)
    ]


def moved_copies(blocks, rank, j, bufs, sems):
    heads = bufs[0].shape[1]
    copies = []
    for b, src in enumerate(blocks):
        for kv in range(2):
            for h in range(heads):
                at = pl.multiple_of(((kv * 2 + rank) * heads + h) * BLK, BLK)
                copies.append(
                    pltpu.make_async_copy(
                        src.at[pl.ds(at, BLK), :],
                        bufs[kv].at[j, h, pl.ds(b * BLK, BLK), :],
                        sems.at[j, len(copies)],
                    )
                )
    return copies


def each_node(body):
    def step(n, carry):
        body(n)
        return carry

    lax.fori_loop(0, NODE, step, 0)


def local_body(scale, where_ref, list_ref, blocks_ref, q_ref, nk_ref, nv_ref, *refs):
    caches = refs[0:2]
    moved = refs[2:4]
    w_ref, att_ref, w0_ref, table_ref = refs[4:8]
    kbuf, vbuf, wide_ref, ids_ref, todo_ref, sems, sem, wsem = refs[8:]
    bufs = (kbuf, vbuf)
    here = where_ref[1]
    tp = where_ref[2]
    col = here % NX

    def place(j, counts):
        parent = list_ref[j]
        moving = parent != here * NODE + j
        dist = jnp.where(moving, (col - (parent // NODE) % NX + NX) % NX, NX)
        rank = jnp.int32(0)
        after = []
        for d in range(NX):
            hit = dist == d
            rank = jnp.where(hit, counts[d], rank)
            after.append(counts[d] + hit.astype(jnp.int32))
        rank = jnp.minimum(rank, FAST - 1)
        table_ref[T_FROM + j] = dist
        table_ref[T_RANK + j] = rank

        @pl.when(dist == NX)
        def _():
            for c in cache_copies(caches, j, bufs, sems):
                c.start()

        @pl.when(dist == 0)
        def _():
            for c in moved_copies(moved, rank, j, bufs, sems):
                c.start()

        return tuple(after)

    lax.fori_loop(0, NODE, place, (jnp.int32(0),) * NX)
    loads = weight_loads(w_ref, w0_ref, 0, wsem)
    for load in loads:
        load.start()
    rows = moved[0].shape[0]
    spill([moved[0][rows - META :, :]], wide_ref, ids_ref, sem)
    for i in range(T_FIT, T_SIZE):
        table_ref[i] = ids_ref[0, FAST]

    def measure(n):
        blocks = jnp.where(
            table_ref[T_FROM + n] == NX, blocks_ref[n], ids_ref[0, table_ref[T_RANK + n]]
        )
        table_ref[T_LEN + n] = blocks

    each_node(measure)

    def chosen(n):
        return (table_ref[T_FROM + n] == NX) | (table_ref[T_FROM + n] == 0)

    def wait(n):
        @pl.when(table_ref[T_FROM + n] == NX)
        def _():
            for c in cache_copies(caches, n, bufs, sems):
                c.wait()

        @pl.when(table_ref[T_FROM + n] == 0)
        def _():
            for c in moved_copies(moved, 0, n, bufs, sems):
                c.wait()

    def run(nodes):
        blocks = [table_ref[T_LEN + n] for n in nodes]
        attend_nodes(
            nodes, blocks, 2 * BLK, scale, tp, q_ref, nk_ref, nv_ref, kbuf, vbuf, att_ref
        )

    attend_pairs(chosen, wait, todo_ref, run)
    for load in loads:
        load.wait()


def weight_loads(w_ref, dst, at, sems):
    rows = dst.shape[0] // LOADS
    cols = pl.ds(at, dst.shape[1])
    return [
        pltpu.make_async_copy(
            w_ref.at[pl.ds(i * rows, rows), cols], dst.at[pl.ds(i * rows, rows), :], sems.at[i]
        )
        for i in range(LOADS)
    ]


def weight_part(weight, parts):
    return pltpu.VMEM((weight.shape[0], weight.shape[1] // parts), weight.dtype)


def node_scratch(keys, per_node):
    return [
        pltpu.VMEM(keys.shape, keys.dtype),
        pltpu.VMEM(keys.shape, keys.dtype),
        pltpu.VMEM((NX, 128), jnp.int32),
        pltpu.SMEM((NX, 128), jnp.int32),
        pltpu.SMEM((NODE + 2,), jnp.int32),
        pltpu.SemaphoreType.DMA((NODE, per_node)),
        pltpu.SemaphoreType.DMA,
        pltpu.SemaphoreType.DMA((LOADS,)),
    ]


def local(where, own_list, blocks, queries, new_keys, new_values, keys, values, moved, weight):
    return pl.pallas_call(
        functools.partial(local_body, float(keys.shape[3]) ** -0.5),
        out_shape=(
            pltpu.VMEM(queries.shape, queries.dtype),
            weight_part(weight, 2),
            jax.ShapeDtypeStruct((T_SIZE,), jnp.int32),
        ),
        in_specs=[SMEM, SMEM, SMEM, VMEM, VMEM, VMEM, ANY, ANY, VMEM, VMEM, ANY],
        out_specs=(VMEM, VMEM, SMEM),
        scratch_shapes=node_scratch(keys, 4 * keys.shape[1]),
        compiler_params=params(8),
        name="local",
    )(where, own_list, blocks, queries, new_keys, new_values, keys, values, *moved, weight)


def early_body(scale, where_ref, old_table, q_ref, nk_ref, nv_ref, *refs):
    moved = refs[: NX - 1]
    refs = refs[NX - 1 :]
    w_ref, old_ref, att_ref, w1_ref, table_ref = refs[:5]
    kbuf, vbuf, wide_ref, ids_ref, todo_ref, sems, sem, wsem = refs[5:]
    del old_ref
    bufs = (kbuf, vbuf)

    def start(n):
        for d in range(1, NX):

            @pl.when(old_table[T_FROM + n] == d)
            def _(d=d):
                for c in moved_copies(moved[d - 1 : d], old_table[T_RANK + n], n, bufs, sems):
                    c.start()

    each_node(start)
    loads = weight_loads(w_ref, w1_ref, 2 * w1_ref.shape[1], wsem)
    for load in loads:
        load.start()
    spill([m[m.shape[0] - META :, :] for m in moved], wide_ref, ids_ref, sem)
    for i in range(T_LEN):
        table_ref[i] = old_table[i]
    fit = old_table[T_FIT]
    for d in range(1, NX):
        fit = jnp.minimum(fit, ids_ref[d - 1, FAST])
    for i in range(T_FIT, T_SIZE):
        table_ref[i] = fit

    def is_far(n):
        return (old_table[T_FROM + n] > 0) & (old_table[T_FROM + n] < NX)

    def wait(n):
        for c in moved_copies(moved[:1], 0, n, bufs, sems):
            c.wait()

    def measure(n):
        at = jnp.clip(old_table[T_FROM + n] - 1, 0, NX - 2)
        blocks = jnp.where(
            is_far(n), ids_ref[at, old_table[T_RANK + n]], old_table[T_LEN + n]
        )
        table_ref[T_LEN + n] = blocks

        @pl.when(is_far(n) & (blocks == 2))
        def _():
            wait(n)

    each_node(measure)

    def chosen(n):
        return is_far(n) & (table_ref[T_LEN + n] == 1)

    def run(nodes):
        attend_nodes(
            nodes, None, BLK, scale, where_ref[2], q_ref, nk_ref, nv_ref, kbuf, vbuf, att_ref
        )

    attend_pairs(chosen, wait, todo_ref, run)
    for load in loads:
        load.wait()


def early(where, table, queries, new_keys, new_values, moved, weight, att, keys):
    return pl.pallas_call(
        functools.partial(early_body, float(keys.shape[3]) ** -0.5),
        out_shape=(
            pltpu.VMEM(queries.shape, queries.dtype),
            weight_part(weight, 4),
            jax.ShapeDtypeStruct((T_SIZE,), jnp.int32),
        ),
        in_specs=[SMEM, SMEM, VMEM, VMEM, VMEM] + [VMEM] * (NX - 1) + [ANY, VMEM],
        out_specs=(VMEM, VMEM, SMEM),
        scratch_shapes=node_scratch(keys, 2 * keys.shape[1]),
        input_output_aliases={5 + NX: 0},
        compiler_params=params(8),
        name="early",
    )(where, table, queries, new_keys, new_values, *moved, weight, att)


def project_half(chunk, tile, att_ref, sides, own_ref, relay_a, relay_b, da, db, ca, cb):
    part, half = relay_a.shape
    base = chunk * half

    def step(side, c, carry):
        at = pl.multiple_of(c * tile, tile)
        cols = pl.ds(pl.multiple_of(side * half + at, tile), tile)
        far = pl.ds(pl.multiple_of(base + at, tile), tile)
        w_ref, first = sides[side]
        from_w = pl.ds(pl.multiple_of(first + at, tile), tile)
        res = jnp.dot(att_ref[...], w_ref[:, from_w], preferred_element_type=jnp.float32)
        res = res.astype(own_ref.dtype)
        own_ref[:, cols] = res[:part]
        (ca, db)[side][:, far] = res[part : 2 * part]
        (relay_a, relay_b)[side][:, pl.ds(at, tile)] = res[2 * part : 3 * part]
        (da, cb)[side][:, far] = res[3 * part :]
        return carry

    for side in range(2):
        lax.fori_loop(0, half // tile, functools.partial(step, side), 0)


def late_body(scale, tile, where_ref, table_ref, q_ref, nk_ref, nv_ref, *refs):
    far = NX - 1
    firsts = refs[:far]
    seconds = refs[far : 2 * far]
    old_ref, w0_ref, w_ref, att_ref, w3_ref = refs[2 * far : 2 * far + 5]
    outs = refs[2 * far + 5 : 2 * far + 12]
    kbuf, vbuf, todo_ref, sems, wsem = refs[2 * far + 12 :]
    del old_ref
    bufs = (kbuf, vbuf)

    def is_late(n):
        dist = table_ref[T_FROM + n]
        return (dist > 0) & (dist < NX) & (table_ref[T_LEN + n] == 2)

    def start(n):
        for d in range(1, NX):

            @pl.when(is_late(n) & (table_ref[T_FROM + n] == d))
            def _(d=d):
                pair = (firsts[d - 1], seconds[d - 1])
                for c in moved_copies(pair, table_ref[T_RANK + n], n, bufs, sems):
                    c.start()

    each_node(start)
    loads = weight_loads(w_ref, w3_ref, 3 * w3_ref.shape[1], wsem)
    for load in loads:
        load.start()

    def wait(n):
        for c in moved_copies((firsts[0], seconds[0]), 0, n, bufs, sems):
            c.wait()

    def run(nodes):
        attend_nodes(
            nodes, None, 2 * BLK, scale, where_ref[2], q_ref, nk_ref, nv_ref, kbuf, vbuf, att_ref
        )

    attend_pairs(is_late, wait, todo_ref, run)
    half = w3_ref.shape[1]
    project_half(0, tile, att_ref, ((w0_ref, 0), (w0_ref, half)), *outs)
    for load in loads:
        load.wait()


def late(
    where, table, queries, new_keys, new_values, firsts, seconds, att, weight0, weight, shape, tile
):
    dtype = queries.dtype
    part = att.shape[0] // NTP
    half = weight0.shape[1]
    wide = pltpu.VMEM((part, half), dtype)
    slim = pltpu.VMEM((part, half // 2), dtype)
    far = NX - 1
    return pl.pallas_call(
        functools.partial(late_body, float(shape[3]) ** -0.5, tile),
        out_shape=(pltpu.VMEM(att.shape, dtype), weight_part(weight, 4))
        + (wide, slim, slim, wide, wide, wide, wide),
        in_specs=[SMEM, SMEM, VMEM, VMEM, VMEM] + [ANY] * (2 * far) + [VMEM, VMEM, ANY],
        out_specs=(VMEM,) * 9,
        scratch_shapes=[
            pltpu.VMEM(shape, dtype),
            pltpu.VMEM(shape, dtype),
            pltpu.SMEM((NODE + 2,), jnp.int32),
            pltpu.SemaphoreType.DMA((NODE, 4 * shape[1])),
            pltpu.SemaphoreType.DMA((LOADS,)),
        ],
        input_output_aliases={5 + 2 * far: 0},
        compiler_params=params(8),
        name="late",
    )(where, table, queries, new_keys, new_values, *firsts, *seconds, att, weight0, weight)


def project_body(tile, att_ref, w2_ref, w3_ref, da0, db0, ca0, cb0, own_ref, ra, rb, da, db, ca, cb):
    del da0, db0, ca0, cb0
    project_half(1, tile, att_ref, ((w2_ref, 0), (w3_ref, 0)), own_ref, ra, rb, da, db, ca, cb)


def project(att, weights, shared, tile):
    part = att.shape[0] // NTP
    half = 2 * weights[0].shape[1]
    wide = pltpu.VMEM((part, half), att.dtype)
    slim = pltpu.VMEM((part, half // 2), att.dtype)
    return pl.pallas_call(
        functools.partial(project_body, tile),
        out_shape=(wide, slim, slim, wide, wide, wide, wide),
        in_specs=[VMEM] * 7,
        out_specs=(VMEM,) * 7,
        input_output_aliases={3 + i: 3 + i for i in range(4)},
        compiler_params=params(6),
        name="project",
    )(att, *weights, *shared)


def combine_body(base_ref, low_ref, high_ref, out_ref):
    half = low_ref.shape[1]
    for i, ref in enumerate((low_ref, high_ref)):
        cols = slice(i * half, (i + 1) * half)
        total = base_ref[:, cols].astype(jnp.float32) + ref[...].astype(jnp.float32)
        out_ref[:, cols] = total.astype(out_ref.dtype)


def combine(base, low, high):
    return pl.pallas_call(
        combine_body,
        out_shape=pltpu.VMEM(base.shape, base.dtype),
        in_specs=[VMEM] * 3,
        out_specs=VMEM,
        compiler_params=params(2),
        name="combine",
    )(base, low, high)


def finish_body(own0, own1, da, db, fa, fb, out_ref):
    half = own0.shape[1] // 2
    for c, own in enumerate((own0, own1)):
        here = slice(c * half, (c + 1) * half)
        for side, (near, far) in enumerate(((da, fa), (db, fb))):
            cols = slice(side * half, (side + 1) * half)
            total = own[:, cols].astype(jnp.float32) + near[:, here].astype(jnp.float32)
            total = total + far[:, here].astype(jnp.float32)
            at = 2 * c * half + side * half
            out_ref[:, at : at + half] = total.astype(out_ref.dtype)


def finish(*args):
    part, half = args[0].shape
    return pl.pallas_call(
        finish_body,
        out_shape=jax.ShapeDtypeStruct((part, 2 * half), args[0].dtype),
        in_specs=[VMEM] * 6,
        out_specs=VMEM,
        compiler_params=params(4),
        name="finish",
    )(*args)


def general(
    where, mine, other, queries, keys, values, new_keys, new_values, weight, cache_blocks
):
    n_slot = lax.axis_size("slot")
    slot_here = lax.axis_index("slot")
    tp_here = lax.axis_index("tp")
    heads, tokens, dim = keys.shape[1:]
    rows, width = queries.shape
    group = width // (heads * dim)
    scale = float(dim) ** -0.5
    f32 = jnp.float32
    first, second, own = pack(where, mine, other, cache_blocks, keys, values)
    size = second.shape[0]
    each = heads * BLK

    def turn(t, carry):
        buf, got, blocks = carry
        from_slot = (slot_here - t + n_slot) % n_slot
        ids = buf[size].astype(jnp.int32)

        def take(j, state):
            got, blocks = state
            hit = (own[j] != slot_here * NODE + j) & (own[j] // NODE == from_slot)
            rank = (own[j] % NODE == ids[1]).astype(jnp.int32)

            def put(state):
                got, blocks = state
                for b in range(2):
                    for kv in range(2):
                        start = b * (size + META) + (kv * 2 + rank) * each
                        unit = lax.dynamic_slice_in_dim(buf, start, each)
                        got = lax.dynamic_update_slice(got, unit[None, None, None], (j, kv, b, 0, 0))
                return got, lax.dynamic_update_slice(blocks, ids[2 + rank][None], (j,))

            return lax.cond(hit, put, lambda state: state, (got, blocks))

        got, blocks = lax.fori_loop(0, NODE, take, (got, blocks))
        pairs = [(s, (s + 1) % n_slot) for s in range(n_slot)]
        return lax.ppermute(buf, "slot", pairs), got, blocks

    local = jnp.stack([keys, values], axis=1).reshape(NODE, 2, heads, 2, BLK, dim)
    local = local.transpose(0, 1, 3, 2, 4, 5).reshape(NODE, 2, 2, each, dim)
    carry = (jnp.concatenate([first, second]), local, cache_blocks)
    got, blocks = lax.fori_loop(0, n_slot, turn, carry)[1:]
    row_at = lax.broadcasted_iota(jnp.int32, (STEP * group, 1), 0) // group
    step_ok = lax.broadcasted_iota(jnp.int32, (1, STEP), 1) <= row_at
    token_at = lax.broadcasted_iota(jnp.int32, (1, tokens), 1)

    def unit(n, att):
        j, h = n // heads, n % heads

        def cut(a, wide):
            return lax.dynamic_slice(a, (j * STEP, h * wide), (STEP, wide))

        def cache(kv):
            return lax.dynamic_slice(got, (j, kv, 0, h * BLK, 0), (1, 1, 2, BLK, dim)).reshape(
                tokens, dim
            )

        q = cut(queries, group * dim).reshape(STEP * group, dim)
        k = jnp.concatenate([cache(0), cut(new_keys, dim)])
        v = jnp.concatenate([cache(1), cut(new_values, dim)])
        ok = jnp.concatenate(
            [jnp.broadcast_to(token_at < blocks[j] * BLK, (STEP * group, tokens)), step_ok], axis=1
        )
        logits = jnp.dot(q, k.T, preferred_element_type=f32) * scale
        logits = jnp.where(ok, logits, -jnp.inf)
        weights = jnp.exp(logits - jnp.max(logits, axis=1, keepdims=True))
        out = jnp.dot(weights.astype(v.dtype), v, preferred_element_type=f32)
        out = out / jnp.sum(weights, axis=1, keepdims=True)
        out = out.astype(att.dtype).reshape(STEP, group * dim)
        return lax.dynamic_update_slice(att, out, (j * STEP, h * group * dim))

    att = lax.fori_loop(0, NODE * heads, unit, jnp.zeros_like(queries))
    part = rows // NTP
    cols = weight.shape[1]
    tile = 512

    def piece(i):
        mine = lax.dynamic_slice_in_dim(att, (tp_here + i) % NTP * part, part)

        def column(c, total):
            w = lax.dynamic_slice_in_dim(weight, c * tile, tile, axis=1)
            res = jnp.dot(mine, w, preferred_element_type=f32)
            return lax.dynamic_update_slice(total, res, (0, c * tile))

        return lax.fori_loop(0, cols // tile, column, jnp.zeros((part, cols), f32))

    def pass_on(k, total):
        return lax.ppermute(total, "tp", yperm(1)) + piece(2 * NTP - 1 - k)

    total = lax.fori_loop(0, NTP, pass_on, jnp.zeros((part, cols), f32))
    return total.astype(att.dtype)


def shards(
    queries, cache_keys, cache_values, new_keys, new_values, out_weight, fork_src, cache_blocks
):
    queries, keys, values = queries[0], cache_keys[0], cache_values[0]
    new_keys, new_values, weight = new_keys[0], new_values[0], out_weight[0]
    n_slot = lax.axis_size("slot")
    where = jnp.stack([lax.axis_index(name).astype(jnp.int32) for name in ("role", "slot", "tp")])

    mine = lax.ppermute(fork_src, ("role", "slot"), halves_perm(0, n_slot))
    other = lax.ppermute(fork_src, ("role", "slot"), halves_perm(1, n_slot))
    first, second, own_list = pack(where, mine, other, cache_blocks, keys, values)
    first1 = ring_step((first, first))
    second1 = ring_step((second, second))
    lists = [own_list]
    for d in (1, 2, 3):
        lists.append(lax.ppermute(own_list, "slot", xperm(-d)))
    first2 = ring_step(first1)
    second2 = ring_step(second1)
    first3 = ring_step(first2)
    second3 = ring_step(second2)
    got_first = ring_list(first, first1, first2, first3, ring_last(first3, True))
    got_second = ring_list(second, second1, second2, second3, ring_last(second3, False))
    *outs_first, picks = select_first(where, lists, got_first)
    firsts = []
    for d in (1, 2, 3):
        firsts.append(lax.ppermute(outs_first[d], "slot", xperm(d)))
    outs_second = select_second(picks, got_second)
    seconds = []
    for d in (1, 2, 3):
        seconds.append(lax.ppermute(outs_second[d], "slot", xperm(d)))
    att, weight0, table = local(
        where, own_list, cache_blocks, queries, new_keys, new_values, keys, values,
        (outs_first[0], outs_second[0]), weight,
    )
    att, weight2, table = early(
        where, table, queries, new_keys, new_values, firsts, weight, att, keys
    )
    att, weight3, own0, relay_a0, relay_b0, *shared = late(
        where, table, queries, new_keys, new_values, firsts, seconds, att, weight0, weight,
        keys.shape, 1024
    )
    up, down = yperm(1), yperm(-1)
    relay_a0 = lax.ppermute(relay_a0, "tp", up)
    relay_b0 = lax.ppermute(relay_b0, "tp", down)
    own1, relay_a1, relay_b1, da, db, ca, cb = project(att, (weight2, weight3), shared, 1024)
    relay_a1 = lax.ppermute(relay_a1, "tp", up)
    relay_b1 = lax.ppermute(relay_b1, "tp", down)
    da = lax.ppermute(da, "tp", down)
    db = lax.ppermute(db, "tp", up)
    far_a = lax.ppermute(combine(ca, relay_a0, relay_a1), "tp", up)
    far_b = lax.ppermute(combine(cb, relay_b0, relay_b1), "tp", down)
    out = finish(own0, own1, da, db, far_a, far_b)
    args = (where, mine, other, queries, keys, values, new_keys, new_values, weight, cache_blocks)
    out = lax.cond(table[T_FIT] == 1, lambda o, *_: o, lambda o, *a: general(*a), out, *args)
    return out[None]


def solution(mesh):
    in_specs = (
        P("role", "slot", "tp"),
        P("role", "slot", "tp", None, None),
        P("role", "slot", "tp", None, None),
        P("role", "slot", "tp"),
        P("role", "slot", "tp"),
        P("role", "tp", None),
        P(("role", "slot")),
        P("slot"),
    )
    out_specs = P("role", ("slot", "tp"), None)

    return jax.shard_map(shards, mesh=mesh, in_specs=in_specs, out_specs=out_specs, check_vma=False)
```
